32 devices in a mesh: shard: 4 (over z), ctx: 2 (over y), tp: 4 (over x, core).
Axes of the slice: x: 2, y: 2, z: 4, core: 2. Of those that a mesh axis runs over, the one named last changes fastest.
Arguments:
- inputs: float32 [8, 256, 1024], P('shard', 'ctx'), may hold values from -12 to 12
- segment_ids: int32 [8, 256], P('shard', 'ctx'), may hold values from 0 to 3, never falling along the last dimension, each value on 1 to 128 neighbouring positions
- gains: bfloat16 [2, 1024], P(None, ('shard', 'ctx')), may hold values from 0.5 to 1.5
- shifts: bfloat16 [2, 1024], P(None, ('shard', 'ctx')), may hold values from -3 to 3
- attend_weight: bfloat16 [1024, 3, 1024], P(('shard', 'ctx'), None, 'tp'), may hold values from -1 to 1
- merge_weight: bfloat16 [1024, 1024], P(('shard', 'ctx'), 'tp'), may hold values from -0.75 to 0.75
- expand_weight: bfloat16 [1024, 4096], P(('shard', 'ctx'), 'tp'), may hold values from -0.1875 to 0.1875
- expand_bias: bfloat16 [4, 1024], P('tp', ('shard', 'ctx')), may hold values from -3 to 3
- reduce_weight: bfloat16 [1024, 4096], P(('shard', 'ctx'), 'tp'), may hold values from -0.09375 to 0.09375
- cotangent: float32 [8, 256, 1024], P('shard', 'ctx'), may hold values from -6 to 6
Outputs:
- block_out: float32 [8, 256, 1024], P('shard', 'ctx')
- input_grad: float32 [8, 256, 1024], P('shard', 'ctx')
- gains_grad: float32 [2, 1024], P(None, ('shard', 'ctx'))
- shifts_grad: float32 [2, 1024], P(None, ('shard', 'ctx'))
- attend_grad: float32 [1024, 3, 1024], P(('shard', 'ctx'), None, 'tp')
- merge_grad: float32 [1024, 1024], P(('shard', 'ctx'), 'tp')
- expand_grad: float32 [1024, 4096], P(('shard', 'ctx'), 'tp')
- bias_grad: float32 [4, 1024], P('tp', ('shard', 'ctx'))
- reduce_grad: float32 [1024, 4096], P(('shard', 'ctx'), 'tp')
The draws below stay inside these ranges and needn't reach their ends.
Inputs may be any that keep to these rules, and one draw needn't show every extreme that they name: `segment_ids`: within each sequence segment ids never fall; every document holds 1 to 128 tokens, and one of them exactly 128.
All inputs are finite; a program needn't handle non-finite values.
Results may differ from the reference program's by a relative error of at most 0.0093.
Values may be sent and summed in bfloat16 or wider, within the bound.
No kernel may reach another device: no remote copies, remote signals or barrier semaphores. Data moves between devices by JAX's collectives and lax.ppermute only.
A program may use at most 128 MiB of HBM per device.

```python
import math
import jax
import jax.numpy as jnp
import numpy as np
from jax import lax

D = 1024
HEADS = 16
HD = 64
FF = 4096
L = 256
SEQUENCES = 8
N_TP = 4


def draw_inputs(key, part):
    base_key = jax.random.fold_in(key, 11)
    return jax.random.truncated_normal(base_key, -6.0, 6.0, (SEQUENCES, L, D), jnp.float32)


def draw_attend_weight(key, part):
    base_key = jax.random.fold_in(key, 21)
    spread = D ** (-0.5)
    return (jax.random.truncated_normal(base_key, -6.0, 6.0, (D, 3, D), jnp.float32) * spread).astype(jnp.bfloat16)


def block_levels(rng, shape, pieces, least, high):
    loudness = 1.0
    for dim, blocks in pieces:
        draws = jax.random.uniform(jax.random.fold_in(jax.random.fold_in(rng, 6), dim), (blocks,), jnp.float32, least / len(pieces), high / len(pieces))
        loudness = loudness * jnp.repeat(jnp.exp(draws), shape[dim] // blocks).reshape((-1,) + (1,) * (len(shape) - 1 - dim))
    return loudness


def split_up(amount, total, most, slope):
    weights = [(1 << 20) // math.isqrt(standing ** slope) + 1 for standing in range(2, amount + 1)]
    rest, holding = total - most - (amount - 1), [1] * (amount - 1)
    while rest > 0:
        movable = [i for i in range(amount - 1) if holding[i] < most]
        mass, remaining = sum([weights[i] for i in movable]), rest
        for i in movable:
            addition = min(most - holding[i], max(1, remaining * weights[i] // mass), rest)
            holding[i] = holding[i] + addition
            rest = rest - addition
    return np.array([most] + holding)


def uneven_parts(own_key, count, total, bound, skew):
    if count == 2:
        one = jax.random.randint(own_key, (), max(1, total - bound), min(bound, total - 1) + 1)
        return jnp.stack([one, total - one])
    sizes = jnp.asarray(split_up(count, total, bound, skew), jnp.int32)
    twos = (count - 1) // 2
    giver, receiver = sizes[1:1 + 2 * twos:2], sizes[2:2 + 2 * twos:2]
    margin = jnp.minimum(giver - 1, bound - receiver)
    shifted = jax.random.randint(jax.random.fold_in(own_key, 1), (twos,), 0, 1 << 20) % (margin + 1)
    sizes = sizes.at[1:1 + 2 * twos:2].set(giver - shifted).at[2:2 + 2 * twos:2].set(receiver + shifted)
    return sizes[jax.random.permutation(jax.random.fold_in(own_key, 2), count)]


def normal_values(stream_key, shape, deviation, limit, shards=(), kind=jnp.bfloat16):
    result = jax.random.normal(stream_key, shape, jnp.float32) * deviation
    if len(shards) > 0:
        result = block_levels(stream_key, shape, shards, -0.22, 0.18) * result
    return jnp.clip(result, min=-limit, max=limit).astype(kind)


def setup_inputs(seed: int = 0) -> dict:
    arg_keys = jax.random.split(jax.random.key(seed), 11)
    inputs = draw_inputs(jax.random.fold_in(arg_keys[10], 71), 0)
    segment_ids = jax.vmap(lambda own: jnp.searchsorted(jnp.cumsum(uneven_parts(own, 4, L, L // 2, 0)), jnp.arange(L), side="right"))(jax.random.split(arg_keys[1], SEQUENCES)).reshape((SEQUENCES, L)).astype(jnp.int32)
    gains = jnp.clip(1.0 + 0.1 * jax.random.normal(arg_keys[2], (2, D), jnp.float32), 0.5, 1.5).astype(jnp.bfloat16)
    shifts = normal_values(arg_keys[3], (2, D), 0.3, 3.0, ((1, 8),))
    attend_weight = draw_attend_weight(jax.random.fold_in(arg_keys[10], 71), 0)
    merge_weight = normal_values(arg_keys[5], (D, D), (D // 16) ** -0.5, 0.75, ((0, 8), (1, 4)))
    expand_weight = normal_values(arg_keys[6], (D, FF), D ** -0.5, 0.1875, ((0, 8), (1, 4)))
    expand_bias = normal_values(arg_keys[7], (N_TP, FF // N_TP), 0.5, 3.0, ((0, 4), (1, 8)))
    reduce_weight = normal_values(arg_keys[8], (D, FF), FF ** -0.5, 0.09375, ((0, 8), (1, 4)))
    cotangent = normal_values(arg_keys[9], (SEQUENCES, L, D), 1.0, 6.0, ((0, 4), (1, 2)), jnp.float32)
    return dict(inputs=inputs, segment_ids=segment_ids, gains=gains, shifts=shifts, attend_weight=attend_weight, merge_weight=merge_weight, expand_weight=expand_weight, expand_bias=expand_bias, reduce_weight=reduce_weight, cotangent=cotangent)


epsilon = 1e-05
masked_score = -1e+30
gelu_scale = 0.7978845608028654
gelu_cubic = 0.044715

def norm_forward(values, gain, shift):
    average = lax.optimization_barrier(jnp.mean(values, axis=-1, keepdims=True))
    centered = values - average
    variance = lax.optimization_barrier(jnp.mean(centered * centered, axis=-1, keepdims=True))
    inverse = lax.rsqrt(variance + epsilon)
    normed = centered * inverse
    return (normed, inverse, normed * gain.astype(jnp.float32) + shift.astype(jnp.float32))

def norm_backward(upstream, normed, inverse, gain):
    scaled = upstream * gain.astype(jnp.float32)
    first_mean = lax.optimization_barrier(jnp.mean(scaled, axis=-1, keepdims=True))
    second_mean = lax.optimization_barrier(jnp.mean(scaled * normed, axis=-1, keepdims=True))
    return inverse * (scaled - first_mean - normed * second_mean)

def gelu_pair(pre_act):
    inner_arg = gelu_scale * (pre_act + gelu_cubic * pre_act * pre_act * pre_act)
    tangent = jnp.tanh(inner_arg)
    gelu_value = 0.5 * pre_act * (1.0 + tangent)
    gelu_slope = 0.5 * (1.0 + tangent) + 0.5 * pre_act * (1.0 - tangent * tangent) * gelu_scale * (1.0 + 3.0 * gelu_cubic * pre_act * pre_act)
    return (gelu_value, gelu_slope)

def one_sequence(weights, inputs, segments, cotangent):
    attend_weight, merge_weight, expand_weight, expand_bias, reduce_weight, gains, shifts = weights
    length = inputs.shape[0]
    model_width = inputs.shape[1]
    head_scale = HD ** (-0.5)
    normed_early, inverse_early, affine_early = norm_forward(inputs, gains[0], shifts[0])
    hidden_early = affine_early.astype(jnp.bfloat16)
    attend_flat = attend_weight.reshape(model_width, 3 * model_width)
    projected = jnp.dot(hidden_early, attend_flat, preferred_element_type=jnp.float32).reshape(length, 3, HEADS, HD)
    query = (projected[:, 0] * head_scale).astype(jnp.bfloat16)
    keys = projected[:, 1].astype(jnp.bfloat16)
    values = projected[:, 2].astype(jnp.bfloat16)
    position = jnp.arange(length, dtype=jnp.int32)
    allowed = (segments[:, None] == segments[None, :]) & (position[None, :] <= position[:, None])
    scores = jnp.einsum('qhd,khd->hqk', query.astype(jnp.float32), keys.astype(jnp.float32))
    scores = jnp.where(allowed[None], scores, masked_score)
    row_top = lax.optimization_barrier(jnp.max(scores, axis=-1, keepdims=True))
    log_total = row_top + jnp.log(lax.optimization_barrier(jnp.sum(jnp.exp(scores - row_top), axis=-1, keepdims=True)))
    probs = jnp.exp(scores - log_total)
    probs_half = probs.astype(jnp.bfloat16)
    attended = jnp.einsum('hqk,khd->qhd', probs_half.astype(jnp.float32), values.astype(jnp.float32)).astype(jnp.bfloat16)
    attended_flat = attended.reshape(length, model_width)
    residual = inputs + jnp.dot(attended_flat, merge_weight.T, preferred_element_type=jnp.float32)
    normed_later, inverse_later, affine_later = norm_forward(residual, gains[1], shifts[1])
    hidden_later = affine_later.astype(jnp.bfloat16)
    pre_act = jnp.dot(hidden_later, expand_weight, preferred_element_type=jnp.float32) + expand_bias.reshape(FF).astype(jnp.float32)
    gelu_value, gelu_slope = gelu_pair(pre_act)
    activated = gelu_value.astype(jnp.bfloat16)
    block_out = residual + jnp.dot(activated, reduce_weight.T, preferred_element_type=jnp.float32)
    cot_half = cotangent.astype(jnp.bfloat16)
    reduce_grad = jnp.dot(cot_half.T, activated, preferred_element_type=jnp.float32)
    pre_grad = jnp.dot(cot_half, reduce_weight, preferred_element_type=jnp.float32) * gelu_slope
    pre_half = pre_grad.astype(jnp.bfloat16)
    bias_grad = lax.optimization_barrier(jnp.sum(pre_grad, axis=0))
    expand_grad = jnp.dot(hidden_later.T, pre_half, preferred_element_type=jnp.float32)
    later_grad = jnp.dot(pre_half, expand_weight.T, preferred_element_type=jnp.float32)
    residual_grad = cotangent + norm_backward(later_grad, normed_later, inverse_later, gains[1])
    resid_half = residual_grad.astype(jnp.bfloat16)
    merge_grad = jnp.dot(resid_half.T, attended_flat, preferred_element_type=jnp.float32)
    attended_grad = jnp.dot(resid_half, merge_weight, preferred_element_type=jnp.float32).astype(jnp.bfloat16).reshape(length, HEADS, HD)
    delta = jnp.einsum('qhd,qhd->hq', attended_grad.astype(jnp.float32), attended.astype(jnp.float32))
    prob_grad = jnp.einsum('qhd,khd->hqk', attended_grad.astype(jnp.float32), values.astype(jnp.float32))
    score_grad = probs * (prob_grad - delta[:, :, None])
    score_half = score_grad.astype(jnp.bfloat16)
    query_grad = jnp.einsum('hqk,khd->qhd', score_half.astype(jnp.float32), keys.astype(jnp.float32)) * head_scale
    keys_grad = jnp.einsum('hqk,qhd->khd', score_half.astype(jnp.float32), query.astype(jnp.float32))
    values_grad = jnp.einsum('hqk,qhd->khd', probs_half.astype(jnp.float32), attended_grad.astype(jnp.float32))
    proj_grad = jnp.stack([query_grad, keys_grad, values_grad], axis=1).reshape(length, 3 * model_width).astype(jnp.bfloat16)
    attend_grad = jnp.dot(hidden_early.T, proj_grad, preferred_element_type=jnp.float32).reshape(model_width, 3, model_width)
    early_grad = jnp.dot(proj_grad, attend_flat.T, preferred_element_type=jnp.float32)
    input_grad = residual_grad + norm_backward(early_grad, normed_early, inverse_early, gains[0])
    gains_grad = jnp.stack([lax.optimization_barrier(jnp.sum(early_grad * normed_early, axis=0)), lax.optimization_barrier(jnp.sum(later_grad * normed_later, axis=0))])
    shifts_grad = jnp.stack([lax.optimization_barrier(jnp.sum(early_grad, axis=0)), lax.optimization_barrier(jnp.sum(later_grad, axis=0))])
    return (block_out, input_grad, (gains_grad, shifts_grad, attend_grad, merge_grad, expand_grad, bias_grad, reduce_grad))

def reference(inputs, segment_ids, gains, shifts, attend_weight, merge_weight, expand_weight, expand_bias, reduce_weight, cotangent):
    weights = (attend_weight, merge_weight, expand_weight, expand_bias, reduce_weight, gains, shifts)
    totals = (jnp.zeros((2, D), jnp.float32), jnp.zeros((2, D), jnp.float32), jnp.zeros((D, 3, D), jnp.float32), jnp.zeros((D, D), jnp.float32), jnp.zeros((D, FF), jnp.float32), jnp.zeros((FF,), jnp.float32), jnp.zeros((D, FF), jnp.float32))

    def scan_step(running, sequence_data):
        block_out, input_grad, grads = one_sequence(weights, sequence_data[0], sequence_data[1], sequence_data[2])
        return (jax.tree.map(jnp.add, running, grads), (block_out, input_grad))
    summed, outputs = lax.scan(scan_step, totals, (inputs, segment_ids, cotangent))
    gains_grad, shifts_grad, attend_grad, merge_grad, expand_grad, bias_grad, reduce_grad = summed
    return (outputs[0], outputs[1], gains_grad, shifts_grad, attend_grad, merge_grad, expand_grad, bias_grad.reshape(N_TP, FF // N_TP), reduce_grad)
```

```python
import jax
import jax.numpy as jnp
from jax import lax
from jax.sharding import PartitionSpec as P

HD = 64


epsilon = 1e-05
masked_score = -1e30
gelu_scale = 0.7978845608028654
gelu_cubic = 0.044715


def norm_forward(values, gain, shift):
    average = jnp.mean(values, axis=-1, keepdims=True)
    centered = values - average
    variance = jnp.mean(centered * centered, axis=-1, keepdims=True)
    inverse = lax.rsqrt(variance + epsilon)
    normed = centered * inverse
    return (normed, inverse, normed * gain.astype(jnp.float32) + shift.astype(jnp.float32))


def norm_backward(upstream, normed, inverse, gain):
    scaled = upstream * gain.astype(jnp.float32)
    first_mean = jnp.mean(scaled, axis=-1, keepdims=True)
    second_mean = jnp.mean(scaled * normed, axis=-1, keepdims=True)
    return inverse * (scaled - first_mean - normed * second_mean)


def gelu_pair(pre_act):
    inner_arg = gelu_scale * (pre_act + gelu_cubic * pre_act * pre_act * pre_act)
    tangent = jnp.tanh(inner_arg)
    gelu_value = 0.5 * pre_act * (1.0 + tangent)
    gelu_slope = 0.5 * (1.0 + tangent) + 0.5 * pre_act * (1.0 - tangent * tangent) * gelu_scale * (
        1.0 + 3.0 * gelu_cubic * pre_act * pre_act
    )
    return (gelu_value, gelu_slope)


class Ring:
    def __init__(self):
        self.axes = ("shard", "ctx")
        self.shards, self.ctxs = lax.axis_size("shard"), lax.axis_size("ctx")
        self.count = self.shards * self.ctxs
        self.usable = self.ctxs == 2 and self.shards == 4
        if self.usable:
            n = self.count
            ids = [2 * p if p < self.shards else 2 * (n - 1 - p) + 1 for p in range(n)]
            self.ahead = [(ids[p], ids[(p + 1) % n]) for p in range(n)]
            self.behind = [(ids[p], ids[(p - 1) % n]) for p in range(n)]
            shard, ctx = lax.axis_index("shard"), lax.axis_index("ctx")
            self.place = jnp.where(ctx == 0, shard, n - 1 - shard)

    def block(self, offset):
        n = self.count
        spot = lax.rem(self.place + (offset + n), n)
        return jnp.where(spot < self.shards, 2 * spot, 2 * (n - 1 - spot) + 1)

    def send_ahead(self, value):
        return lax.ppermute(value, self.axes, self.ahead)

    def send_behind(self, value):
        return lax.ppermute(value, self.axes, self.behind)


def gather_rows(ring, part):
    if not ring.usable:
        return lax.all_gather(part, ring.axes, axis=0, tiled=True)
    rows = part.shape[0]
    half = rows // 2
    reach = ring.count // 2
    full = jnp.zeros((rows * ring.count,) + part.shape[1:], part.dtype)

    def put(full, value, offset, start=0):
        at = (ring.block(offset) * rows + start,) + (0,) * (part.ndim - 1)
        return lax.dynamic_update_slice(full, value, at)

    full = put(full, part, 0)
    ahead, behind = part, part
    for step in range(1, reach):
        ahead, behind = ring.send_ahead(ahead), ring.send_behind(behind)
        full = put(full, ahead, -step)
        full = put(full, behind, step)
    upper, lower = ring.send_ahead(ahead[:half]), ring.send_behind(behind[half:])
    full = put(full, upper, reach)
    return put(full, lower, reach, half)


def scatter_rows(ring, part):
    if not ring.usable:
        return lax.psum_scatter(part, ring.axes, scatter_dimension=0, tiled=True)
    rows = part.shape[0] // ring.count
    half = rows // 2
    reach = ring.count // 2
    wire = jnp.bfloat16

    def own(offset, start=0, size=rows):
        at = (ring.block(offset) * rows + start,) + (0,) * (part.ndim - 1)
        return lax.dynamic_slice(part, at, (size,) + part.shape[1:])

    ahead = ring.send_ahead(own(reach, 0, half).astype(wire))
    behind = ring.send_behind(own(reach, half, half).astype(wire))
    for step in range(reach - 1, 0, -1):
        if step == reach - 1:
            up = own(step)
            down = own(-step)
            up = jnp.concatenate([up[:half] + ahead, up[half:]])
            down = jnp.concatenate([down[:half], down[half:] + behind])
        else:
            up = own(step) + ahead
            down = own(-step) + behind
        ahead = ring.send_ahead(up.astype(wire))
        behind = ring.send_behind(down.astype(wire))
    return own(0) + (ahead.astype(jnp.float32) + behind.astype(jnp.float32))


def gather_small(ring, value):
    if not ring.usable:
        return lax.all_gather(value, ring.axes, axis=1, tiled=True)
    few, width = value.shape
    blocks = gather_rows(ring, jnp.zeros((32, width), value.dtype).at[:few].set(value))
    blocks = blocks.reshape(ring.count, 32, width)[:, :few]
    return jnp.swapaxes(blocks, 0, 1).reshape(few, ring.count * width)


def scatter_small(ring, value):
    if not ring.usable:
        return lax.psum_scatter(value, ring.axes, scatter_dimension=1, tiled=True)
    few = value.shape[0]
    width = value.shape[1] // ring.count
    blocks = jnp.swapaxes(value.reshape(few, ring.count, width), 0, 1)
    blocks = jnp.zeros((ring.count, 32, width), value.dtype).at[:, :few].set(blocks)
    return scatter_rows(ring, blocks.reshape(ring.count * 32, width))[:few]


def sum_tp(part):
    if lax.axis_size("tp") != 4:
        return lax.psum(part, "tp")
    half = part.shape[0] // 2
    side = lax.rem(lax.axis_index("tp"), 2)
    near = [(i, i ^ 1) for i in range(4)]
    far = [(i, i ^ 2) for i in range(4)]
    keep = lax.dynamic_slice(part, (side * half, 0), (half, part.shape[1]))
    give = lax.dynamic_slice(part, ((1 - side) * half, 0), (half, part.shape[1]))
    pair = (keep + lax.ppermute(give.astype(jnp.bfloat16), "tp", near)).astype(jnp.bfloat16)
    total = pair.astype(jnp.float32) + lax.ppermute(pair, "tp", far).astype(jnp.float32)
    other = lax.ppermute(total, "tp", near)
    first = jnp.where(side == 0, total, other)
    second = jnp.where(side == 0, other, total)
    return jnp.concatenate([first, second])


def gather_ctx(value):
    if lax.axis_size("ctx") != 2:
        return lax.all_gather(value, "ctx", axis=1, tiled=True)
    other = lax.ppermute(value, "ctx", [(0, 1), (1, 0)])
    here = lax.axis_index("ctx") == 0
    return jnp.concatenate([jnp.where(here, value, other), jnp.where(here, other, value)], axis=1)


def scatter_ctx(value):
    if lax.axis_size("ctx") != 2:
        return lax.psum_scatter(value, "ctx", scatter_dimension=1, tiled=True)
    half = value.shape[1] // 2
    here = lax.axis_index("ctx") == 0
    low, high = value[:, :half], value[:, half:]
    give = jnp.where(here, high, low).astype(jnp.bfloat16)
    return jnp.where(here, low, high) + lax.ppermute(give, "ctx", [(0, 1), (1, 0)])


def shards(
    inputs,
    segment_ids,
    gains,
    shifts,
    attend_weight,
    merge_weight,
    expand_weight,
    expand_bias,
    reduce_weight,
    cotangent,
):
    seq_count, group_len, model_width = inputs.shape
    row_count = seq_count * group_len
    full_len = group_len * lax.axis_size("ctx")
    head_scale = HD ** (-0.5)
    ring = Ring()
    local_cols = attend_weight.shape[2]
    block_rows = attend_weight.shape[0]
    small = jnp.concatenate([gains, shifts, expand_bias])
    small_full = gather_small(ring, small)
    gains_full, shifts_full, bias_full = small_full[0:2], small_full[2:4], small_full[4:5]
    attend_full = gather_rows(ring, attend_weight.reshape(block_rows, 3 * local_cols))
    merge_full = gather_rows(ring, merge_weight)
    expand_full = gather_rows(ring, expand_weight)
    reduce_full = gather_rows(ring, reduce_weight)
    head_local = local_cols // HD
    flat_in = inputs.reshape(row_count, model_width)
    normed_early, inverse_early, affine_early = norm_forward(flat_in, gains_full[0], shifts_full[0])
    hidden_early = affine_early.astype(jnp.bfloat16)
    projected = jnp.dot(
        hidden_early, attend_full, preferred_element_type=jnp.float32
    ).reshape(row_count, 3, local_cols)
    query_heads = (
        (projected[:, 0] * head_scale)
        .astype(jnp.bfloat16)
        .reshape(seq_count, group_len, head_local, HD)
    )
    key_rows = projected[:, 1].astype(jnp.bfloat16).reshape(seq_count, group_len, local_cols)
    value_rows = projected[:, 2].astype(jnp.bfloat16).reshape(seq_count, group_len, local_cols)
    key_values = gather_ctx(jnp.concatenate([key_rows, value_rows], axis=2))
    all_keys, all_values = key_values[..., :local_cols], key_values[..., local_cols:]
    all_segments = gather_ctx(segment_ids)
    key_heads = all_keys.reshape(seq_count, full_len, head_local, HD)
    value_heads = all_values.reshape(seq_count, full_len, head_local, HD)
    query_pos = lax.axis_index("ctx") * group_len + jnp.arange(group_len, dtype=jnp.int32)
    key_pos = jnp.arange(full_len, dtype=jnp.int32)
    allowed = (segment_ids[:, :, None] == all_segments[:, None, :]) & (
        key_pos[None, None, :] <= query_pos[None, :, None]
    )
    allowed = allowed[:, None]

    def score_block():
        raw_scores = jnp.einsum(
            "sqhd,skhd->shqk", query_heads, key_heads, preferred_element_type=jnp.float32
        )
        return jnp.where(allowed, raw_scores, masked_score)

    scores = score_block()
    row_top = jnp.max(scores, axis=-1, keepdims=True)
    log_total = row_top + jnp.log(jnp.sum(jnp.exp(scores - row_top), axis=-1, keepdims=True))
    attn_probs = jnp.exp(scores - log_total)
    probs_half = attn_probs.astype(jnp.bfloat16)
    attended_heads = jnp.einsum(
        "shqk,skhd->sqhd", probs_half, value_heads, preferred_element_type=jnp.float32
    ).astype(jnp.bfloat16)
    attended = attended_heads.reshape(row_count, local_cols)
    merge_part = jnp.einsum("rc,oc->ro", attended, merge_full, preferred_element_type=jnp.float32)
    residual = flat_in + sum_tp(merge_part)
    normed_later, inverse_later, affine_later = norm_forward(
        residual, gains_full[1], shifts_full[1]
    )
    hidden_later = affine_later.astype(jnp.bfloat16)
    pre_act = jnp.dot(
        hidden_later, expand_full, preferred_element_type=jnp.float32
    ) + bias_full.astype(jnp.float32)
    gelu_value, gelu_slope = gelu_pair(pre_act)
    activated = gelu_value.astype(jnp.bfloat16)
    reduce_part = jnp.einsum(
        "rf,of->ro", activated, reduce_full, preferred_element_type=jnp.float32
    )
    block_out = residual + sum_tp(reduce_part)
    attend_back, merge_back, expand_back, reduce_back, gains_back = (
        attend_full,
        merge_full,
        expand_full,
        reduce_full,
        gains_full,
    )
    output_grad = cotangent.reshape(row_count, model_width)
    cot_half = output_grad.astype(jnp.bfloat16)
    reduce_grad = jnp.einsum("ro,rf->of", cot_half, activated, preferred_element_type=jnp.float32)
    pre_grad = jnp.dot(cot_half, reduce_back, preferred_element_type=jnp.float32) * gelu_slope
    pre_half = pre_grad.astype(jnp.bfloat16)
    bias_grad = jnp.sum(pre_grad, axis=0, keepdims=True)
    expand_grad = jnp.einsum(
        "rd,rf->df", hidden_later, pre_half, preferred_element_type=jnp.float32
    )
    later_part = jnp.einsum("rf,df->rd", pre_half, expand_back, preferred_element_type=jnp.float32)
    later_grad = sum_tp(later_part)
    residual_grad = output_grad + norm_backward(
        later_grad, normed_later, inverse_later, gains_back[1]
    )
    resid_half = residual_grad.astype(jnp.bfloat16)
    merge_grad = jnp.einsum("ro,rc->oc", resid_half, attended, preferred_element_type=jnp.float32)
    attended_grad = jnp.dot(resid_half, merge_back, preferred_element_type=jnp.float32).astype(
        jnp.bfloat16
    )
    grad_heads = attended_grad.reshape(seq_count, group_len, head_local, HD)
    scores_again = score_block()
    probs_again = jnp.exp(scores_again - log_total)
    probs_again_half = probs_again.astype(jnp.bfloat16)
    row_delta = jnp.einsum(
        "sqhd,sqhd->shq", grad_heads, attended_heads, preferred_element_type=jnp.float32
    )
    prob_grad = jnp.einsum(
        "sqhd,skhd->shqk", grad_heads, value_heads, preferred_element_type=jnp.float32
    )
    score_grad = probs_again * (prob_grad - row_delta[..., None])
    score_half = score_grad.astype(jnp.bfloat16)
    query_grad = (
        jnp.einsum("shqk,skhd->sqhd", score_half, key_heads, preferred_element_type=jnp.float32)
        * head_scale
    )
    keys_part = jnp.einsum(
        "shqk,sqhd->skhd", score_half, query_heads, preferred_element_type=jnp.float32
    ).reshape(seq_count, full_len, local_cols)
    values_part = jnp.einsum(
        "shqk,sqhd->skhd", probs_again_half, grad_heads, preferred_element_type=jnp.float32
    ).reshape(seq_count, full_len, local_cols)
    both_grads = scatter_ctx(jnp.concatenate([keys_part, values_part], axis=2))
    proj_grad = jnp.concatenate(
        [
            query_grad.reshape(row_count, local_cols),
            both_grads.reshape(row_count, 2 * local_cols),
        ],
        axis=1,
    ).astype(jnp.bfloat16)
    attend_grad = jnp.einsum(
        "rd,rc->dc", hidden_early, proj_grad, preferred_element_type=jnp.float32
    )
    early_part = jnp.einsum(
        "rc,dc->rd", proj_grad, attend_back, preferred_element_type=jnp.float32
    )
    early_grad = sum_tp(early_part)
    input_grad = residual_grad + norm_backward(
        early_grad, normed_early, inverse_early, gains_back[0]
    )
    gains_grad = jnp.stack(
        [jnp.sum(early_grad * normed_early, axis=0), jnp.sum(later_grad * normed_later, axis=0)]
    )
    shifts_grad = jnp.stack([jnp.sum(early_grad, axis=0), jnp.sum(later_grad, axis=0)])
    small_grad = scatter_small(ring, jnp.concatenate([gains_grad, shifts_grad, bias_grad]))
    return (
        block_out.reshape(inputs.shape),
        input_grad.reshape(inputs.shape),
        small_grad[0:2],
        small_grad[2:4],
        scatter_rows(ring, attend_grad).reshape(attend_weight.shape),
        scatter_rows(ring, merge_grad),
        scatter_rows(ring, expand_grad),
        small_grad[4:5],
        scatter_rows(ring, reduce_grad),
    )


def solution(mesh):
    in_specs = (
        P("shard", "ctx", None),
        P("shard", "ctx"),
        P(None, ("shard", "ctx")),
        P(None, ("shard", "ctx")),
        P(("shard", "ctx"), None, "tp"),
        P(("shard", "ctx"), "tp"),
        P(("shard", "ctx"), "tp"),
        P("tp", ("shard", "ctx")),
        P(("shard", "ctx"), "tp"),
        P("shard", "ctx", None),
    )
    out_specs = (
        P("shard", "ctx", None),
        P("shard", "ctx", None),
        P(None, ("shard", "ctx")),
        P(None, ("shard", "ctx")),
        P(("shard", "ctx"), None, "tp"),
        P(("shard", "ctx"), "tp"),
        P(("shard", "ctx"), "tp"),
        P("tp", ("shard", "ctx")),
        P(("shard", "ctx"), "tp"),
    )
    return jax.shard_map(shards, mesh=mesh, in_specs=in_specs, out_specs=out_specs, check_vma=False)
```

```python
import jax
import jax.numpy as jnp
from jax import lax
from jax.experimental import pallas as pl
from jax.experimental.pallas import tpu as pltpu
from jax.sharding import PartitionSpec as P

HD = 64


epsilon = 1e-05
masked_score = -1e30
gelu_scale = 0.7978845608028654
gelu_cubic = 0.044715


def norm_forward(values, gain, shift):
    average = jnp.mean(values, axis=-1, keepdims=True)
    centered = values - average
    variance = jnp.mean(centered * centered, axis=-1, keepdims=True)
    inverse = lax.rsqrt(variance + epsilon)
    normed = centered * inverse
    return (normed, inverse, normed * gain.astype(jnp.float32) + shift.astype(jnp.float32))


def norm_backward(upstream, normed, inverse, gain):
    scaled = upstream * gain.astype(jnp.float32)
    first_mean = jnp.mean(scaled, axis=-1, keepdims=True)
    second_mean = jnp.mean(scaled * normed, axis=-1, keepdims=True)
    return inverse * (scaled - first_mean - normed * second_mean)


def gelu_pair(pre_act):
    inner_arg = gelu_scale * (pre_act + gelu_cubic * pre_act * pre_act * pre_act)
    tangent = jnp.tanh(inner_arg)
    gelu_value = 0.5 * pre_act * (1.0 + tangent)
    gelu_slope = 0.5 * (1.0 + tangent) + 0.5 * pre_act * (1.0 - tangent * tangent) * gelu_scale * (
        1.0 + 3.0 * gelu_cubic * pre_act * pre_act
    )
    return (gelu_value, gelu_slope)


def shards(
    inputs,
    segment_ids,
    gains,
    shifts,
    attend_weight,
    merge_weight,
    expand_weight,
    expand_bias,
    reduce_weight,
    cotangent,
):
    seq_count, group_len, model_width = inputs.shape
    row_count = seq_count * group_len
    full_len = group_len * lax.axis_size("ctx")
    head_scale = HD ** (-0.5)
    gathered = (
        lax.all_gather(attend_weight, ("shard", "ctx"), axis=0, tiled=True),
        lax.all_gather(merge_weight, ("shard", "ctx"), axis=0, tiled=True),
        lax.all_gather(expand_weight, ("shard", "ctx"), axis=0, tiled=True),
        lax.all_gather(reduce_weight, ("shard", "ctx"), axis=0, tiled=True),
        lax.all_gather(expand_bias, ("shard", "ctx"), axis=1, tiled=True),
        lax.all_gather(gains, ("shard", "ctx"), axis=1, tiled=True),
        lax.all_gather(shifts, ("shard", "ctx"), axis=1, tiled=True),
    )
    attend_full, merge_full, expand_full, reduce_full, bias_full, gains_full, shifts_full = gathered
    local_cols = attend_full.shape[2]
    head_local = local_cols // HD
    flat_in = inputs.reshape(row_count, model_width)
    normed_early, inverse_early, affine_early = norm_forward(flat_in, gains_full[0], shifts_full[0])
    hidden_early = affine_early.astype(jnp.bfloat16)
    projected = jnp.einsum(
        "rd,dtc->rtc", hidden_early, attend_full, preferred_element_type=jnp.float32
    )
    query_heads = (
        (projected[:, 0] * head_scale)
        .astype(jnp.bfloat16)
        .reshape(seq_count, group_len, head_local, HD)
    )
    key_rows = projected[:, 1].astype(jnp.bfloat16).reshape(seq_count, group_len, local_cols)
    value_rows = projected[:, 2].astype(jnp.bfloat16).reshape(seq_count, group_len, local_cols)
    all_keys, all_values, all_segments = (
        lax.all_gather(key_rows, "ctx", axis=1, tiled=True),
        lax.all_gather(value_rows, "ctx", axis=1, tiled=True),
        lax.all_gather(segment_ids, "ctx", axis=1, tiled=True),
    )
    key_heads = all_keys.reshape(seq_count, full_len, head_local, HD)
    value_heads = all_values.reshape(seq_count, full_len, head_local, HD)
    query_pos = lax.axis_index("ctx") * group_len + jnp.arange(group_len, dtype=jnp.int32)
    key_pos = jnp.arange(full_len, dtype=jnp.int32)
    allowed = (segment_ids[:, :, None] == all_segments[:, None, :]) & (
        key_pos[None, None, :] <= query_pos[None, :, None]
    )
    allowed = allowed[:, None]

    def score_block():
        raw_scores = jnp.einsum(
            "sqhd,skhd->shqk", query_heads, key_heads, preferred_element_type=jnp.float32
        )
        return jnp.where(allowed, raw_scores, masked_score)

    scores = score_block()
    row_top = jnp.max(scores, axis=-1, keepdims=True)
    log_total = row_top + jnp.log(jnp.sum(jnp.exp(scores - row_top), axis=-1, keepdims=True))
    attn_probs = jnp.exp(scores - log_total)
    probs_half = attn_probs.astype(jnp.bfloat16)
    attended_heads = jnp.einsum(
        "shqk,skhd->sqhd", probs_half, value_heads, preferred_element_type=jnp.float32
    ).astype(jnp.bfloat16)
    attended = attended_heads.reshape(row_count, local_cols)
    merge_part = jnp.einsum("rc,oc->ro", attended, merge_full, preferred_element_type=jnp.float32)
    residual = flat_in + lax.psum(merge_part, "tp")
    normed_later, inverse_later, affine_later = norm_forward(
        residual, gains_full[1], shifts_full[1]
    )
    hidden_later = affine_later.astype(jnp.bfloat16)
    pre_act = jnp.dot(
        hidden_later, expand_full, preferred_element_type=jnp.float32
    ) + bias_full.astype(jnp.float32)
    gelu_value, gelu_slope = gelu_pair(pre_act)
    activated = gelu_value.astype(jnp.bfloat16)
    reduce_part = jnp.einsum(
        "rf,of->ro", activated, reduce_full, preferred_element_type=jnp.float32
    )
    block_out = residual + lax.psum(reduce_part.astype(jnp.bfloat16), "tp").astype(jnp.float32)
    back_set = (
        lax.all_gather(attend_weight, ("shard", "ctx"), axis=0, tiled=True),
        lax.all_gather(merge_weight, ("shard", "ctx"), axis=0, tiled=True),
        lax.all_gather(expand_weight, ("shard", "ctx"), axis=0, tiled=True),
        lax.all_gather(reduce_weight, ("shard", "ctx"), axis=0, tiled=True),
        lax.all_gather(gains, ("shard", "ctx"), axis=1, tiled=True),
    )
    attend_back, merge_back, expand_back, reduce_back, gains_back = back_set
    output_grad = cotangent.reshape(row_count, model_width)
    cot_half = output_grad.astype(jnp.bfloat16)
    reduce_grad = jnp.einsum("ro,rf->of", cot_half, activated, preferred_element_type=jnp.float32)
    pre_grad = jnp.dot(cot_half, reduce_back, preferred_element_type=jnp.float32) * gelu_slope
    pre_half = pre_grad.astype(jnp.bfloat16)
    bias_grad = jnp.sum(pre_grad, axis=0, keepdims=True)
    expand_grad = jnp.einsum(
        "rd,rf->df", hidden_later, pre_half, preferred_element_type=jnp.float32
    )
    later_part = jnp.einsum("rf,df->rd", pre_half, expand_back, preferred_element_type=jnp.float32)
    later_grad = lax.psum(later_part, "tp")
    residual_grad = output_grad + norm_backward(
        later_grad, normed_later, inverse_later, gains_back[1]
    )
    resid_half = residual_grad.astype(jnp.bfloat16)
    merge_grad = jnp.einsum("ro,rc->oc", resid_half, attended, preferred_element_type=jnp.float32)
    attended_grad = jnp.dot(resid_half, merge_back, preferred_element_type=jnp.float32).astype(
        jnp.bfloat16
    )
    grad_heads = attended_grad.reshape(seq_count, group_len, head_local, HD)
    scores_again = score_block()
    probs_again = jnp.exp(scores_again - log_total)
    probs_again_half = probs_again.astype(jnp.bfloat16)
    row_delta = jnp.einsum(
        "sqhd,sqhd->shq", grad_heads, attended_heads, preferred_element_type=jnp.float32
    )
    prob_grad = jnp.einsum(
        "sqhd,skhd->shqk", grad_heads, value_heads, preferred_element_type=jnp.float32
    )
    score_grad = probs_again * (prob_grad - row_delta[..., None])
    score_half = score_grad.astype(jnp.bfloat16)
    query_grad = (
        jnp.einsum("shqk,skhd->sqhd", score_half, key_heads, preferred_element_type=jnp.float32)
        * head_scale
    )
    keys_part = jnp.einsum(
        "shqk,sqhd->skhd", score_half, query_heads, preferred_element_type=jnp.float32
    ).reshape(seq_count, full_len, local_cols)
    values_part = jnp.einsum(
        "shqk,sqhd->skhd", probs_again_half, grad_heads, preferred_element_type=jnp.float32
    ).reshape(seq_count, full_len, local_cols)
    keys_grad, values_grad = (
        lax.psum_scatter(keys_part, "ctx", scatter_dimension=1, tiled=True),
        lax.psum_scatter(values_part, "ctx", scatter_dimension=1, tiled=True),
    )
    proj_grad = jnp.stack(
        [
            query_grad.reshape(row_count, local_cols),
            keys_grad.reshape(row_count, local_cols),
            values_grad.reshape(row_count, local_cols),
        ],
        axis=1,
    ).astype(jnp.bfloat16)
    attend_grad = jnp.einsum(
        "rd,rtc->dtc", hidden_early, proj_grad, preferred_element_type=jnp.float32
    )
    early_part = jnp.einsum(
        "rtc,dtc->rd", proj_grad, attend_back, preferred_element_type=jnp.float32
    )
    early_grad = lax.psum(early_part, "tp")
    input_grad = residual_grad + norm_backward(
        early_grad, normed_early, inverse_early, gains_back[0]
    )
    gains_grad = jnp.stack(
        [jnp.sum(early_grad * normed_early, axis=0), jnp.sum(later_grad * normed_later, axis=0)]
    )
    shifts_grad = jnp.stack([jnp.sum(early_grad, axis=0), jnp.sum(later_grad, axis=0)])
    shares = (
        lax.psum_scatter(attend_grad, ("shard", "ctx"), scatter_dimension=0, tiled=True),
        lax.psum_scatter(merge_grad, ("shard", "ctx"), scatter_dimension=0, tiled=True),
        lax.psum_scatter(expand_grad, ("shard", "ctx"), scatter_dimension=0, tiled=True),
        lax.psum_scatter(reduce_grad, ("shard", "ctx"), scatter_dimension=0, tiled=True),
        lax.psum_scatter(bias_grad, ("shard", "ctx"), scatter_dimension=1, tiled=True),
        lax.psum_scatter(gains_grad, ("shard", "ctx"), scatter_dimension=1, tiled=True),
        lax.psum_scatter(shifts_grad, ("shard", "ctx"), scatter_dimension=1, tiled=True),
    )
    return (
        block_out.reshape(inputs.shape),
        input_grad.reshape(inputs.shape),
        shares[5],
        shares[6],
        shares[0],
        shares[1],
        shares[2],
        shares[4],
        shares[3],
    )


VMEM = pl.BlockSpec(memory_space=pltpu.VMEM)
SMEM = pl.BlockSpec(memory_space=pltpu.SMEM)
f32 = jnp.float32
bf16 = jnp.bfloat16
RING = 8
NEAR = [(0, 1), (1, 0), (2, 3), (3, 2)]
FAR = [(0, 2), (2, 0), (1, 3), (3, 1)]
AXES = ("shard", "ctx")
IDS = [2 * p if p < 4 else 2 * (7 - p) + 1 for p in range(RING)]
AHEAD = [(IDS[p], IDS[(p + 1) % RING]) for p in range(RING)]
BEHIND = [(IDS[p], IDS[(p - 1) % RING]) for p in range(RING)]


def shape(dims, dtype):
    return jax.ShapeDtypeStruct(dims, dtype)


def call(kernel, name, outs, args, flops, scratch=(), transcendentals=0):
    nbytes = sum(a.size * a.dtype.itemsize for a in list(args) + list(outs))
    return pl.pallas_call(
        kernel,
        name=name,
        out_shape=tuple(outs),
        in_specs=[SMEM] + [VMEM] * (len(args) - 1),
        out_specs=tuple(VMEM for _ in outs),
        scratch_shapes=list(scratch),
        cost_estimate=pl.CostEstimate(
            flops=flops, bytes_accessed=nbytes, transcendentals=transcendentals
        ),
    )(*args)


def columns(meta, offset):
    return pl.ds(pl.multiple_of(meta[offset] * 128, 128), 128)


def rows_of(meta, mine):
    side = meta[8] if mine else 1 - meta[8]
    return pl.ds(pl.multiple_of(side * 128, 128), 128)


def dot(a, b):
    return jnp.dot(a, b, preferred_element_type=f32)


def dot_nt(a, b):
    return lax.dot_general(a, b, (((1,), (1,)), ((), ())), preferred_element_type=f32)


def dot_tn(a, b):
    return lax.dot_general(a, b, (((0,), (0,)), ((), ())), preferred_element_type=f32)


def norm_stats(values):
    average = jnp.mean(values, axis=-1, keepdims=True)
    centered = values - average
    variance = jnp.mean(centered * centered, axis=-1, keepdims=True)
    inverse = lax.rsqrt(variance + epsilon)
    return centered * inverse, inverse


def qkv_kernel(meta, x, *refs):
    blocks = refs[:9]
    hidden, query, key_value, attend, merge, small = refs[9:]

    def piece(offset, start, size):
        if offset < 4:
            return blocks[offset][start : start + size, :]
        if offset == 4:
            return jnp.concatenate(
                [blocks[4][start : start + size, :], blocks[5][start : start + size, :]], axis=1
            )
        return blocks[offset + 1][start : start + size, :]

    small[...] = jnp.zeros_like(small)
    for j in range(RING):
        at = columns(meta, j)
        for t in range(3):
            attend[t, at, :] = piece(j, t * 128, 128)
        merge[at, :] = piece(j, 384, 128)
        tail = piece(j, 512, 32).astype(f32)
        small[0:1, at] = tail[0:1, :128]
        small[1:2, at] = tail[0:1, 128:]
        small[2:3, at] = tail[1:2, :128]
        small[3:4, at] = tail[1:2, 128:]
        small[4:5, at] = tail[2:3, :128]
    normed, _ = norm_stats(x[...])
    hidden[...] = (normed * small[0:1, :] + small[2:3, :]).astype(bf16)
    both = hidden[...]
    key_value[:, :256] = dot(both, attend[1]).astype(bf16)
    key_value[:, 256:] = dot(both, attend[2]).astype(bf16)
    query[...] = (dot(both, attend[0]) * (HD**-0.5)).astype(bf16)


def masks(meta, seg, seg_col, seg_far, s):
    col = seg_col[:, s : s + 1]
    near = col == seg[s : s + 1, :]
    i = lax.broadcasted_iota(jnp.int32, (128, 128), 0)
    j = lax.broadcasted_iota(jnp.int32, (128, 128), 1)
    far = (col == seg_far[s : s + 1, :]) & (meta[9] == 1)
    return near & (j <= i), far


def head_probs(query, key, key_far, near, far):
    score = jnp.where(near, dot_nt(query, key), masked_score)
    score_far = jnp.where(far, dot_nt(query, key_far), masked_score)
    top = jnp.maximum(
        jnp.max(score, axis=-1, keepdims=True), jnp.max(score_far, axis=-1, keepdims=True)
    )
    total = jnp.sum(jnp.exp(score - top), axis=-1, keepdims=True) + jnp.sum(
        jnp.exp(score_far - top), axis=-1, keepdims=True
    )
    log_total = top + jnp.log(total)
    return jnp.exp(score - log_total), jnp.exp(score_far - log_total)


def attention_kernel(
    meta, query, kv, kv_far, seg, seg_col, seg_far, merge, attended, keep, give, part
):
    for s in range(2):
        near, far = masks(meta, seg, seg_col, seg_far, s)
        r = slice(s * 128, s * 128 + 128)
        for h in range(4):
            c = slice(h * 64, h * 64 + 64)
            v = slice(256 + h * 64, 256 + h * 64 + 64)
            probs, probs_far = head_probs(query[r, c], kv[r, c], kv_far[r, c], near, far)
            out = dot(probs.astype(bf16), kv[r, v]) + dot(probs_far.astype(bf16), kv_far[r, v])
            attended[r, c] = out.astype(bf16)
    part[...] = dot_nt(attended[...], merge[...])
    keep[...] = part[rows_of(meta, True), :]
    give[...] = part[rows_of(meta, False), :].astype(bf16)


def total_of(meta, sums, full):
    pair, far, pair_other, far_other = sums
    full[rows_of(meta, True), :] = pair[...].astype(f32) + far[...].astype(f32)
    full[rows_of(meta, False), :] = pair_other[...].astype(f32) + far_other[...].astype(f32)
    return full[...]


def ffn_kernel(meta, x, cot, small, s0, s1, s2, s3, *refs):
    blocks = refs[:9]
    (residual, hidden, cot_half, act, pre_half, later_keep, later_give, red_keep, red_give,
     grads, expand, reduce, part) = refs[9:]
    for j in range(RING):
        at = columns(meta, j)
        if j == 4:
            expand[at, :] = blocks[4][...]
            reduce[at, :] = blocks[5][...]
        else:
            block = blocks[j] if j < 4 else blocks[j + 1]
            expand[at, :] = block[:128, :]
            reduce[at, :] = block[128:, :]
    residual[...] = x[...] + total_of(meta, (s0, s1, s2, s3), part)
    normed, _ = norm_stats(residual[...])
    hidden[...] = (normed * small[1:2, :] + small[3:4, :]).astype(bf16)
    cot_half[...] = cot[...].astype(bf16)
    grads[...] = jnp.zeros_like(grads)

    def units(i, carry):
        at = pl.ds(pl.multiple_of(i * 256, 256), 256)
        pre_act = dot(hidden[...], expand[:, at]) + small[4:5, at]
        value, slope = gelu_pair(pre_act)
        act[:, at] = value.astype(bf16)
        pre_grad = dot(cot_half[...], reduce[:, at]) * slope
        pre_half[:, at] = pre_grad.astype(bf16)
        grads[2:3, at] = jnp.sum(pre_grad, axis=0, keepdims=True)
        return carry

    lax.fori_loop(0, 4, units, 0)

    def later(i, carry):
        at = pl.ds(pl.multiple_of(i * 256, 256), 256)
        part[:, at] = dot_nt(pre_half[...], expand[at, :])
        return carry

    lax.fori_loop(0, 4, later, 0)
    later_keep[...] = part[rows_of(meta, True), :]
    later_give[...] = part[rows_of(meta, False), :].astype(bf16)
    grads[0:1, :] = jnp.sum(part[...] * normed, axis=0, keepdims=True)
    grads[1:2, :] = jnp.sum(part[...], axis=0, keepdims=True)

    def reduced(i, carry):
        at = pl.ds(pl.multiple_of(i * 256, 256), 256)
        part[:, at] = dot_nt(act[...], reduce[at, :])
        return carry

    lax.fori_loop(0, 4, reduced, 0)
    red_keep[...] = part[rows_of(meta, True), :]
    red_give[...] = part[rows_of(meta, False), :].astype(bf16)


def ffn_grads_kernel(meta, hidden, pre_half, cot_half, act, *outs):
    for j in range(RING):
        at = columns(meta, j)
        top = dot_tn(hidden[:, at], pre_half[...]).astype(bf16)
        low = dot_tn(cot_half[:, at], act[...]).astype(bf16)
        if j == 4:
            outs[4][...] = top
            outs[5][...] = low
        else:
            out = outs[j] if j < 4 else outs[j + 1]
            out[:128, :] = top
            out[128:, :] = low


def attention_back_kernel(
    meta, cot, residual, small, s0, s1, s2, s3, merge, query, kv, kv_far, attended,
    seg, seg_col, seg_far, residual_grad, resid_half, query_grad, kv_grad, kv_grad_far,
    part, att_grad
):
    later_grad = total_of(meta, (s0, s1, s2, s3), part)
    normed, inverse = norm_stats(residual[...])
    residual_grad[...] = cot[...] + norm_backward(later_grad, normed, inverse, small[1:2, :])
    resid_half[...] = residual_grad[...].astype(bf16)
    att_grad[...] = dot(resid_half[...], merge[...]).astype(bf16)
    for s in range(2):
        near, far = masks(meta, seg, seg_col, seg_far, s)
        r = slice(s * 128, s * 128 + 128)
        for h in range(4):
            c = slice(h * 64, h * 64 + 64)
            v = slice(256 + h * 64, 256 + h * 64 + 64)
            q, k, k_far = query[r, c], kv[r, c], kv_far[r, c]
            probs, probs_far = head_probs(q, k, k_far, near, far)
            up = att_grad[r, c]
            delta = jnp.sum(up.astype(f32) * attended[r, c].astype(f32), axis=-1, keepdims=True)
            score = (probs * (dot_nt(up, kv[r, v]) - delta)).astype(bf16)
            score_far = (probs_far * (dot_nt(up, kv_far[r, v]) - delta)).astype(bf16)
            query_grad[r, c] = (dot(score, k) + dot(score_far, k_far)) * (HD**-0.5)
            kv_grad[r, c] = dot_tn(score, q)
            kv_grad[r, v] = dot_tn(probs.astype(bf16), up)
            kv_grad_far[r, c] = dot_tn(score_far, q).astype(bf16)
            kv_grad_far[r, v] = dot_tn(probs_far.astype(bf16), up).astype(bf16)


def project_back_kernel(
    meta, x, hidden, query_grad, kv_grad, kv_grad_in, attend, keep, give, proj, sums, part
):
    proj[:, :256] = query_grad[...].astype(bf16)
    proj[:, 256:] = (kv_grad[...] + kv_grad_in[...].astype(f32)).astype(bf16)
    part[...] = (
        dot_nt(proj[:, :256], attend[0])
        + dot_nt(proj[:, 256:512], attend[1])
        + dot_nt(proj[:, 512:], attend[2])
    )
    keep[...] = part[rows_of(meta, True), :]
    give[...] = part[rows_of(meta, False), :].astype(bf16)
    normed, _ = norm_stats(x[...])
    sums[...] = jnp.zeros_like(sums)
    sums[0:1, :] = jnp.sum(part[...] * normed, axis=0, keepdims=True)
    sums[1:2, :] = jnp.sum(part[...], axis=0, keepdims=True)


def attention_grads_kernel(meta, hidden, proj, resid_half, attended, sums, grads, *outs):
    for j in range(RING):
        at = columns(meta, j)
        lhs = hidden[:, at]
        pieces = [dot_tn(lhs, proj[:, t * 256 : t * 256 + 256]).astype(bf16) for t in range(3)]
        pieces.append(dot_tn(resid_half[:, at], attended[...]).astype(bf16))
        zero = jnp.zeros((1, 128), f32)
        tail = jnp.concatenate(
            [
                jnp.concatenate([sums[0:1, at], grads[0:1, at]], axis=1),
                jnp.concatenate([sums[1:2, at], grads[1:2, at]], axis=1),
                jnp.concatenate([grads[2:3, at], zero], axis=1),
                jnp.zeros((29, 256), f32),
            ],
            axis=0,
        )
        pieces.append(tail.astype(bf16))
        start = 0
        for value in pieces:
            span = slice(start, start + value.shape[0])
            start += value.shape[0]
            if j == 4:
                outs[4][span, :] = value[:, :128]
                outs[5][span, :] = value[:, 128:]
            else:
                out = outs[j] if j < 4 else outs[j + 1]
                out[span, :] = value


def block_out_kernel(meta, residual, s0, s1, s2, s3, out, part):
    out[...] = residual[...] + total_of(meta, (s0, s1, s2, s3), part)


def input_grad_kernel(meta, x, residual_grad, small, s0, s1, s2, s3, out, part):
    early_grad = total_of(meta, (s0, s1, s2, s3), part)
    normed, inverse = norm_stats(x[...])
    out[...] = residual_grad[...] + norm_backward(early_grad, normed, inverse, small[0:1, :])


def send_ahead(value):
    return lax.ppermute(value, AXES, AHEAD)


def send_behind(value):
    return lax.ppermute(value, AXES, BEHIND)


def gather_blocks(own, first, second):
    blocks = [own] + [None] * 8
    ahead, behind = own, own
    for step in range(1, 4):
        ahead, behind = send_ahead(ahead), send_behind(behind)
        blocks[9 - step], blocks[step] = ahead, behind
    blocks[4], blocks[5] = send_ahead(first(ahead)), send_behind(second(behind))
    return blocks


def sum_blocks(parts, join_first, join_second):
    ahead, behind = send_ahead(parts[4]), send_behind(parts[5])
    for step in range(3, 0, -1):
        up, down = parts[step].astype(f32), parts[9 - step].astype(f32)
        if step == 3:
            up, down = join_first(up, ahead.astype(f32)), join_second(down, behind.astype(f32))
        else:
            up, down = up + ahead.astype(f32), down + behind.astype(f32)
        ahead, behind = send_ahead(up.astype(bf16)), send_behind(down.astype(bf16))
    return parts[0].astype(f32) + (ahead.astype(f32) + behind.astype(f32))


def tp_exchange(keep, give):
    pair = (keep + lax.ppermute(give, "tp", NEAR).astype(f32)).astype(bf16)
    far = lax.ppermute(pair, "tp", FAR)
    return pair, far, lax.ppermute(pair, "tp", NEAR), lax.ppermute(far, "tp", NEAR)


def fast_shards(
    inputs, segment_ids, gains, shifts, attend_weight, merge_weight, expand_weight,
    expand_bias, reduce_weight, cotangent,
):
    shard, ctx = lax.axis_index("shard"), lax.axis_index("ctx")
    place = jnp.where(ctx == 0, shard, RING - 1 - shard)
    spots = lax.rem(place + jnp.arange(RING, dtype=jnp.int32), RING)
    owners = jnp.where(spots < 4, 2 * spots, 2 * (7 - spots) + 1)
    side = lax.rem(lax.axis_index("tp"), 2)
    meta = jnp.concatenate([owners, jnp.stack([side, ctx])]).astype(jnp.int32)

    x = inputs.reshape(256, 1024)
    cot = cotangent.reshape(256, 1024)
    small_part = jnp.zeros((32, 256), bf16)
    small_part = jnp.concatenate(
        [
            gains.reshape(1, 256),
            shifts.reshape(1, 256),
            jnp.pad(expand_bias, ((0, 0), (0, 128))),
            jnp.zeros((29, 256), bf16),
        ]
    )
    pack = jnp.concatenate(
        [jnp.swapaxes(attend_weight, 0, 1).reshape(384, 256), merge_weight, small_part]
    )
    seg_far = lax.ppermute(segment_ids, "ctx", [(0, 1)])
    seg_col = segment_ids.T
    blocks = gather_blocks(pack, lambda v: v[:, :128], lambda v: v[:, 128:])
    wide = jnp.concatenate([expand_weight, reduce_weight])
    wide, _ = lax.optimization_barrier((wide, blocks[START_AFTER]))
    wide_blocks = gather_blocks(wide, lambda v: v[:128], lambda v: v[128:])

    rows = (256, 1024)
    hidden_early, query, kv, attend, merge, small = call(
        qkv_kernel, "qkv",
        [shape(rows, bf16), shape((256, 256), bf16), shape((256, 512), bf16),
         shape((3, 1024, 256), bf16), shape((1024, 256), bf16), shape((8, 1024), f32)],
        [meta, x] + blocks, 400_000_000,
    )
    kv_far = lax.ppermute(kv, "ctx", [(0, 1)])
    half = (128, 1024)
    part = pltpu.VMEM(rows, f32)
    attended, keep, give = call(
        attention_kernel, "attention",
        [shape((256, 256), bf16), shape(half, f32), shape(half, bf16)],
        [meta, query, kv, kv_far, segment_ids, seg_col, seg_far, merge],
        300_000_000, [part], 800_000,
    )
    (residual, hidden_later, cot_half, act, pre_half, later_keep, later_give, red_keep,
     red_give, grads) = call(
        ffn_kernel, "ffn",
        [shape(rows, f32)] + [shape(rows, bf16)] * 4
        + [shape(half, f32), shape(half, bf16)] * 2 + [shape((8, 1024), f32)],
        [meta, x, cot, small, *tp_exchange(keep, give)] + wide_blocks,
        2_200_000_000,
        [pltpu.VMEM((1024, 1024), bf16), pltpu.VMEM((1024, 1024), bf16), part], 300_000,
    )
    later_sums = tp_exchange(later_keep, later_give)
    wide_shapes = [shape((256, 1024), bf16)] * 9
    wide_shapes[4] = wide_shapes[5] = shape((128, 1024), bf16)
    wide_parts = call(
        ffn_grads_kernel, "ffn_grads", wide_shapes,
        [meta, hidden_later, pre_half, cot_half, act], 1_100_000_000,
    )
    residual_grad, resid_half, query_grad, kv_grad, kv_grad_far = call(
        attention_back_kernel, "attention_back",
        [shape(rows, f32), shape(rows, bf16), shape((256, 256), f32), shape((256, 512), f32),
         shape((256, 512), bf16)],
        [meta, cot, residual, small, *later_sums, merge, query, kv, kv_far, attended,
         segment_ids, seg_col, seg_far],
        500_000_000, [part, pltpu.VMEM((256, 256), bf16)], 800_000,
    )
    kv_grad_in = lax.ppermute(kv_grad_far, "ctx", [(1, 0)])
    early_keep, early_give, proj, sums = call(
        project_back_kernel, "project_back",
        [shape(half, f32), shape(half, bf16), shape((256, 768), bf16), shape((8, 1024), f32)],
        [meta, x, hidden_early, query_grad, kv_grad, kv_grad_in, attend],
        400_000_000, [part],
    )
    early_sums = tp_exchange(early_keep, early_give)
    pack_shapes = [shape((544, 256), bf16)] * 9
    pack_shapes[4] = pack_shapes[5] = shape((544, 128), bf16)
    pack_parts = call(
        attention_grads_kernel, "attention_grads", pack_shapes,
        [meta, hidden_early, proj, resid_half, attended, sums, grads], 500_000_000,
    )
    wide_grad = sum_blocks(
        wide_parts,
        lambda v, a: jnp.concatenate([v[:128] + a, v[128:]]),
        lambda v, a: jnp.concatenate([v[:128], v[128:] + a]),
    )
    pack_grad = sum_blocks(
        pack_parts,
        lambda v, a: jnp.concatenate([v[:, :128] + a, v[:, 128:]], axis=1),
        lambda v, a: jnp.concatenate([v[:, :128], v[:, 128:] + a], axis=1),
    )
    (block_out,) = call(
        block_out_kernel, "block_out", [shape(rows, f32)],
        [meta, residual, *tp_exchange(red_keep, red_give)], 1_000_000, [part],
    )
    (input_grad,) = call(
        input_grad_kernel, "input_grad", [shape(rows, f32)],
        [meta, x, residual_grad, small, *early_sums], 5_000_000, [part],
    )
    tail = pack_grad[512:516]
    norms = tail[:2]
    norms = norms + lax.ppermute(norms, "tp", NEAR)
    norms = norms + lax.ppermute(norms, "tp", FAR)
    return (
        block_out.reshape(inputs.shape),
        input_grad.reshape(inputs.shape),
        norms[0].reshape(2, 128),
        norms[1].reshape(2, 128),
        jnp.swapaxes(pack_grad[:384].reshape(3, 128, 256), 0, 1),
        pack_grad[384:512],
        wide_grad[:128],
        tail[2:3, :128],
        wide_grad[128:],
    )


START_AFTER = 3


def fits(mesh_sizes, *args):
    shapes = tuple(a.shape for a in args)
    return mesh_sizes == (4, 2, 4) and shapes == (
        (2, 128, 1024), (2, 128), (2, 128), (2, 128), (128, 3, 256), (128, 256),
        (128, 1024), (1, 128), (128, 1024), (2, 128, 1024),
    )


def either(*args):
    sizes = tuple(lax.axis_size(name) for name in ("shard", "ctx", "tp"))
    return fast_shards(*args) if fits(sizes, *args) else shards(*args)


def solution(mesh):
    in_specs = (
        P("shard", "ctx", None),
        P("shard", "ctx"),
        P(None, ("shard", "ctx")),
        P(None, ("shard", "ctx")),
        P(("shard", "ctx"), None, "tp"),
        P(("shard", "ctx"), "tp"),
        P(("shard", "ctx"), "tp"),
        P("tp", ("shard", "ctx")),
        P(("shard", "ctx"), "tp"),
        P("shard", "ctx", None),
    )
    out_specs = (
        P("shard", "ctx", None),
        P("shard", "ctx", None),
        P(None, ("shard", "ctx")),
        P(None, ("shard", "ctx")),
        P(("shard", "ctx"), None, "tp"),
        P(("shard", "ctx"), "tp"),
        P(("shard", "ctx"), "tp"),
        P("tp", ("shard", "ctx")),
        P(("shard", "ctx"), "tp"),
    )
    return jax.shard_map(either, mesh=mesh, in_specs=in_specs, out_specs=out_specs, check_vma=False)
```

```python
import jax
import jax.numpy as jnp
from jax import lax
from jax.experimental import pallas as pl
from jax.experimental.pallas import tpu as pltpu
from jax.sharding import PartitionSpec as P

HD = 64


epsilon = 1e-05
masked_score = -1e30
gelu_scale = 0.7978845608028654
gelu_cubic = 0.044715


def norm_forward(values, gain, shift):
    average = jnp.mean(values, axis=-1, keepdims=True)
    centered = values - average
    variance = jnp.mean(centered * centered, axis=-1, keepdims=True)
    inverse = lax.rsqrt(variance + epsilon)
    normed = centered * inverse
    return (normed, inverse, normed * gain.astype(jnp.float32) + shift.astype(jnp.float32))


def norm_backward(upstream, normed, inverse, gain):
    scaled = upstream * gain.astype(jnp.float32)
    first_mean = jnp.mean(scaled, axis=-1, keepdims=True)
    second_mean = jnp.mean(scaled * normed, axis=-1, keepdims=True)
    return inverse * (scaled - first_mean - normed * second_mean)


def gelu_pair(pre_act):
    inner_arg = gelu_scale * (pre_act + gelu_cubic * pre_act * pre_act * pre_act)
    tangent = jnp.tanh(inner_arg)
    gelu_value = 0.5 * pre_act * (1.0 + tangent)
    gelu_slope = 0.5 * (1.0 + tangent) + 0.5 * pre_act * (1.0 - tangent * tangent) * gelu_scale * (
        1.0 + 3.0 * gelu_cubic * pre_act * pre_act
    )
    return (gelu_value, gelu_slope)


def shards(
    inputs,
    segment_ids,
    gains,
    shifts,
    attend_weight,
    merge_weight,
    expand_weight,
    expand_bias,
    reduce_weight,
    cotangent,
):
    seq_count, group_len, model_width = inputs.shape
    row_count = seq_count * group_len
    full_len = group_len * lax.axis_size("ctx")
    head_scale = HD ** (-0.5)
    gathered = (
        lax.all_gather(attend_weight, ("shard", "ctx"), axis=0, tiled=True),
        lax.all_gather(merge_weight, ("shard", "ctx"), axis=0, tiled=True),
        lax.all_gather(expand_weight, ("shard", "ctx"), axis=0, tiled=True),
        lax.all_gather(reduce_weight, ("shard", "ctx"), axis=0, tiled=True),
        lax.all_gather(expand_bias, ("shard", "ctx"), axis=1, tiled=True),
        lax.all_gather(gains, ("shard", "ctx"), axis=1, tiled=True),
        lax.all_gather(shifts, ("shard", "ctx"), axis=1, tiled=True),
    )
    attend_full, merge_full, expand_full, reduce_full, bias_full, gains_full, shifts_full = gathered
    local_cols = attend_full.shape[2]
    head_local = local_cols // HD
    flat_in = inputs.reshape(row_count, model_width)
    normed_early, inverse_early, affine_early = norm_forward(flat_in, gains_full[0], shifts_full[0])
    hidden_early = affine_early.astype(jnp.bfloat16)
    projected = jnp.einsum(
        "rd,dtc->rtc", hidden_early, attend_full, preferred_element_type=jnp.float32
    )
    query_heads = (
        (projected[:, 0] * head_scale)
        .astype(jnp.bfloat16)
        .reshape(seq_count, group_len, head_local, HD)
    )
    key_rows = projected[:, 1].astype(jnp.bfloat16).reshape(seq_count, group_len, local_cols)
    value_rows = projected[:, 2].astype(jnp.bfloat16).reshape(seq_count, group_len, local_cols)
    all_keys, all_values, all_segments = (
        lax.all_gather(key_rows, "ctx", axis=1, tiled=True),
        lax.all_gather(value_rows, "ctx", axis=1, tiled=True),
        lax.all_gather(segment_ids, "ctx", axis=1, tiled=True),
    )
    key_heads = all_keys.reshape(seq_count, full_len, head_local, HD)
    value_heads = all_values.reshape(seq_count, full_len, head_local, HD)
    query_pos = lax.axis_index("ctx") * group_len + jnp.arange(group_len, dtype=jnp.int32)
    key_pos = jnp.arange(full_len, dtype=jnp.int32)
    allowed = (segment_ids[:, :, None] == all_segments[:, None, :]) & (
        key_pos[None, None, :] <= query_pos[None, :, None]
    )
    allowed = allowed[:, None]

    def score_block():
        raw_scores = jnp.einsum(
            "sqhd,skhd->shqk", query_heads, key_heads, preferred_element_type=jnp.float32
        )
        return jnp.where(allowed, raw_scores, masked_score)

    scores = score_block()
    row_top = jnp.max(scores, axis=-1, keepdims=True)
    log_total = row_top + jnp.log(jnp.sum(jnp.exp(scores - row_top), axis=-1, keepdims=True))
    attn_probs = jnp.exp(scores - log_total)
    probs_half = attn_probs.astype(jnp.bfloat16)
    attended_heads = jnp.einsum(
        "shqk,skhd->sqhd", probs_half, value_heads, preferred_element_type=jnp.float32
    ).astype(jnp.bfloat16)
    attended = attended_heads.reshape(row_count, local_cols)
    merge_part = jnp.einsum("rc,oc->ro", attended, merge_full, preferred_element_type=jnp.float32)
    residual = flat_in + lax.psum(merge_part, "tp")
    normed_later, inverse_later, affine_later = norm_forward(
        residual, gains_full[1], shifts_full[1]
    )
    hidden_later = affine_later.astype(jnp.bfloat16)
    pre_act = jnp.dot(
        hidden_later, expand_full, preferred_element_type=jnp.float32
    ) + bias_full.astype(jnp.float32)
    gelu_value, gelu_slope = gelu_pair(pre_act)
    activated = gelu_value.astype(jnp.bfloat16)
    reduce_part = jnp.einsum(
        "rf,of->ro", activated, reduce_full, preferred_element_type=jnp.float32
    )
    block_out = residual + lax.psum(reduce_part.astype(jnp.bfloat16), "tp").astype(jnp.float32)
    back_set = (
        lax.all_gather(attend_weight, ("shard", "ctx"), axis=0, tiled=True),
        lax.all_gather(merge_weight, ("shard", "ctx"), axis=0, tiled=True),
        lax.all_gather(expand_weight, ("shard", "ctx"), axis=0, tiled=True),
        lax.all_gather(reduce_weight, ("shard", "ctx"), axis=0, tiled=True),
        lax.all_gather(gains, ("shard", "ctx"), axis=1, tiled=True),
    )
    attend_back, merge_back, expand_back, reduce_back, gains_back = back_set
    output_grad = cotangent.reshape(row_count, model_width)
    cot_half = output_grad.astype(jnp.bfloat16)
    reduce_grad = jnp.einsum("ro,rf->of", cot_half, activated, preferred_element_type=jnp.float32)
    pre_grad = jnp.dot(cot_half, reduce_back, preferred_element_type=jnp.float32) * gelu_slope
    pre_half = pre_grad.astype(jnp.bfloat16)
    bias_grad = jnp.sum(pre_grad, axis=0, keepdims=True)
    expand_grad = jnp.einsum(
        "rd,rf->df", hidden_later, pre_half, preferred_element_type=jnp.float32
    )
    later_part = jnp.einsum("rf,df->rd", pre_half, expand_back, preferred_element_type=jnp.float32)
    later_grad = lax.psum(later_part, "tp")
    residual_grad = output_grad + norm_backward(
        later_grad, normed_later, inverse_later, gains_back[1]
    )
    resid_half = residual_grad.astype(jnp.bfloat16)
    merge_grad = jnp.einsum("ro,rc->oc", resid_half, attended, preferred_element_type=jnp.float32)
    attended_grad = jnp.dot(resid_half, merge_back, preferred_element_type=jnp.float32).astype(
        jnp.bfloat16
    )
    grad_heads = attended_grad.reshape(seq_count, group_len, head_local, HD)
    scores_again = score_block()
    probs_again = jnp.exp(scores_again - log_total)
    probs_again_half = probs_again.astype(jnp.bfloat16)
    row_delta = jnp.einsum(
        "sqhd,sqhd->shq", grad_heads, attended_heads, preferred_element_type=jnp.float32
    )
    prob_grad = jnp.einsum(
        "sqhd,skhd->shqk", grad_heads, value_heads, preferred_element_type=jnp.float32
    )
    score_grad = probs_again * (prob_grad - row_delta[..., None])
    score_half = score_grad.astype(jnp.bfloat16)
    query_grad = (
        jnp.einsum("shqk,skhd->sqhd", score_half, key_heads, preferred_element_type=jnp.float32)
        * head_scale
    )
    keys_part = jnp.einsum(
        "shqk,sqhd->skhd", score_half, query_heads, preferred_element_type=jnp.float32
    ).reshape(seq_count, full_len, local_cols)
    values_part = jnp.einsum(
        "shqk,sqhd->skhd", probs_again_half, grad_heads, preferred_element_type=jnp.float32
    ).reshape(seq_count, full_len, local_cols)
    keys_grad, values_grad = (
        lax.psum_scatter(keys_part, "ctx", scatter_dimension=1, tiled=True),
        lax.psum_scatter(values_part, "ctx", scatter_dimension=1, tiled=True),
    )
    proj_grad = jnp.stack(
        [
            query_grad.reshape(row_count, local_cols),
            keys_grad.reshape(row_count, local_cols),
            values_grad.reshape(row_count, local_cols),
        ],
        axis=1,
    ).astype(jnp.bfloat16)
    attend_grad = jnp.einsum(
        "rd,rtc->dtc", hidden_early, proj_grad, preferred_element_type=jnp.float32
    )
    early_part = jnp.einsum(
        "rtc,dtc->rd", proj_grad, attend_back, preferred_element_type=jnp.float32
    )
    early_grad = lax.psum(early_part, "tp")
    input_grad = residual_grad + norm_backward(
        early_grad, normed_early, inverse_early, gains_back[0]
    )
    gains_grad = jnp.stack(
        [jnp.sum(early_grad * normed_early, axis=0), jnp.sum(later_grad * normed_later, axis=0)]
    )
    shifts_grad = jnp.stack([jnp.sum(early_grad, axis=0), jnp.sum(later_grad, axis=0)])
    shares = (
        lax.psum_scatter(attend_grad, ("shard", "ctx"), scatter_dimension=0, tiled=True),
        lax.psum_scatter(merge_grad, ("shard", "ctx"), scatter_dimension=0, tiled=True),
        lax.psum_scatter(expand_grad, ("shard", "ctx"), scatter_dimension=0, tiled=True),
        lax.psum_scatter(reduce_grad, ("shard", "ctx"), scatter_dimension=0, tiled=True),
        lax.psum_scatter(bias_grad, ("shard", "ctx"), scatter_dimension=1, tiled=True),
        lax.psum_scatter(gains_grad, ("shard", "ctx"), scatter_dimension=1, tiled=True),
        lax.psum_scatter(shifts_grad, ("shard", "ctx"), scatter_dimension=1, tiled=True),
    )
    return (
        block_out.reshape(inputs.shape),
        input_grad.reshape(inputs.shape),
        shares[5],
        shares[6],
        shares[0],
        shares[1],
        shares[2],
        shares[4],
        shares[3],
    )


VMEM = pl.BlockSpec(memory_space=pltpu.VMEM)
SMEM = pl.BlockSpec(memory_space=pltpu.SMEM)
f32 = jnp.float32
bf16 = jnp.bfloat16
RING = 8
NEAR = [(0, 1), (1, 0), (2, 3), (3, 2)]
FAR = [(0, 2), (2, 0), (1, 3), (3, 1)]
AXES = ("shard", "ctx")
IDS = [2 * p if p < 4 else 2 * (7 - p) + 1 for p in range(RING)]
AHEAD = [(IDS[p], IDS[(p + 1) % RING]) for p in range(RING)]
BEHIND = [(IDS[p], IDS[(p - 1) % RING]) for p in range(RING)]


def shape(dims, dtype):
    return jax.ShapeDtypeStruct(dims, dtype)


def call(kernel, name, outs, args, flops, scratch=(), transcendentals=0):
    nbytes = sum(a.size * a.dtype.itemsize for a in list(args) + list(outs))
    return pl.pallas_call(
        kernel,
        name=name,
        out_shape=tuple(outs),
        in_specs=[SMEM] + [VMEM] * (len(args) - 1),
        out_specs=tuple(VMEM for _ in outs),
        scratch_shapes=list(scratch),
        cost_estimate=pl.CostEstimate(
            flops=flops, bytes_accessed=nbytes, transcendentals=transcendentals
        ),
    )(*args)


def columns(meta, offset):
    return pl.ds(pl.multiple_of(meta[offset] * 128, 128), 128)


def rows_of(meta, mine):
    side = meta[8] if mine else 1 - meta[8]
    return pl.ds(pl.multiple_of(side * 128, 128), 128)


def dot(a, b):
    return jnp.dot(a, b, preferred_element_type=f32)


def dot_nt(a, b):
    return lax.dot_general(a, b, (((1,), (1,)), ((), ())), preferred_element_type=f32)


def dot_tn(a, b):
    return lax.dot_general(a, b, (((0,), (0,)), ((), ())), preferred_element_type=f32)


def norm_stats(values):
    average = jnp.mean(values, axis=-1, keepdims=True)
    centered = values - average
    variance = jnp.mean(centered * centered, axis=-1, keepdims=True)
    inverse = lax.rsqrt(variance + epsilon)
    return centered * inverse, inverse


def pack_kernel(meta, attend, merge, gains, shifts, bias, seg, out):
    for t in range(3):
        out[t * 128 : t * 128 + 128, :] = attend[t]
    out[384:512, :] = merge[...]
    zero = jnp.zeros((1, 128), f32)
    low, high, ids = gains[...].astype(f32), shifts[...].astype(f32), seg[...].astype(f32)
    tail = [
        jnp.concatenate([low[0:1], low[1:2]], axis=1),
        jnp.concatenate([high[0:1], high[1:2]], axis=1),
        jnp.concatenate([bias[...].astype(f32), zero], axis=1),
        jnp.concatenate([ids[0:1], ids[1:2]], axis=1),
        jnp.zeros((12, 256), f32),
    ]
    out[512:528, :] = jnp.concatenate(tail, axis=0).astype(bf16)


def norm_half_kernel(meta, x, out):
    normed, _ = norm_stats(x[rows_of(meta, True), :])
    out[...] = normed.astype(bf16)


def qkv_kernel(meta, x, far_a, far_b, *refs):
    blocks = refs[:9]
    (hidden, hidden_far, query, key_value, key_value_far, attend, merge, small, seg_far,
     seg_all) = refs[9:]

    def piece(offset, start, size):
        if offset < 4:
            return blocks[offset][start : start + size, :]
        if offset == 4:
            return jnp.concatenate(
                [blocks[4][start : start + size, :], blocks[5][start : start + size, :]], axis=1
            )
        return blocks[offset + 1][start : start + size, :]

    small[...] = jnp.zeros_like(small)
    for j in range(RING):
        at = columns(meta, j)
        for t in range(3):
            attend[t, at, :] = piece(j, t * 128, 128)
        merge[at, :] = piece(j, 384, 128)
        tail = piece(j, 512, 16).astype(f32)
        small[0:1, at] = tail[0:1, :128]
        small[1:2, at] = tail[0:1, 128:]
        small[2:3, at] = tail[1:2, :128]
        small[3:4, at] = tail[1:2, 128:]
        small[4:5, at] = tail[2:3, :128]
        seg_all[pl.ds(meta[j], 1), :] = tail[3:4, :]
    ids = seg_all[pl.ds(2 * meta[10], 1), :]
    seg_far[0:1, :] = ids[:, :128].astype(jnp.int32)
    seg_far[1:2, :] = ids[:, 128:].astype(jnp.int32)
    gain, shift = small[0:1, :], small[2:3, :]
    normed, _ = norm_stats(x[...])
    hidden[...] = (normed * gain + shift).astype(bf16)
    hidden_far[rows_of(meta, True), :] = (far_a[...].astype(f32) * gain + shift).astype(bf16)
    hidden_far[rows_of(meta, False), :] = (far_b[...].astype(f32) * gain + shift).astype(bf16)
    both, other = hidden[...], hidden_far[...]
    key_value[:, :256] = dot(both, attend[1]).astype(bf16)
    key_value[:, 256:] = dot(both, attend[2]).astype(bf16)
    key_value_far[:, :256] = dot(other, attend[1]).astype(bf16)
    key_value_far[:, 256:] = dot(other, attend[2]).astype(bf16)
    query[...] = (dot(both, attend[0]) * (HD**-0.5)).astype(bf16)


def masks(meta, seg, seg_col, seg_far, s):
    col = seg_col[:, s : s + 1]
    near = col == seg[s : s + 1, :]
    i = lax.broadcasted_iota(jnp.int32, (128, 128), 0)
    j = lax.broadcasted_iota(jnp.int32, (128, 128), 1)
    far = (col == seg_far[s : s + 1, :]) & (meta[9] == 1)
    return near & (j <= i), far


def head_probs(query, key, key_far, near, far):
    score = jnp.where(near, dot_nt(query, key), masked_score)
    score_far = jnp.where(far, dot_nt(query, key_far), masked_score)
    top = jnp.maximum(
        jnp.max(score, axis=-1, keepdims=True), jnp.max(score_far, axis=-1, keepdims=True)
    )
    total = jnp.sum(jnp.exp(score - top), axis=-1, keepdims=True) + jnp.sum(
        jnp.exp(score_far - top), axis=-1, keepdims=True
    )
    log_total = top + jnp.log(total)
    return jnp.exp(score - log_total), jnp.exp(score_far - log_total)


def attention_kernel(
    meta, query, kv, kv_far, seg, seg_col, seg_far, merge, attended, keep, give, part
):
    for s in range(2):
        near, far = masks(meta, seg, seg_col, seg_far, s)
        r = slice(s * 128, s * 128 + 128)
        for h in range(4):
            c = slice(h * 64, h * 64 + 64)
            v = slice(256 + h * 64, 256 + h * 64 + 64)
            probs, probs_far = head_probs(query[r, c], kv[r, c], kv_far[r, c], near, far)
            out = dot(probs.astype(bf16), kv[r, v]) + dot(probs_far.astype(bf16), kv_far[r, v])
            attended[r, c] = out.astype(bf16)
    part[...] = dot_nt(attended[...], merge[...])
    keep[...] = part[rows_of(meta, True), :]
    give[...] = part[rows_of(meta, False), :].astype(bf16)


def total_of(meta, sums, full):
    pair, far, pair_other, far_other = sums
    full[rows_of(meta, True), :] = pair[...].astype(f32) + far[...].astype(f32)
    full[rows_of(meta, False), :] = pair_other[...].astype(f32) + far_other[...].astype(f32)
    return full[...]


def assemble(meta, blocks, full):
    for j in range(RING):
        at = columns(meta, j)
        if j == 4:
            start = pl.multiple_of(meta[4] * 128, 128)
            full[pl.ds(start, 64), :] = blocks[4][...]
            full[pl.ds(pl.multiple_of(start + 64, 64), 64), :] = blocks[5][...]
        else:
            full[at, :] = (blocks[j] if j < 4 else blocks[j + 1])[...]


def store_parts(meta, left, right, outs):
    for j in range(RING):
        value = dot_tn(left[:, columns(meta, j)], right[...]).astype(bf16)
        if j == 4:
            outs[4][...] = value[:64]
            outs[5][...] = value[64:]
        else:
            (outs[j] if j < 4 else outs[j + 1])[...] = value


def ffn_first_kernel(meta, x, cot, small, s0, s1, s2, s3, *refs):
    blocks = refs[:9]
    residual, hidden, cot_half, act, slope, expand = refs[9:15]
    outs, part = refs[15:24], refs[24]
    assemble(meta, blocks, expand)
    residual[...] = x[...] + total_of(meta, (s0, s1, s2, s3), part)
    normed, _ = norm_stats(residual[...])
    hidden[...] = (normed * small[1:2, :] + small[3:4, :]).astype(bf16)
    cot_half[...] = cot[...].astype(bf16)

    def units(i, carry):
        at = pl.ds(pl.multiple_of(i * 256, 256), 256)
        pre_act = dot(hidden[...], expand[:, at]) + small[4:5, at]
        value, gradient = gelu_pair(pre_act)
        act[:, at] = value.astype(bf16)
        slope[:, at] = gradient
        return carry

    lax.fori_loop(0, 4, units, 0)
    store_parts(meta, cot_half, act, outs)


def ffn_second_kernel(meta, residual, cot_half, act, slope, expand, *refs):
    blocks = refs[:9]
    pre_half, later_keep, later_give, red_keep, red_give, grads, reduce, part = refs[9:]
    assemble(meta, blocks, reduce)
    grads[...] = jnp.zeros_like(grads)

    def units(i, carry):
        at = pl.ds(pl.multiple_of(i * 256, 256), 256)
        pre_grad = dot(cot_half[...], reduce[:, at]) * slope[:, at]
        pre_half[:, at] = pre_grad.astype(bf16)
        grads[2:3, at] = jnp.sum(pre_grad, axis=0, keepdims=True)
        return carry

    lax.fori_loop(0, 4, units, 0)

    def later(i, carry):
        at = pl.ds(pl.multiple_of(i * 256, 256), 256)
        part[:, at] = dot_nt(pre_half[...], expand[at, :])
        return carry

    lax.fori_loop(0, 4, later, 0)
    later_keep[...] = part[rows_of(meta, True), :]
    later_give[...] = part[rows_of(meta, False), :].astype(bf16)
    normed, _ = norm_stats(residual[...])
    grads[0:1, :] = jnp.sum(part[...] * normed, axis=0, keepdims=True)
    grads[1:2, :] = jnp.sum(part[...], axis=0, keepdims=True)

    def reduced(i, carry):
        at = pl.ds(pl.multiple_of(i * 256, 256), 256)
        part[:, at] = dot_nt(act[...], reduce[at, :])
        return carry

    lax.fori_loop(0, 4, reduced, 0)
    red_keep[...] = part[rows_of(meta, True), :]
    red_give[...] = part[rows_of(meta, False), :].astype(bf16)


def expand_grads_kernel(meta, hidden, pre_half, *outs):
    store_parts(meta, hidden, pre_half, outs)


def attention_back_kernel(
    meta, cot, residual, small, s0, s1, s2, s3, merge, query, kv, kv_far, attended,
    seg, seg_col, seg_far, residual_grad, resid_half, query_grad, kv_grad, kv_grad_far,
    part, att_grad
):
    later_grad = total_of(meta, (s0, s1, s2, s3), part)
    normed, inverse = norm_stats(residual[...])
    residual_grad[...] = cot[...] + norm_backward(later_grad, normed, inverse, small[1:2, :])
    resid_half[...] = residual_grad[...].astype(bf16)
    att_grad[...] = dot(resid_half[...], merge[...]).astype(bf16)
    for s in range(2):
        near, far = masks(meta, seg, seg_col, seg_far, s)
        r = slice(s * 128, s * 128 + 128)
        for h in range(4):
            c = slice(h * 64, h * 64 + 64)
            v = slice(256 + h * 64, 256 + h * 64 + 64)
            q, k, k_far = query[r, c], kv[r, c], kv_far[r, c]
            probs, probs_far = head_probs(q, k, k_far, near, far)
            up = att_grad[r, c]
            delta = jnp.sum(up.astype(f32) * attended[r, c].astype(f32), axis=-1, keepdims=True)
            score = (probs * (dot_nt(up, kv[r, v]) - delta)).astype(bf16)
            score_far = (probs_far * (dot_nt(up, kv_far[r, v]) - delta)).astype(bf16)
            query_grad[r, c] = (dot(score, k) + dot(score_far, k_far)) * (HD**-0.5)
            kv_grad[r, c] = dot_tn(score, q)
            kv_grad[r, v] = dot_tn(probs.astype(bf16), up)
            kv_grad_far[r, c] = dot_tn(score_far, q).astype(bf16)
            kv_grad_far[r, v] = dot_tn(probs_far.astype(bf16), up).astype(bf16)


def attention_grads_kernel(
    meta, x, far_a, far_b, hidden, hidden_far, query_grad, kv_grad, kv_grad_far, resid_half,
    attended, attend, grads, early, *refs
):
    outs, proj, sums, part = refs[:9], refs[9], refs[10], refs[11]
    proj[:, :256] = query_grad[...].astype(bf16)
    proj[:, 256:] = kv_grad[...].astype(bf16)
    early[...] = (
        dot_nt(proj[:, :256], attend[0])
        + dot_nt(proj[:, 256:512], attend[1])
        + dot_nt(proj[:, 512:], attend[2])
    )
    part[...] = dot_nt(kv_grad_far[:, :256], attend[1]) + dot_nt(kv_grad_far[:, 256:], attend[2])
    normed, _ = norm_stats(x[...])
    mine, other = part[rows_of(meta, True), :], part[rows_of(meta, False), :]
    sums[0:1, :] = (
        jnp.sum(early[...] * normed, axis=0, keepdims=True)
        + jnp.sum(mine * far_a[...].astype(f32), axis=0, keepdims=True)
        + jnp.sum(other * far_b[...].astype(f32), axis=0, keepdims=True)
    )
    sums[1:2, :] = jnp.sum(early[...] + part[...], axis=0, keepdims=True)
    for j in range(RING):
        at = columns(meta, j)
        lhs, lhs_far = hidden[:, at], hidden_far[:, at]
        pieces = [dot_tn(lhs, proj[:, :256]).astype(bf16)]
        for t in (1, 2):
            c, c_far = slice(t * 256, t * 256 + 256), slice(t * 256 - 256, t * 256)
            pieces.append((dot_tn(lhs, proj[:, c]) + dot_tn(lhs_far, kv_grad_far[:, c_far])).astype(bf16))
        pieces.append(dot_tn(resid_half[:, at], attended[...]).astype(bf16))
        zero = jnp.zeros((1, 128), f32)
        tail = jnp.concatenate(
            [
                jnp.concatenate([sums[0:1, at], grads[0:1, at]], axis=1),
                jnp.concatenate([sums[1:2, at], grads[1:2, at]], axis=1),
                jnp.concatenate([grads[2:3, at], zero], axis=1),
                jnp.zeros((13, 256), f32),
            ],
            axis=0,
        )
        pieces.append(tail.astype(bf16))
        start = 0
        for value in pieces:
            span = slice(start, start + value.shape[0])
            start += value.shape[0]
            if j == 4:
                outs[4][span, :] = value[:, :128]
                outs[5][span, :] = value[:, 128:]
            else:
                out = outs[j] if j < 4 else outs[j + 1]
                out[span, :] = value


def project_back_kernel(meta, early, kv_grad_in, attend, keep, give, part):
    part[...] = (
        early[...]
        + dot_nt(kv_grad_in[:, :256], attend[1])
        + dot_nt(kv_grad_in[:, 256:], attend[2])
    )
    keep[...] = part[rows_of(meta, True), :]
    give[...] = part[rows_of(meta, False), :].astype(bf16)


def first_rows_kernel(meta, up, down, ahead, behind, up_out, down_out):
    up_out[:64, :] = (up[:64, :].astype(f32) + ahead[...].astype(f32)).astype(bf16)
    up_out[64:, :] = up[64:, :]
    down_out[:64, :] = down[:64, :]
    down_out[64:, :] = (down[64:, :].astype(f32) + behind[...].astype(f32)).astype(bf16)


def first_columns_kernel(meta, up, down, ahead, behind, up_out, down_out):
    up_out[:, :128] = (up[:, :128].astype(f32) + ahead[...].astype(f32)).astype(bf16)
    up_out[:, 128:] = up[:, 128:]
    down_out[:, :128] = down[:, :128]
    down_out[:, 128:] = (down[:, 128:].astype(f32) + behind[...].astype(f32)).astype(bf16)


def step_kernel(meta, up, down, ahead, behind, up_out, down_out):
    up_out[...] = (up[...].astype(f32) + ahead[...].astype(f32)).astype(bf16)
    down_out[...] = (down[...].astype(f32) + behind[...].astype(f32)).astype(bf16)


def last_kernel(meta, own, ahead, behind, out):
    out[...] = own[...].astype(f32) + (ahead[...].astype(f32) + behind[...].astype(f32))


def last_pack_kernel(meta, own, ahead, behind, attend, merge, tail):
    def total(start, size):
        r = slice(start, start + size)
        return own[r, :].astype(f32) + (ahead[r, :].astype(f32) + behind[r, :].astype(f32))

    for t in range(3):
        attend[t] = total(t * 128, 128)
    merge[...] = total(384, 128)
    tail[...] = total(512, 16)


def block_out_kernel(meta, residual, s0, s1, s2, s3, out, part):
    out[...] = residual[...] + total_of(meta, (s0, s1, s2, s3), part)


def input_grad_kernel(meta, x, residual_grad, small, s0, s1, s2, s3, out, part):
    early_grad = total_of(meta, (s0, s1, s2, s3), part)
    normed, inverse = norm_stats(x[...])
    out[...] = residual_grad[...] + norm_backward(early_grad, normed, inverse, small[0:1, :])


def send_ahead(value):
    return lax.ppermute(value, AXES, AHEAD)


def send_behind(value):
    return lax.ppermute(value, AXES, BEHIND)


def gather_blocks(own, first, second):
    blocks = [own] + [None] * 8
    ahead, behind = own, own
    for step in range(1, 4):
        ahead, behind = send_ahead(ahead), send_behind(behind)
        blocks[9 - step], blocks[step] = ahead, behind
    blocks[4], blocks[5] = send_ahead(first(ahead)), send_behind(second(behind))
    return blocks


def sum_blocks(meta, parts, name, first, last, last_shapes):
    ahead, behind = send_ahead(parts[4]), send_behind(parts[5])
    for step in range(3, 0, -1):
        up, down = call(
            first if step == 3 else step_kernel, f"{name}_{step}", [shape(parts[1].shape, bf16)] * 2,
            [meta, parts[step], parts[9 - step], ahead, behind], 1_000_000,
        )
        ahead, behind = send_ahead(up), send_behind(down)
    return call(last, f"{name}_last", last_shapes, [meta, parts[0], ahead, behind], 1_000_000)


def tp_exchange(keep, give):
    pair = (keep + lax.ppermute(give, "tp", NEAR).astype(f32)).astype(bf16)
    far = lax.ppermute(pair, "tp", FAR)
    return pair, far, lax.ppermute(pair, "tp", NEAR), lax.ppermute(far, "tp", NEAR)


def fast_shards(
    inputs, segment_ids, gains, shifts, attend_weight, merge_weight, expand_weight,
    expand_bias, reduce_weight, cotangent,
):
    shard, ctx = lax.axis_index("shard"), lax.axis_index("ctx")
    place = jnp.where(ctx == 0, shard, RING - 1 - shard)
    spots = lax.rem(place + jnp.arange(RING, dtype=jnp.int32), RING)
    owners = jnp.where(spots < 4, 2 * spots, 2 * (7 - spots) + 1)
    side = lax.rem(lax.axis_index("tp"), 2)
    meta = jnp.concatenate([owners, jnp.stack([side, ctx, shard])]).astype(jnp.int32)

    x = inputs.reshape(256, 1024)
    cot = cotangent.reshape(256, 1024)
    rows, half, square = (256, 1024), (128, 1024), (256, 256)
    part = pltpu.VMEM(rows, f32)
    (pack,) = call(
        pack_kernel, "pack", [shape((528, 256), bf16)],
        [meta, jnp.swapaxes(attend_weight, 0, 1), merge_weight, gains, shifts, expand_bias,
         segment_ids], 1_000_000,
    )
    blocks = gather_blocks(pack, lambda v: v[:, :128], lambda v: v[:, 128:])
    (normed_half,) = call(norm_half_kernel, "norm_half", [shape(half, bf16)], [meta, x], 1_000_000)
    far_a = lax.ppermute(normed_half, "ctx", [(0, 1)])
    far_b = lax.ppermute(far_a, "tp", NEAR)
    seg_col = segment_ids.T
    expand_weight, _ = lax.optimization_barrier((expand_weight, blocks[EXPAND_AFTER]))
    expand_blocks = gather_blocks(expand_weight, lambda v: v[:64], lambda v: v[64:])
    reduce_weight, _ = lax.optimization_barrier((reduce_weight, expand_blocks[REDUCE_AFTER]))
    reduce_blocks = gather_blocks(reduce_weight, lambda v: v[:64], lambda v: v[64:])

    hidden_early, hidden_far, query, kv, kv_far, attend, merge, small, seg_far = call(
        qkv_kernel, "qkv",
        [shape(rows, bf16), shape(rows, bf16), shape(square, bf16), shape((256, 512), bf16),
         shape((256, 512), bf16), shape((3, 1024, 256), bf16), shape((1024, 256), bf16),
         shape((8, 1024), f32), shape((2, 128), jnp.int32)],
        [meta, x, far_a, far_b] + blocks, 700_000_000, [pltpu.VMEM((8, 256), f32)],
    )
    attended, keep, give = call(
        attention_kernel, "attention",
        [shape(square, bf16), shape(half, f32), shape(half, bf16)],
        [meta, query, kv, kv_far, segment_ids, seg_col, seg_far, merge],
        300_000_000, [part], 800_000,
    )
    part_shapes = [shape(half, bf16)] * 9
    part_shapes[4] = part_shapes[5] = shape((64, 1024), bf16)
    residual, hidden_later, cot_half, act, slope, expand, *reduce_parts = call(
        ffn_first_kernel, "ffn_first",
        [shape(rows, f32)] + [shape(rows, bf16)] * 3 + [shape(rows, f32)]
        + [shape((1024, 1024), bf16)] + part_shapes,
        [meta, x, cot, small, *tp_exchange(keep, give)] + expand_blocks,
        1_100_000_000, [part], 300_000,
    )
    pre_half, later_keep, later_give, red_keep, red_give, grads = call(
        ffn_second_kernel, "ffn_second",
        [shape(rows, bf16)] + [shape(half, f32), shape(half, bf16)] * 2 + [shape((8, 1024), f32)],
        [meta, residual, cot_half, act, slope, expand] + reduce_blocks,
        1_600_000_000, [pltpu.VMEM((1024, 1024), bf16), part],
    )
    (reduce_grad,) = sum_blocks(
        meta, reduce_parts, "reduce_sum", first_rows_kernel, last_kernel, [shape(half, f32)]
    )
    later_sums = tp_exchange(later_keep, later_give)
    expand_parts = call(
        expand_grads_kernel, "expand_grads", part_shapes,
        [meta, hidden_later, pre_half], 550_000_000,
    )
    (expand_grad,) = sum_blocks(
        meta, expand_parts, "expand_sum", first_rows_kernel, last_kernel, [shape(half, f32)]
    )
    residual_grad, resid_half, query_grad, kv_grad, kv_grad_far = call(
        attention_back_kernel, "attention_back",
        [shape(rows, f32), shape(rows, bf16), shape(square, f32), shape((256, 512), f32),
         shape((256, 512), bf16)],
        [meta, cot, residual, small, *later_sums, merge, query, kv, kv_far, attended,
         segment_ids, seg_col, seg_far],
        500_000_000, [part, pltpu.VMEM(square, bf16)], 800_000,
    )
    kv_grad_in = lax.ppermute(kv_grad_far, "ctx", [(1, 0)])
    pack_shapes = [shape((528, 256), bf16)] * 9
    pack_shapes[4] = pack_shapes[5] = shape((528, 128), bf16)
    early, *pack_parts = call(
        attention_grads_kernel, "attention_grads", [shape(rows, f32)] + pack_shapes,
        [meta, x, far_a, far_b, hidden_early, hidden_far, query_grad, kv_grad, kv_grad_far,
         resid_half, attended, attend, grads], 1_100_000_000,
        [pltpu.VMEM((256, 768), bf16), pltpu.VMEM((8, 1024), f32), part],
    )
    attend_grad, merge_grad, tail = sum_blocks(
        meta, pack_parts, "pack_sum", first_columns_kernel, last_pack_kernel,
        [shape((3, 128, 256), f32), shape((128, 256), f32), shape((16, 256), f32)],
    )
    early_keep, early_give = call(
        project_back_kernel, "project_back", [shape(half, f32), shape(half, bf16)],
        [meta, early, kv_grad_in, attend], 300_000_000, [part],
    )
    early_sums = tp_exchange(early_keep, early_give)
    red_keep, red_give, _ = lax.optimization_barrier((red_keep, red_give, query_grad))
    (block_out,) = call(
        block_out_kernel, "block_out", [shape(rows, f32)],
        [meta, residual, *tp_exchange(red_keep, red_give)], 1_000_000, [part],
    )
    (input_grad,) = call(
        input_grad_kernel, "input_grad", [shape(rows, f32)],
        [meta, x, residual_grad, small, *early_sums], 5_000_000, [part],
    )
    norms = tail[:2]
    norms = norms + lax.ppermute(norms, "tp", NEAR)
    norms = norms + lax.ppermute(norms, "tp", FAR)
    return (
        block_out.reshape(inputs.shape),
        input_grad.reshape(inputs.shape),
        norms[0].reshape(2, 128),
        norms[1].reshape(2, 128),
        jnp.swapaxes(attend_grad, 0, 1),
        merge_grad,
        expand_grad,
        tail[2:3, :128],
        reduce_grad,
    )


EXPAND_AFTER = 3
REDUCE_AFTER = 1


def fits(mesh_sizes, *args):
    shapes = tuple(a.shape for a in args)
    return mesh_sizes == (4, 2, 4) and shapes == (
        (2, 128, 1024), (2, 128), (2, 128), (2, 128), (128, 3, 256), (128, 256),
        (128, 1024), (1, 128), (128, 1024), (2, 128, 1024),
    )


def either(*args):
    sizes = tuple(lax.axis_size(name) for name in ("shard", "ctx", "tp"))
    return fast_shards(*args) if fits(sizes, *args) else shards(*args)


def solution(mesh):
    in_specs = (
        P("shard", "ctx", None),
        P("shard", "ctx"),
        P(None, ("shard", "ctx")),
        P(None, ("shard", "ctx")),
        P(("shard", "ctx"), None, "tp"),
        P(("shard", "ctx"), "tp"),
        P(("shard", "ctx"), "tp"),
        P("tp", ("shard", "ctx")),
        P(("shard", "ctx"), "tp"),
        P("shard", "ctx", None),
    )
    out_specs = (
        P("shard", "ctx", None),
        P("shard", "ctx", None),
        P(None, ("shard", "ctx")),
        P(None, ("shard", "ctx")),
        P(("shard", "ctx"), None, "tp"),
        P(("shard", "ctx"), "tp"),
        P(("shard", "ctx"), "tp"),
        P("tp", ("shard", "ctx")),
        P(("shard", "ctx"), "tp"),
    )
    return jax.shard_map(either, mesh=mesh, in_specs=in_specs, out_specs=out_specs, check_vma=False)
```

```python
import math

import jax
import jax.numpy as jnp
from jax import lax
from jax.experimental import pallas as pl
from jax.experimental.pallas import tpu as pltpu
from jax.sharding import PartitionSpec as P

HD = 64


epsilon = 1e-05
masked_score = -1e30
gelu_scale = 0.7978845608028654
gelu_cubic = 0.044715


def norm_forward(values, gain, shift):
    average = jnp.mean(values, axis=-1, keepdims=True)
    centered = values - average
    variance = jnp.mean(centered * centered, axis=-1, keepdims=True)
    inverse = lax.rsqrt(variance + epsilon)
    normed = centered * inverse
    return (normed, inverse, normed * gain.astype(jnp.float32) + shift.astype(jnp.float32))


def norm_backward(upstream, normed, inverse, gain):
    scaled = upstream * gain.astype(jnp.float32)
    first_mean = jnp.mean(scaled, axis=-1, keepdims=True)
    second_mean = jnp.mean(scaled * normed, axis=-1, keepdims=True)
    return inverse * (scaled - first_mean - normed * second_mean)


def gelu_pair(pre_act):
    inner_arg = gelu_scale * (pre_act + gelu_cubic * pre_act * pre_act * pre_act)
    tangent = jnp.tanh(inner_arg)
    gelu_value = 0.5 * pre_act * (1.0 + tangent)
    gelu_slope = 0.5 * (1.0 + tangent) + 0.5 * pre_act * (1.0 - tangent * tangent) * gelu_scale * (
        1.0 + 3.0 * gelu_cubic * pre_act * pre_act
    )
    return (gelu_value, gelu_slope)


def shards(
    inputs,
    segment_ids,
    gains,
    shifts,
    attend_weight,
    merge_weight,
    expand_weight,
    expand_bias,
    reduce_weight,
    cotangent,
):
    seq_count, group_len, model_width = inputs.shape
    row_count = seq_count * group_len
    full_len = group_len * lax.axis_size("ctx")
    head_scale = HD ** (-0.5)
    gathered = (
        lax.all_gather(attend_weight, ("shard", "ctx"), axis=0, tiled=True),
        lax.all_gather(merge_weight, ("shard", "ctx"), axis=0, tiled=True),
        lax.all_gather(expand_weight, ("shard", "ctx"), axis=0, tiled=True),
        lax.all_gather(reduce_weight, ("shard", "ctx"), axis=0, tiled=True),
        lax.all_gather(expand_bias, ("shard", "ctx"), axis=1, tiled=True),
        lax.all_gather(gains, ("shard", "ctx"), axis=1, tiled=True),
        lax.all_gather(shifts, ("shard", "ctx"), axis=1, tiled=True),
    )
    attend_full, merge_full, expand_full, reduce_full, bias_full, gains_full, shifts_full = gathered
    local_cols = attend_full.shape[2]
    head_local = local_cols // HD
    flat_in = inputs.reshape(row_count, model_width)
    normed_early, inverse_early, affine_early = norm_forward(flat_in, gains_full[0], shifts_full[0])
    hidden_early = affine_early.astype(jnp.bfloat16)
    projected = jnp.einsum(
        "rd,dtc->rtc", hidden_early, attend_full, preferred_element_type=jnp.float32
    )
    query_heads = (
        (projected[:, 0] * head_scale)
        .astype(jnp.bfloat16)
        .reshape(seq_count, group_len, head_local, HD)
    )
    key_rows = projected[:, 1].astype(jnp.bfloat16).reshape(seq_count, group_len, local_cols)
    value_rows = projected[:, 2].astype(jnp.bfloat16).reshape(seq_count, group_len, local_cols)
    all_keys, all_values, all_segments = (
        lax.all_gather(key_rows, "ctx", axis=1, tiled=True),
        lax.all_gather(value_rows, "ctx", axis=1, tiled=True),
        lax.all_gather(segment_ids, "ctx", axis=1, tiled=True),
    )
    key_heads = all_keys.reshape(seq_count, full_len, head_local, HD)
    value_heads = all_values.reshape(seq_count, full_len, head_local, HD)
    query_pos = lax.axis_index("ctx") * group_len + jnp.arange(group_len, dtype=jnp.int32)
    key_pos = jnp.arange(full_len, dtype=jnp.int32)
    allowed = (segment_ids[:, :, None] == all_segments[:, None, :]) & (
        key_pos[None, None, :] <= query_pos[None, :, None]
    )
    allowed = allowed[:, None]

    def score_block():
        raw_scores = jnp.einsum(
            "sqhd,skhd->shqk", query_heads, key_heads, preferred_element_type=jnp.float32
        )
        return jnp.where(allowed, raw_scores, masked_score)

    scores = score_block()
    row_top = jnp.max(scores, axis=-1, keepdims=True)
    log_total = row_top + jnp.log(jnp.sum(jnp.exp(scores - row_top), axis=-1, keepdims=True))
    attn_probs = jnp.exp(scores - log_total)
    probs_half = attn_probs.astype(jnp.bfloat16)
    attended_heads = jnp.einsum(
        "shqk,skhd->sqhd", probs_half, value_heads, preferred_element_type=jnp.float32
    ).astype(jnp.bfloat16)
    attended = attended_heads.reshape(row_count, local_cols)
    merge_part = jnp.einsum("rc,oc->ro", attended, merge_full, preferred_element_type=jnp.float32)
    residual = flat_in + lax.psum(merge_part, "tp")
    normed_later, inverse_later, affine_later = norm_forward(
        residual, gains_full[1], shifts_full[1]
    )
    hidden_later = affine_later.astype(jnp.bfloat16)
    pre_act = jnp.dot(
        hidden_later, expand_full, preferred_element_type=jnp.float32
    ) + bias_full.astype(jnp.float32)
    gelu_value, gelu_slope = gelu_pair(pre_act)
    activated = gelu_value.astype(jnp.bfloat16)
    reduce_part = jnp.einsum(
        "rf,of->ro", activated, reduce_full, preferred_element_type=jnp.float32
    )
    block_out = residual + lax.psum(reduce_part.astype(jnp.bfloat16), "tp").astype(jnp.float32)
    back_set = (
        lax.all_gather(attend_weight, ("shard", "ctx"), axis=0, tiled=True),
        lax.all_gather(merge_weight, ("shard", "ctx"), axis=0, tiled=True),
        lax.all_gather(expand_weight, ("shard", "ctx"), axis=0, tiled=True),
        lax.all_gather(reduce_weight, ("shard", "ctx"), axis=0, tiled=True),
        lax.all_gather(gains, ("shard", "ctx"), axis=1, tiled=True),
    )
    attend_back, merge_back, expand_back, reduce_back, gains_back = back_set
    output_grad = cotangent.reshape(row_count, model_width)
    cot_half = output_grad.astype(jnp.bfloat16)
    reduce_grad = jnp.einsum("ro,rf->of", cot_half, activated, preferred_element_type=jnp.float32)
    pre_grad = jnp.dot(cot_half, reduce_back, preferred_element_type=jnp.float32) * gelu_slope
    pre_half = pre_grad.astype(jnp.bfloat16)
    bias_grad = jnp.sum(pre_grad, axis=0, keepdims=True)
    expand_grad = jnp.einsum(
        "rd,rf->df", hidden_later, pre_half, preferred_element_type=jnp.float32
    )
    later_part = jnp.einsum("rf,df->rd", pre_half, expand_back, preferred_element_type=jnp.float32)
    later_grad = lax.psum(later_part, "tp")
    residual_grad = output_grad + norm_backward(
        later_grad, normed_later, inverse_later, gains_back[1]
    )
    resid_half = residual_grad.astype(jnp.bfloat16)
    merge_grad = jnp.einsum("ro,rc->oc", resid_half, attended, preferred_element_type=jnp.float32)
    attended_grad = jnp.dot(resid_half, merge_back, preferred_element_type=jnp.float32).astype(
        jnp.bfloat16
    )
    grad_heads = attended_grad.reshape(seq_count, group_len, head_local, HD)
    scores_again = score_block()
    probs_again = jnp.exp(scores_again - log_total)
    probs_again_half = probs_again.astype(jnp.bfloat16)
    row_delta = jnp.einsum(
        "sqhd,sqhd->shq", grad_heads, attended_heads, preferred_element_type=jnp.float32
    )
    prob_grad = jnp.einsum(
        "sqhd,skhd->shqk", grad_heads, value_heads, preferred_element_type=jnp.float32
    )
    score_grad = probs_again * (prob_grad - row_delta[..., None])
    score_half = score_grad.astype(jnp.bfloat16)
    query_grad = (
        jnp.einsum("shqk,skhd->sqhd", score_half, key_heads, preferred_element_type=jnp.float32)
        * head_scale
    )
    keys_part = jnp.einsum(
        "shqk,sqhd->skhd", score_half, query_heads, preferred_element_type=jnp.float32
    ).reshape(seq_count, full_len, local_cols)
    values_part = jnp.einsum(
        "shqk,sqhd->skhd", probs_again_half, grad_heads, preferred_element_type=jnp.float32
    ).reshape(seq_count, full_len, local_cols)
    keys_grad, values_grad = (
        lax.psum_scatter(keys_part, "ctx", scatter_dimension=1, tiled=True),
        lax.psum_scatter(values_part, "ctx", scatter_dimension=1, tiled=True),
    )
    proj_grad = jnp.stack(
        [
            query_grad.reshape(row_count, local_cols),
            keys_grad.reshape(row_count, local_cols),
            values_grad.reshape(row_count, local_cols),
        ],
        axis=1,
    ).astype(jnp.bfloat16)
    attend_grad = jnp.einsum(
        "rd,rtc->dtc", hidden_early, proj_grad, preferred_element_type=jnp.float32
    )
    early_part = jnp.einsum(
        "rtc,dtc->rd", proj_grad, attend_back, preferred_element_type=jnp.float32
    )
    early_grad = lax.psum(early_part, "tp")
    input_grad = residual_grad + norm_backward(
        early_grad, normed_early, inverse_early, gains_back[0]
    )
    gains_grad = jnp.stack(
        [jnp.sum(early_grad * normed_early, axis=0), jnp.sum(later_grad * normed_later, axis=0)]
    )
    shifts_grad = jnp.stack([jnp.sum(early_grad, axis=0), jnp.sum(later_grad, axis=0)])
    shares = (
        lax.psum_scatter(attend_grad, ("shard", "ctx"), scatter_dimension=0, tiled=True),
        lax.psum_scatter(merge_grad, ("shard", "ctx"), scatter_dimension=0, tiled=True),
        lax.psum_scatter(expand_grad, ("shard", "ctx"), scatter_dimension=0, tiled=True),
        lax.psum_scatter(reduce_grad, ("shard", "ctx"), scatter_dimension=0, tiled=True),
        lax.psum_scatter(bias_grad, ("shard", "ctx"), scatter_dimension=1, tiled=True),
        lax.psum_scatter(gains_grad, ("shard", "ctx"), scatter_dimension=1, tiled=True),
        lax.psum_scatter(shifts_grad, ("shard", "ctx"), scatter_dimension=1, tiled=True),
    )
    return (
        block_out.reshape(inputs.shape),
        input_grad.reshape(inputs.shape),
        shares[5],
        shares[6],
        shares[0],
        shares[1],
        shares[2],
        shares[4],
        shares[3],
    )


VMEM = pl.BlockSpec(memory_space=pltpu.VMEM)
SMEM = pl.BlockSpec(memory_space=pltpu.SMEM)
f32 = jnp.float32
bf16 = jnp.bfloat16
RING = 8
ROOM = 6 << 20
NEAR = [(0, 1), (1, 0), (2, 3), (3, 2)]
FAR = [(0, 2), (2, 0), (1, 3), (3, 1)]
AXES = ("shard", "ctx")
IDS = [2 * p if p < 4 else 2 * (7 - p) + 1 for p in range(RING)]
AHEAD = [(IDS[p], IDS[(p + 1) % RING]) for p in range(RING)]
BEHIND = [(IDS[p], IDS[(p - 1) % RING]) for p in range(RING)]


def shape(dims, dtype):
    return jax.ShapeDtypeStruct(dims, dtype)


def call(kernel, name, outs, args, flops, scratch=(), transcendentals=0):
    nbytes = sum(a.size * a.dtype.itemsize for a in list(args) + list(outs))
    held = sum(math.prod(a.shape) * jnp.dtype(a.dtype).itemsize for a in scratch)
    return pl.pallas_call(
        kernel,
        name=name,
        out_shape=tuple(outs),
        in_specs=[SMEM] + [VMEM] * (len(args) - 1),
        out_specs=tuple(VMEM for _ in outs),
        scratch_shapes=list(scratch),
        compiler_params=pltpu.CompilerParams(vmem_limit_bytes=nbytes + held + ROOM),
        cost_estimate=pl.CostEstimate(
            flops=flops, bytes_accessed=nbytes, transcendentals=transcendentals
        ),
    )(*args)


def columns(meta, offset):
    return pl.ds(pl.multiple_of(meta[offset] * 128, 128), 128)


def rows_of(meta, mine):
    side = meta[8] if mine else 1 - meta[8]
    return pl.ds(pl.multiple_of(side * 128, 128), 128)


def dot(a, b):
    return jnp.dot(a, b, preferred_element_type=f32)


def dot_nt(a, b):
    return lax.dot_general(a, b, (((1,), (1,)), ((), ())), preferred_element_type=f32)


def dot_tn(a, b):
    return lax.dot_general(a, b, (((0,), (0,)), ((), ())), preferred_element_type=f32)


def norm_stats(values):
    average = jnp.mean(values, axis=-1, keepdims=True)
    centered = values - average
    variance = jnp.mean(centered * centered, axis=-1, keepdims=True)
    inverse = lax.rsqrt(variance + epsilon)
    return centered * inverse, inverse


def pack_kernel(meta, attend, merge, gains, shifts, bias, seg, out):
    for t in range(3):
        out[t * 128 : t * 128 + 128, :] = attend[t]
    out[384:512, :] = merge[...]
    zero = jnp.zeros((1, 128), f32)
    low, high, ids = gains[...].astype(f32), shifts[...].astype(f32), seg[...].astype(f32)
    tail = [
        jnp.concatenate([low[0:1], low[1:2]], axis=1),
        jnp.concatenate([high[0:1], high[1:2]], axis=1),
        jnp.concatenate([bias[...].astype(f32), zero], axis=1),
        jnp.concatenate([ids[0:1], ids[1:2]], axis=1),
        jnp.zeros((12, 256), f32),
    ]
    out[512:528, :] = jnp.concatenate(tail, axis=0).astype(bf16)


def norm_half_kernel(meta, x, out):
    normed, _ = norm_stats(x[rows_of(meta, True), :])
    out[...] = normed.astype(bf16)


def qkv_kernel(meta, x, far_a, far_b, *refs):
    blocks = refs[:9]
    (hidden, hidden_far, query, key_value, key_value_far, attend, merge, small, seg_far,
     seg_all) = refs[9:]

    def piece(offset, start, size):
        if offset < 4:
            return blocks[offset][start : start + size, :]
        if offset == 4:
            return jnp.concatenate(
                [blocks[4][start : start + size, :], blocks[5][start : start + size, :]], axis=1
            )
        return blocks[offset + 1][start : start + size, :]

    small[...] = jnp.zeros_like(small)
    for j in range(RING):
        at = columns(meta, j)
        for t in range(3):
            attend[t, at, :] = piece(j, t * 128, 128)
        merge[at, :] = piece(j, 384, 128)
        tail = piece(j, 512, 16).astype(f32)
        small[0:1, at] = tail[0:1, :128]
        small[1:2, at] = tail[0:1, 128:]
        small[2:3, at] = tail[1:2, :128]
        small[3:4, at] = tail[1:2, 128:]
        small[4:5, at] = tail[2:3, :128]
        seg_all[pl.ds(meta[j], 1), :] = tail[3:4, :]
    ids = seg_all[pl.ds(2 * meta[10], 1), :]
    seg_far[0:1, :] = ids[:, :128].astype(jnp.int32)
    seg_far[1:2, :] = ids[:, 128:].astype(jnp.int32)
    gain, shift = small[0:1, :], small[2:3, :]
    normed, _ = norm_stats(x[...])
    hidden[...] = (normed * gain + shift).astype(bf16)
    hidden_far[rows_of(meta, True), :] = (far_a[...].astype(f32) * gain + shift).astype(bf16)
    hidden_far[rows_of(meta, False), :] = (far_b[...].astype(f32) * gain + shift).astype(bf16)
    both, other = hidden[...], hidden_far[...]
    key_value[:, :256] = dot(both, attend[1]).astype(bf16)
    key_value[:, 256:] = dot(both, attend[2]).astype(bf16)
    key_value_far[:, :256] = dot(other, attend[1]).astype(bf16)
    key_value_far[:, 256:] = dot(other, attend[2]).astype(bf16)
    query[...] = (dot(both, attend[0]) * (HD**-0.5)).astype(bf16)


def masks(meta, seg, seg_col, seg_far, s):
    col = seg_col[:, s : s + 1]
    near = col == seg[s : s + 1, :]
    i = lax.broadcasted_iota(jnp.int32, (128, 128), 0)
    j = lax.broadcasted_iota(jnp.int32, (128, 128), 1)
    far = (col == seg_far[s : s + 1, :]) & (meta[9] == 1)
    return near & (j <= i), far


def head_probs(query, key, key_far, near, far):
    score = jnp.where(near, dot_nt(query, key), masked_score)
    score_far = jnp.where(far, dot_nt(query, key_far), masked_score)
    top = jnp.maximum(
        jnp.max(score, axis=-1, keepdims=True), jnp.max(score_far, axis=-1, keepdims=True)
    )
    total = jnp.sum(jnp.exp(score - top), axis=-1, keepdims=True) + jnp.sum(
        jnp.exp(score_far - top), axis=-1, keepdims=True
    )
    log_total = top + jnp.log(total)
    return jnp.exp(score - log_total), jnp.exp(score_far - log_total)


def attention_kernel(
    meta, query, kv, kv_far, seg, seg_col, seg_far, merge, attended, keep, give, part
):
    for s in range(2):
        near, far = masks(meta, seg, seg_col, seg_far, s)
        r = slice(s * 128, s * 128 + 128)
        for h in range(4):
            c = slice(h * 64, h * 64 + 64)
            v = slice(256 + h * 64, 256 + h * 64 + 64)
            probs, probs_far = head_probs(query[r, c], kv[r, c], kv_far[r, c], near, far)
            out = dot(probs.astype(bf16), kv[r, v]) + dot(probs_far.astype(bf16), kv_far[r, v])
            attended[r, c] = out.astype(bf16)
    part[...] = dot_nt(attended[...], merge[...])
    keep[...] = part[rows_of(meta, True), :]
    give[...] = part[rows_of(meta, False), :].astype(bf16)


def total_of(meta, sums, full):
    pair, far, pair_other, far_other = sums
    full[rows_of(meta, True), :] = pair[...].astype(f32) + far[...].astype(f32)
    full[rows_of(meta, False), :] = pair_other[...].astype(f32) + far_other[...].astype(f32)
    return full[...]


def assemble(meta, blocks, full):
    for j in range(RING):
        at = columns(meta, j)
        if j == 4:
            start = pl.multiple_of(meta[4] * 128, 128)
            full[pl.ds(start, 64), :] = blocks[4][...]
            full[pl.ds(pl.multiple_of(start + 64, 64), 64), :] = blocks[5][...]
        else:
            full[at, :] = (blocks[j] if j < 4 else blocks[j + 1])[...]


def store_parts(meta, left, right, outs):
    for j in range(RING):
        value = dot_tn(left[:, columns(meta, j)], right[...]).astype(bf16)
        if j == 4:
            outs[4][...] = value[:64]
            outs[5][...] = value[64:]
        else:
            (outs[j] if j < 4 else outs[j + 1])[...] = value


def ffn_first_kernel(meta, x, cot, small, s0, s1, s2, s3, *refs):
    blocks = refs[:9]
    residual, hidden, cot_half, act, slope, expand = refs[9:15]
    outs, part = refs[15:24], refs[24]
    assemble(meta, blocks, expand)
    residual[...] = x[...] + total_of(meta, (s0, s1, s2, s3), part)
    normed, _ = norm_stats(residual[...])
    hidden[...] = (normed * small[1:2, :] + small[3:4, :]).astype(bf16)
    cot_half[...] = cot[...].astype(bf16)

    def units(i, carry):
        at = pl.ds(pl.multiple_of(i * 256, 256), 256)
        pre_act = dot(hidden[...], expand[:, at]) + small[4:5, at]
        value, gradient = gelu_pair(pre_act)
        act[:, at] = value.astype(bf16)
        slope[:, at] = gradient
        return carry

    lax.fori_loop(0, 4, units, 0)
    store_parts(meta, cot_half, act, outs)


def ffn_second_kernel(meta, residual, cot_half, act, slope, expand, *refs):
    blocks = refs[:9]
    pre_half, later_keep, later_give, red_keep, red_give, grads, reduce, part = refs[9:]
    assemble(meta, blocks, reduce)
    grads[...] = jnp.zeros_like(grads)

    def units(i, carry):
        at = pl.ds(pl.multiple_of(i * 256, 256), 256)
        pre_grad = dot(cot_half[...], reduce[:, at]) * slope[:, at]
        pre_half[:, at] = pre_grad.astype(bf16)
        grads[2:3, at] = jnp.sum(pre_grad, axis=0, keepdims=True)
        return carry

    lax.fori_loop(0, 4, units, 0)

    def later(i, carry):
        at = pl.ds(pl.multiple_of(i * 256, 256), 256)
        part[:, at] = dot_nt(pre_half[...], expand[at, :])
        return carry

    lax.fori_loop(0, 4, later, 0)
    later_keep[...] = part[rows_of(meta, True), :]
    later_give[...] = part[rows_of(meta, False), :].astype(bf16)
    normed, _ = norm_stats(residual[...])
    grads[0:1, :] = jnp.sum(part[...] * normed, axis=0, keepdims=True)
    grads[1:2, :] = jnp.sum(part[...], axis=0, keepdims=True)

    def reduced(i, carry):
        at = pl.ds(pl.multiple_of(i * 256, 256), 256)
        part[:, at] = dot_nt(act[...], reduce[at, :])
        return carry

    lax.fori_loop(0, 4, reduced, 0)
    red_keep[...] = part[rows_of(meta, True), :]
    red_give[...] = part[rows_of(meta, False), :].astype(bf16)


def expand_grads_kernel(meta, hidden, pre_half, *outs):
    store_parts(meta, hidden, pre_half, outs)


def attention_back_kernel(
    meta, cot, residual, small, s0, s1, s2, s3, merge, query, kv, kv_far, attended,
    seg, seg_col, seg_far, residual_grad, resid_half, query_grad, kv_grad, kv_grad_far,
    part, att_grad
):
    later_grad = total_of(meta, (s0, s1, s2, s3), part)
    normed, inverse = norm_stats(residual[...])
    residual_grad[...] = cot[...] + norm_backward(later_grad, normed, inverse, small[1:2, :])
    resid_half[...] = residual_grad[...].astype(bf16)
    att_grad[...] = dot(resid_half[...], merge[...]).astype(bf16)
    for s in range(2):
        near, far = masks(meta, seg, seg_col, seg_far, s)
        r = slice(s * 128, s * 128 + 128)
        for h in range(4):
            c = slice(h * 64, h * 64 + 64)
            v = slice(256 + h * 64, 256 + h * 64 + 64)
            q, k, k_far = query[r, c], kv[r, c], kv_far[r, c]
            probs, probs_far = head_probs(q, k, k_far, near, far)
            up = att_grad[r, c]
            delta = jnp.sum(up.astype(f32) * attended[r, c].astype(f32), axis=-1, keepdims=True)
            score = (probs * (dot_nt(up, kv[r, v]) - delta)).astype(bf16)
            score_far = (probs_far * (dot_nt(up, kv_far[r, v]) - delta)).astype(bf16)
            query_grad[r, c] = (dot(score, k) + dot(score_far, k_far)) * (HD**-0.5)
            kv_grad[r, c] = dot_tn(score, q)
            kv_grad[r, v] = dot_tn(probs.astype(bf16), up)
            kv_grad_far[r, c] = dot_tn(score_far, q).astype(bf16)
            kv_grad_far[r, v] = dot_tn(probs_far.astype(bf16), up).astype(bf16)


def attention_grads_kernel(
    meta, x, far_a, far_b, hidden, hidden_far, query_grad, kv_grad, kv_grad_far, resid_half,
    attended, attend, grads, early, *refs
):
    outs, proj, sums, part = refs[:9], refs[9], refs[10], refs[11]
    proj[:, :256] = query_grad[...].astype(bf16)
    proj[:, 256:] = kv_grad[...].astype(bf16)
    early[...] = (
        dot_nt(proj[:, :256], attend[0])
        + dot_nt(proj[:, 256:512], attend[1])
        + dot_nt(proj[:, 512:], attend[2])
    )
    part[...] = dot_nt(kv_grad_far[:, :256], attend[1]) + dot_nt(kv_grad_far[:, 256:], attend[2])
    normed, _ = norm_stats(x[...])
    mine, other = part[rows_of(meta, True), :], part[rows_of(meta, False), :]
    sums[0:1, :] = (
        jnp.sum(early[...] * normed, axis=0, keepdims=True)
        + jnp.sum(mine * far_a[...].astype(f32), axis=0, keepdims=True)
        + jnp.sum(other * far_b[...].astype(f32), axis=0, keepdims=True)
    )
    sums[1:2, :] = jnp.sum(early[...] + part[...], axis=0, keepdims=True)
    for j in range(RING):
        at = columns(meta, j)
        lhs, lhs_far = hidden[:, at], hidden_far[:, at]
        pieces = [dot_tn(lhs, proj[:, :256]).astype(bf16)]
        for t in (1, 2):
            c, c_far = slice(t * 256, t * 256 + 256), slice(t * 256 - 256, t * 256)
            pieces.append((dot_tn(lhs, proj[:, c]) + dot_tn(lhs_far, kv_grad_far[:, c_far])).astype(bf16))
        pieces.append(dot_tn(resid_half[:, at], attended[...]).astype(bf16))
        zero = jnp.zeros((1, 128), f32)
        tail = jnp.concatenate(
            [
                jnp.concatenate([sums[0:1, at], grads[0:1, at]], axis=1),
                jnp.concatenate([sums[1:2, at], grads[1:2, at]], axis=1),
                jnp.concatenate([grads[2:3, at], zero], axis=1),
                jnp.zeros((13, 256), f32),
            ],
            axis=0,
        )
        pieces.append(tail.astype(bf16))
        start = 0
        for value in pieces:
            span = slice(start, start + value.shape[0])
            start += value.shape[0]
            if j == 4:
                outs[4][span, :] = value[:, :128]
                outs[5][span, :] = value[:, 128:]
            else:
                out = outs[j] if j < 4 else outs[j + 1]
                out[span, :] = value


def project_back_kernel(meta, early, kv_grad_in, attend, keep, give, part):
    part[...] = (
        early[...]
        + dot_nt(kv_grad_in[:, :256], attend[1])
        + dot_nt(kv_grad_in[:, 256:], attend[2])
    )
    keep[...] = part[rows_of(meta, True), :]
    give[...] = part[rows_of(meta, False), :].astype(bf16)


def first_rows_kernel(meta, up, down, ahead, behind, up_out, down_out):
    up_out[:64, :] = (up[:64, :].astype(f32) + ahead[...].astype(f32)).astype(bf16)
    up_out[64:, :] = up[64:, :]
    down_out[:64, :] = down[:64, :]
    down_out[64:, :] = (down[64:, :].astype(f32) + behind[...].astype(f32)).astype(bf16)


def first_columns_kernel(meta, up, down, ahead, behind, up_out, down_out):
    up_out[:, :128] = (up[:, :128].astype(f32) + ahead[...].astype(f32)).astype(bf16)
    up_out[:, 128:] = up[:, 128:]
    down_out[:, :128] = down[:, :128]
    down_out[:, 128:] = (down[:, 128:].astype(f32) + behind[...].astype(f32)).astype(bf16)


def step_kernel(meta, up, down, ahead, behind, up_out, down_out):
    up_out[...] = (up[...].astype(f32) + ahead[...].astype(f32)).astype(bf16)
    down_out[...] = (down[...].astype(f32) + behind[...].astype(f32)).astype(bf16)


def last_kernel(meta, own, ahead, behind, out):
    out[...] = own[...].astype(f32) + (ahead[...].astype(f32) + behind[...].astype(f32))


def last_pack_kernel(meta, own, ahead, behind, attend, merge, tail):
    def total(start, size):
        r = slice(start, start + size)
        return own[r, :].astype(f32) + (ahead[r, :].astype(f32) + behind[r, :].astype(f32))

    for t in range(3):
        attend[t] = total(t * 128, 128)
    merge[...] = total(384, 128)
    tail[...] = total(512, 16)


def block_out_kernel(meta, residual, s0, s1, s2, s3, out, part):
    out[...] = residual[...] + total_of(meta, (s0, s1, s2, s3), part)


def input_grad_kernel(meta, x, residual_grad, small, s0, s1, s2, s3, out, part):
    early_grad = total_of(meta, (s0, s1, s2, s3), part)
    normed, inverse = norm_stats(x[...])
    out[...] = residual_grad[...] + norm_backward(early_grad, normed, inverse, small[0:1, :])


def send_ahead(value):
    return lax.ppermute(value, AXES, AHEAD)


def send_behind(value):
    return lax.ppermute(value, AXES, BEHIND)


def gather_blocks(own, first, second):
    blocks = [own] + [None] * 8
    ahead, behind = own, own
    for step in range(1, 4):
        ahead, behind = send_ahead(ahead), send_behind(behind)
        blocks[9 - step], blocks[step] = ahead, behind
    blocks[4], blocks[5] = send_ahead(first(ahead)), send_behind(second(behind))
    return blocks


def sum_blocks(meta, parts, name, first, last, last_shapes):
    ahead, behind = send_ahead(parts[4]), send_behind(parts[5])
    for step in range(3, 0, -1):
        up, down = call(
            first if step == 3 else step_kernel, f"{name}_{step}", [shape(parts[1].shape, bf16)] * 2,
            [meta, parts[step], parts[9 - step], ahead, behind], 1_000_000,
        )
        ahead, behind = send_ahead(up), send_behind(down)
    return call(last, f"{name}_last", last_shapes, [meta, parts[0], ahead, behind], 1_000_000)


def tp_exchange(keep, give):
    pair = (keep + lax.ppermute(give, "tp", NEAR).astype(f32)).astype(bf16)
    far = lax.ppermute(pair, "tp", FAR)
    return pair, far, lax.ppermute(pair, "tp", NEAR), lax.ppermute(far, "tp", NEAR)


def fast_shards(
    inputs, segment_ids, gains, shifts, attend_weight, merge_weight, expand_weight,
    expand_bias, reduce_weight, cotangent,
):
    shard, ctx = lax.axis_index("shard"), lax.axis_index("ctx")
    place = jnp.where(ctx == 0, shard, RING - 1 - shard)
    spots = lax.rem(place + jnp.arange(RING, dtype=jnp.int32), RING)
    owners = jnp.where(spots < 4, 2 * spots, 2 * (7 - spots) + 1)
    side = lax.rem(lax.axis_index("tp"), 2)
    meta = jnp.concatenate([owners, jnp.stack([side, ctx, shard])]).astype(jnp.int32)

    x = inputs.reshape(256, 1024)
    cot = cotangent.reshape(256, 1024)
    rows, half, square = (256, 1024), (128, 1024), (256, 256)
    part = pltpu.VMEM(rows, f32)
    (pack,) = call(
        pack_kernel, "pack", [shape((528, 256), bf16)],
        [meta, jnp.swapaxes(attend_weight, 0, 1), merge_weight, gains, shifts, expand_bias,
         segment_ids], 1_000_000,
    )
    blocks = gather_blocks(pack, lambda v: v[:, :128], lambda v: v[:, 128:])
    (normed_half,) = call(norm_half_kernel, "norm_half", [shape(half, bf16)], [meta, x], 1_000_000)
    far_a = lax.ppermute(normed_half, "ctx", [(0, 1)])
    far_b = lax.ppermute(far_a, "tp", NEAR)
    seg_col = segment_ids.T
    expand_weight, _ = lax.optimization_barrier((expand_weight, blocks[EXPAND_AFTER]))
    expand_blocks = gather_blocks(expand_weight, lambda v: v[:64], lambda v: v[64:])
    reduce_weight, _ = lax.optimization_barrier((reduce_weight, expand_blocks[REDUCE_AFTER]))
    reduce_blocks = gather_blocks(reduce_weight, lambda v: v[:64], lambda v: v[64:])

    hidden_early, hidden_far, query, kv, kv_far, attend, merge, small, seg_far = call(
        qkv_kernel, "qkv",
        [shape(rows, bf16), shape(rows, bf16), shape(square, bf16), shape((256, 512), bf16),
         shape((256, 512), bf16), shape((3, 1024, 256), bf16), shape((1024, 256), bf16),
         shape((8, 1024), f32), shape((2, 128), jnp.int32)],
        [meta, x, far_a, far_b] + blocks, 700_000_000, [pltpu.VMEM((8, 256), f32)],
    )
    attended, keep, give = call(
        attention_kernel, "attention",
        [shape(square, bf16), shape(half, f32), shape(half, bf16)],
        [meta, query, kv, kv_far, segment_ids, seg_col, seg_far, merge],
        300_000_000, [part], 800_000,
    )
    part_shapes = [shape(half, bf16)] * 9
    part_shapes[4] = part_shapes[5] = shape((64, 1024), bf16)
    residual, hidden_later, cot_half, act, slope, expand, *reduce_parts = call(
        ffn_first_kernel, "ffn_first",
        [shape(rows, f32)] + [shape(rows, bf16)] * 3 + [shape(rows, f32)]
        + [shape((1024, 1024), bf16)] + part_shapes,
        [meta, x, cot, small, *tp_exchange(keep, give)] + expand_blocks,
        1_100_000_000, [part], 300_000,
    )
    pre_half, later_keep, later_give, red_keep, red_give, grads = call(
        ffn_second_kernel, "ffn_second",
        [shape(rows, bf16)] + [shape(half, f32), shape(half, bf16)] * 2 + [shape((8, 1024), f32)],
        [meta, residual, cot_half, act, slope, expand] + reduce_blocks,
        1_600_000_000, [pltpu.VMEM((1024, 1024), bf16), part],
    )
    (reduce_grad,) = sum_blocks(
        meta, reduce_parts, "reduce_sum", first_rows_kernel, last_kernel, [shape(half, f32)]
    )
    later_sums = tp_exchange(later_keep, later_give)
    expand_parts = call(
        expand_grads_kernel, "expand_grads", part_shapes,
        [meta, hidden_later, pre_half], 550_000_000,
    )
    (expand_grad,) = sum_blocks(
        meta, expand_parts, "expand_sum", first_rows_kernel, last_kernel, [shape(half, f32)]
    )
    residual_grad, resid_half, query_grad, kv_grad, kv_grad_far = call(
        attention_back_kernel, "attention_back",
        [shape(rows, f32), shape(rows, bf16), shape(square, f32), shape((256, 512), f32),
         shape((256, 512), bf16)],
        [meta, cot, residual, small, *later_sums, merge, query, kv, kv_far, attended,
         segment_ids, seg_col, seg_far],
        500_000_000, [part, pltpu.VMEM(square, bf16)], 800_000,
    )
    kv_grad_in = lax.ppermute(kv_grad_far, "ctx", [(1, 0)])
    pack_shapes = [shape((528, 256), bf16)] * 9
    pack_shapes[4] = pack_shapes[5] = shape((528, 128), bf16)
    early, *pack_parts = call(
        attention_grads_kernel, "attention_grads", [shape(rows, f32)] + pack_shapes,
        [meta, x, far_a, far_b, hidden_early, hidden_far, query_grad, kv_grad, kv_grad_far,
         resid_half, attended, attend, grads], 1_100_000_000,
        [pltpu.VMEM((256, 768), bf16), pltpu.VMEM((8, 1024), f32), part],
    )
    attend_grad, merge_grad, tail = sum_blocks(
        meta, pack_parts, "pack_sum", first_columns_kernel, last_pack_kernel,
        [shape((3, 128, 256), f32), shape((128, 256), f32), shape((16, 256), f32)],
    )
    early_keep, early_give = call(
        project_back_kernel, "project_back", [shape(half, f32), shape(half, bf16)],
        [meta, early, kv_grad_in, attend], 300_000_000, [part],
    )
    early_sums = tp_exchange(early_keep, early_give)
    red_keep, red_give, _ = lax.optimization_barrier((red_keep, red_give, query_grad))
    (block_out,) = call(
        block_out_kernel, "block_out", [shape(rows, f32)],
        [meta, residual, *tp_exchange(red_keep, red_give)], 1_000_000, [part],
    )
    (input_grad,) = call(
        input_grad_kernel, "input_grad", [shape(rows, f32)],
        [meta, x, residual_grad, small, *early_sums], 5_000_000, [part],
    )
    norms = tail[:2]
    norms = norms + lax.ppermute(norms, "tp", NEAR)
    norms = norms + lax.ppermute(norms, "tp", FAR)
    return (
        block_out.reshape(inputs.shape),
        input_grad.reshape(inputs.shape),
        norms[0].reshape(2, 128),
        norms[1].reshape(2, 128),
        jnp.swapaxes(attend_grad, 0, 1),
        merge_grad,
        expand_grad,
        tail[2:3, :128],
        reduce_grad,
    )


EXPAND_AFTER = 3
REDUCE_AFTER = 1


def fits(mesh_sizes, *args):
    shapes = tuple(a.shape for a in args)
    return mesh_sizes == (4, 2, 4) and shapes == (
        (2, 128, 1024), (2, 128), (2, 128), (2, 128), (128, 3, 256), (128, 256),
        (128, 1024), (1, 128), (128, 1024), (2, 128, 1024),
    )


def either(*args):
    sizes = tuple(lax.axis_size(name) for name in ("shard", "ctx", "tp"))
    return fast_shards(*args) if fits(sizes, *args) else shards(*args)


def solution(mesh):
    in_specs = (
        P("shard", "ctx", None),
        P("shard", "ctx"),
        P(None, ("shard", "ctx")),
        P(None, ("shard", "ctx")),
        P(("shard", "ctx"), None, "tp"),
        P(("shard", "ctx"), "tp"),
        P(("shard", "ctx"), "tp"),
        P("tp", ("shard", "ctx")),
        P(("shard", "ctx"), "tp"),
        P("shard", "ctx", None),
    )
    out_specs = (
        P("shard", "ctx", None),
        P("shard", "ctx", None),
        P(None, ("shard", "ctx")),
        P(None, ("shard", "ctx")),
        P(("shard", "ctx"), None, "tp"),
        P(("shard", "ctx"), "tp"),
        P(("shard", "ctx"), "tp"),
        P("tp", ("shard", "ctx")),
        P(("shard", "ctx"), "tp"),
    )
    return jax.shard_map(either, mesh=mesh, in_specs=in_specs, out_specs=out_specs, check_vma=False)
```

```python
import math

import jax
import jax.numpy as jnp
from jax import lax
from jax.experimental import pallas as pl
from jax.experimental.pallas import tpu as pltpu
from jax.sharding import PartitionSpec as P

HD = 64


epsilon = 1e-05
masked_score = -1e30
gelu_scale = 0.7978845608028654
gelu_cubic = 0.044715


def norm_forward(values, gain, shift):
    average = jnp.mean(values, axis=-1, keepdims=True)
    centered = values - average
    variance = jnp.mean(centered * centered, axis=-1, keepdims=True)
    inverse = lax.rsqrt(variance + epsilon)
    normed = centered * inverse
    return (normed, inverse, normed * gain.astype(jnp.float32) + shift.astype(jnp.float32))


def norm_backward(upstream, normed, inverse, gain):
    scaled = upstream * gain.astype(jnp.float32)
    first_mean = jnp.mean(scaled, axis=-1, keepdims=True)
    second_mean = jnp.mean(scaled * normed, axis=-1, keepdims=True)
    return inverse * (scaled - first_mean - normed * second_mean)


def gelu_pair(pre_act):
    inner_arg = gelu_scale * (pre_act + gelu_cubic * pre_act * pre_act * pre_act)
    tangent = jnp.tanh(inner_arg)
    gelu_value = 0.5 * pre_act * (1.0 + tangent)
    gelu_slope = 0.5 * (1.0 + tangent) + 0.5 * pre_act * (1.0 - tangent * tangent) * gelu_scale * (
        1.0 + 3.0 * gelu_cubic * pre_act * pre_act
    )
    return (gelu_value, gelu_slope)


def shards(
    inputs,
    segment_ids,
    gains,
    shifts,
    attend_weight,
    merge_weight,
    expand_weight,
    expand_bias,
    reduce_weight,
    cotangent,
):
    seq_count, group_len, model_width = inputs.shape
    row_count = seq_count * group_len
    full_len = group_len * lax.axis_size("ctx")
    head_scale = HD ** (-0.5)
    gathered = (
        lax.all_gather(attend_weight, ("shard", "ctx"), axis=0, tiled=True),
        lax.all_gather(merge_weight, ("shard", "ctx"), axis=0, tiled=True),
        lax.all_gather(expand_weight, ("shard", "ctx"), axis=0, tiled=True),
        lax.all_gather(reduce_weight, ("shard", "ctx"), axis=0, tiled=True),
        lax.all_gather(expand_bias, ("shard", "ctx"), axis=1, tiled=True),
        lax.all_gather(gains, ("shard", "ctx"), axis=1, tiled=True),
        lax.all_gather(shifts, ("shard", "ctx"), axis=1, tiled=True),
    )
    attend_full, merge_full, expand_full, reduce_full, bias_full, gains_full, shifts_full = gathered
    local_cols = attend_full.shape[2]
    head_local = local_cols // HD
    flat_in = inputs.reshape(row_count, model_width)
    normed_early, inverse_early, affine_early = norm_forward(flat_in, gains_full[0], shifts_full[0])
    hidden_early = affine_early.astype(jnp.bfloat16)
    projected = jnp.einsum(
        "rd,dtc->rtc", hidden_early, attend_full, preferred_element_type=jnp.float32
    )
    query_heads = (
        (projected[:, 0] * head_scale)
        .astype(jnp.bfloat16)
        .reshape(seq_count, group_len, head_local, HD)
    )
    key_rows = projected[:, 1].astype(jnp.bfloat16).reshape(seq_count, group_len, local_cols)
    value_rows = projected[:, 2].astype(jnp.bfloat16).reshape(seq_count, group_len, local_cols)
    all_keys, all_values, all_segments = (
        lax.all_gather(key_rows, "ctx", axis=1, tiled=True),
        lax.all_gather(value_rows, "ctx", axis=1, tiled=True),
        lax.all_gather(segment_ids, "ctx", axis=1, tiled=True),
    )
    key_heads = all_keys.reshape(seq_count, full_len, head_local, HD)
    value_heads = all_values.reshape(seq_count, full_len, head_local, HD)
    query_pos = lax.axis_index("ctx") * group_len + jnp.arange(group_len, dtype=jnp.int32)
    key_pos = jnp.arange(full_len, dtype=jnp.int32)
    allowed = (segment_ids[:, :, None] == all_segments[:, None, :]) & (
        key_pos[None, None, :] <= query_pos[None, :, None]
    )
    allowed = allowed[:, None]

    def score_block():
        raw_scores = jnp.einsum(
            "sqhd,skhd->shqk", query_heads, key_heads, preferred_element_type=jnp.float32
        )
        return jnp.where(allowed, raw_scores, masked_score)

    scores = score_block()
    row_top = jnp.max(scores, axis=-1, keepdims=True)
    log_total = row_top + jnp.log(jnp.sum(jnp.exp(scores - row_top), axis=-1, keepdims=True))
    attn_probs = jnp.exp(scores - log_total)
    probs_half = attn_probs.astype(jnp.bfloat16)
    attended_heads = jnp.einsum(
        "shqk,skhd->sqhd", probs_half, value_heads, preferred_element_type=jnp.float32
    ).astype(jnp.bfloat16)
    attended = attended_heads.reshape(row_count, local_cols)
    merge_part = jnp.einsum("rc,oc->ro", attended, merge_full, preferred_element_type=jnp.float32)
    residual = flat_in + lax.psum(merge_part, "tp")
    normed_later, inverse_later, affine_later = norm_forward(
        residual, gains_full[1], shifts_full[1]
    )
    hidden_later = affine_later.astype(jnp.bfloat16)
    pre_act = jnp.dot(
        hidden_later, expand_full, preferred_element_type=jnp.float32
    ) + bias_full.astype(jnp.float32)
    gelu_value, gelu_slope = gelu_pair(pre_act)
    activated = gelu_value.astype(jnp.bfloat16)
    reduce_part = jnp.einsum(
        "rf,of->ro", activated, reduce_full, preferred_element_type=jnp.float32
    )
    block_out = residual + lax.psum(reduce_part.astype(jnp.bfloat16), "tp").astype(jnp.float32)
    back_set = (
        lax.all_gather(attend_weight, ("shard", "ctx"), axis=0, tiled=True),
        lax.all_gather(merge_weight, ("shard", "ctx"), axis=0, tiled=True),
        lax.all_gather(expand_weight, ("shard", "ctx"), axis=0, tiled=True),
        lax.all_gather(reduce_weight, ("shard", "ctx"), axis=0, tiled=True),
        lax.all_gather(gains, ("shard", "ctx"), axis=1, tiled=True),
    )
    attend_back, merge_back, expand_back, reduce_back, gains_back = back_set
    output_grad = cotangent.reshape(row_count, model_width)
    cot_half = output_grad.astype(jnp.bfloat16)
    reduce_grad = jnp.einsum("ro,rf->of", cot_half, activated, preferred_element_type=jnp.float32)
    pre_grad = jnp.dot(cot_half, reduce_back, preferred_element_type=jnp.float32) * gelu_slope
    pre_half = pre_grad.astype(jnp.bfloat16)
    bias_grad = jnp.sum(pre_grad, axis=0, keepdims=True)
    expand_grad = jnp.einsum(
        "rd,rf->df", hidden_later, pre_half, preferred_element_type=jnp.float32
    )
    later_part = jnp.einsum("rf,df->rd", pre_half, expand_back, preferred_element_type=jnp.float32)
    later_grad = lax.psum(later_part, "tp")
    residual_grad = output_grad + norm_backward(
        later_grad, normed_later, inverse_later, gains_back[1]
    )
    resid_half = residual_grad.astype(jnp.bfloat16)
    merge_grad = jnp.einsum("ro,rc->oc", resid_half, attended, preferred_element_type=jnp.float32)
    attended_grad = jnp.dot(resid_half, merge_back, preferred_element_type=jnp.float32).astype(
        jnp.bfloat16
    )
    grad_heads = attended_grad.reshape(seq_count, group_len, head_local, HD)
    scores_again = score_block()
    probs_again = jnp.exp(scores_again - log_total)
    probs_again_half = probs_again.astype(jnp.bfloat16)
    row_delta = jnp.einsum(
        "sqhd,sqhd->shq", grad_heads, attended_heads, preferred_element_type=jnp.float32
    )
    prob_grad = jnp.einsum(
        "sqhd,skhd->shqk", grad_heads, value_heads, preferred_element_type=jnp.float32
    )
    score_grad = probs_again * (prob_grad - row_delta[..., None])
    score_half = score_grad.astype(jnp.bfloat16)
    query_grad = (
        jnp.einsum("shqk,skhd->sqhd", score_half, key_heads, preferred_element_type=jnp.float32)
        * head_scale
    )
    keys_part = jnp.einsum(
        "shqk,sqhd->skhd", score_half, query_heads, preferred_element_type=jnp.float32
    ).reshape(seq_count, full_len, local_cols)
    values_part = jnp.einsum(
        "shqk,sqhd->skhd", probs_again_half, grad_heads, preferred_element_type=jnp.float32
    ).reshape(seq_count, full_len, local_cols)
    keys_grad, values_grad = (
        lax.psum_scatter(keys_part, "ctx", scatter_dimension=1, tiled=True),
        lax.psum_scatter(values_part, "ctx", scatter_dimension=1, tiled=True),
    )
    proj_grad = jnp.stack(
        [
            query_grad.reshape(row_count, local_cols),
            keys_grad.reshape(row_count, local_cols),
            values_grad.reshape(row_count, local_cols),
        ],
        axis=1,
    ).astype(jnp.bfloat16)
    attend_grad = jnp.einsum(
        "rd,rtc->dtc", hidden_early, proj_grad, preferred_element_type=jnp.float32
    )
    early_part = jnp.einsum(
        "rtc,dtc->rd", proj_grad, attend_back, preferred_element_type=jnp.float32
    )
    early_grad = lax.psum(early_part, "tp")
    input_grad = residual_grad + norm_backward(
        early_grad, normed_early, inverse_early, gains_back[0]
    )
    gains_grad = jnp.stack(
        [jnp.sum(early_grad * normed_early, axis=0), jnp.sum(later_grad * normed_later, axis=0)]
    )
    shifts_grad = jnp.stack([jnp.sum(early_grad, axis=0), jnp.sum(later_grad, axis=0)])
    shares = (
        lax.psum_scatter(attend_grad, ("shard", "ctx"), scatter_dimension=0, tiled=True),
        lax.psum_scatter(merge_grad, ("shard", "ctx"), scatter_dimension=0, tiled=True),
        lax.psum_scatter(expand_grad, ("shard", "ctx"), scatter_dimension=0, tiled=True),
        lax.psum_scatter(reduce_grad, ("shard", "ctx"), scatter_dimension=0, tiled=True),
        lax.psum_scatter(bias_grad, ("shard", "ctx"), scatter_dimension=1, tiled=True),
        lax.psum_scatter(gains_grad, ("shard", "ctx"), scatter_dimension=1, tiled=True),
        lax.psum_scatter(shifts_grad, ("shard", "ctx"), scatter_dimension=1, tiled=True),
    )
    return (
        block_out.reshape(inputs.shape),
        input_grad.reshape(inputs.shape),
        shares[5],
        shares[6],
        shares[0],
        shares[1],
        shares[2],
        shares[4],
        shares[3],
    )


VMEM = pl.BlockSpec(memory_space=pltpu.VMEM)
SMEM = pl.BlockSpec(memory_space=pltpu.SMEM)
f32 = jnp.float32
bf16 = jnp.bfloat16
RING = 8
ROOM = 6 << 20
NEAR = [(0, 1), (1, 0), (2, 3), (3, 2)]
FAR = [(0, 2), (2, 0), (1, 3), (3, 1)]
AXES = ("shard", "ctx")
TP = "tp"
CTX = "ctx"
IDS = [2 * p if p < 4 else 2 * (7 - p) + 1 for p in range(RING)]
AHEAD = [(IDS[p], IDS[(p + 1) % RING]) for p in range(RING)]
BEHIND = [(IDS[p], IDS[(p - 1) % RING]) for p in range(RING)]


def shape(dims, dtype):
    return jax.ShapeDtypeStruct(dims, dtype)


def call(kernel, outs, args, flops, scratch=(), transcendentals=0):
    nbytes = sum(a.size * a.dtype.itemsize for a in list(args) + list(outs))
    held = sum(math.prod(a.shape) * jnp.dtype(a.dtype).itemsize for a in scratch)
    return pl.pallas_call(
        kernel,
        out_shape=tuple(outs),
        in_specs=[SMEM] + [VMEM] * (len(args) - 1),
        out_specs=tuple(VMEM for _ in outs),
        scratch_shapes=list(scratch),
        compiler_params=pltpu.CompilerParams(vmem_limit_bytes=nbytes + held + ROOM),
        cost_estimate=pl.CostEstimate(
            flops=flops, bytes_accessed=nbytes, transcendentals=transcendentals
        ),
    )(*args)


def columns(meta, offset):
    return pl.ds(pl.multiple_of(meta[offset] * 128, 128), 128)


def rows_of(meta, mine):
    side = meta[8] if mine else 1 - meta[8]
    return pl.ds(pl.multiple_of(side * 128, 128), 128)


def dot(a, b):
    return jnp.dot(a, b, preferred_element_type=f32)


def dot_nt(a, b):
    return lax.dot_general(a, b, (((1,), (1,)), ((), ())), preferred_element_type=f32)


def dot_tn(a, b):
    return lax.dot_general(a, b, (((0,), (0,)), ((), ())), preferred_element_type=f32)


def norm_stats(values):
    average = jnp.mean(values, axis=-1, keepdims=True)
    centered = values - average
    variance = jnp.mean(centered * centered, axis=-1, keepdims=True)
    inverse = lax.rsqrt(variance + epsilon)
    return centered * inverse, inverse


def pack_kernel(meta, attend, merge, gains, shifts, bias, seg, out):
    for t in range(3):
        out[t * 128 : t * 128 + 128, :] = attend[t]
    out[384:512, :] = merge[...]
    zero = jnp.zeros((1, 128), f32)
    low, high, ids = gains[...].astype(f32), shifts[...].astype(f32), seg[...].astype(f32)
    tail = [
        jnp.concatenate([low[0:1], low[1:2]], axis=1),
        jnp.concatenate([high[0:1], high[1:2]], axis=1),
        jnp.concatenate([bias[...].astype(f32), zero], axis=1),
        jnp.concatenate([ids[0:1], ids[1:2]], axis=1),
        jnp.zeros((12, 256), f32),
    ]
    out[512:528, :] = jnp.concatenate(tail, axis=0).astype(bf16)


def norm_half_kernel(meta, x, out):
    normed, _ = norm_stats(x[rows_of(meta, True), :])
    out[...] = normed.astype(bf16)


def qkv_kernel(meta, x, far_a, far_b, *refs):
    blocks = refs[:9]
    (hidden, hidden_far, query, key_value, key_value_far, attend, merge, small, seg_far,
     seg_all) = refs[9:]

    def piece(offset, start, size):
        if offset < 4:
            return blocks[offset][start : start + size, :]
        if offset == 4:
            return jnp.concatenate(
                [blocks[4][start : start + size, :], blocks[5][start : start + size, :]], axis=1
            )
        return blocks[offset + 1][start : start + size, :]

    small[...] = jnp.zeros_like(small)
    for j in range(RING):
        at = columns(meta, j)
        for t in range(3):
            attend[t, at, :] = piece(j, t * 128, 128)
        merge[at, :] = piece(j, 384, 128)
        tail = piece(j, 512, 16).astype(f32)
        small[0:1, at] = tail[0:1, :128]
        small[1:2, at] = tail[0:1, 128:]
        small[2:3, at] = tail[1:2, :128]
        small[3:4, at] = tail[1:2, 128:]
        small[4:5, at] = tail[2:3, :128]
        seg_all[pl.ds(meta[j], 1), :] = tail[3:4, :]
    ids = seg_all[pl.ds(2 * meta[10], 1), :]
    seg_far[0:1, :] = ids[:, :128].astype(jnp.int32)
    seg_far[1:2, :] = ids[:, 128:].astype(jnp.int32)
    gain, shift = small[0:1, :], small[2:3, :]
    normed, _ = norm_stats(x[...])
    hidden[...] = (normed * gain + shift).astype(bf16)
    hidden_far[rows_of(meta, True), :] = (far_a[...].astype(f32) * gain + shift).astype(bf16)
    hidden_far[rows_of(meta, False), :] = (far_b[...].astype(f32) * gain + shift).astype(bf16)
    both, other = hidden[...], hidden_far[...]
    key_value[:, :256] = dot(both, attend[1]).astype(bf16)
    key_value[:, 256:] = dot(both, attend[2]).astype(bf16)
    key_value_far[:, :256] = dot(other, attend[1]).astype(bf16)
    key_value_far[:, 256:] = dot(other, attend[2]).astype(bf16)
    query[...] = (dot(both, attend[0]) * (HD**-0.5)).astype(bf16)


def masks(meta, seg, seg_col, seg_far, s):
    col = seg_col[:, s : s + 1]
    near = col == seg[s : s + 1, :]
    i = lax.broadcasted_iota(jnp.int32, (128, 128), 0)
    j = lax.broadcasted_iota(jnp.int32, (128, 128), 1)
    far = (col == seg_far[s : s + 1, :]) & (meta[9] == 1)
    return near & (j <= i), far


def head_probs(query, key, key_far, near, far):
    score = jnp.where(near, dot_nt(query, key), masked_score)
    score_far = jnp.where(far, dot_nt(query, key_far), masked_score)
    top = jnp.maximum(
        jnp.max(score, axis=-1, keepdims=True), jnp.max(score_far, axis=-1, keepdims=True)
    )
    total = jnp.sum(jnp.exp(score - top), axis=-1, keepdims=True) + jnp.sum(
        jnp.exp(score_far - top), axis=-1, keepdims=True
    )
    log_total = top + jnp.log(total)
    return jnp.exp(score - log_total), jnp.exp(score_far - log_total)


def attention_kernel(
    meta, query, kv, kv_far, seg, seg_col, seg_far, merge, attended, keep, give, part
):
    for s in range(2):
        near, far = masks(meta, seg, seg_col, seg_far, s)
        r = slice(s * 128, s * 128 + 128)
        for h in range(4):
            c = slice(h * 64, h * 64 + 64)
            v = slice(256 + h * 64, 256 + h * 64 + 64)
            probs, probs_far = head_probs(query[r, c], kv[r, c], kv_far[r, c], near, far)
            out = dot(probs.astype(bf16), kv[r, v]) + dot(probs_far.astype(bf16), kv_far[r, v])
            attended[r, c] = out.astype(bf16)
    part[...] = dot_nt(attended[...], merge[...])
    keep[...] = part[rows_of(meta, True), :]
    give[...] = part[rows_of(meta, False), :].astype(bf16)


def total_of(meta, sums, full):
    pair, far, pair_other, far_other = sums
    full[rows_of(meta, True), :] = pair[...].astype(f32) + far[...].astype(f32)
    full[rows_of(meta, False), :] = pair_other[...].astype(f32) + far_other[...].astype(f32)
    return full[...]


def assemble(meta, blocks, full):
    for j in range(RING):
        at = columns(meta, j)
        if j == 4:
            start = pl.multiple_of(meta[4] * 128, 128)
            full[pl.ds(start, 64), :] = blocks[4][...]
            full[pl.ds(pl.multiple_of(start + 64, 64), 64), :] = blocks[5][...]
        else:
            full[at, :] = (blocks[j] if j < 4 else blocks[j + 1])[...]


def store_parts(meta, left, right, outs):
    for j in range(RING):
        value = dot_tn(left[:, columns(meta, j)], right[...]).astype(bf16)
        if j == 4:
            outs[4][...] = value[:64]
            outs[5][...] = value[64:]
        else:
            (outs[j] if j < 4 else outs[j + 1])[...] = value


def ffn_first_kernel(meta, x, cot, small, s0, s1, s2, s3, *refs):
    blocks = refs[:9]
    residual, hidden, cot_half, act, slope, expand = refs[9:15]
    outs, part = refs[15:24], refs[24]
    assemble(meta, blocks, expand)
    residual[...] = x[...] + total_of(meta, (s0, s1, s2, s3), part)
    normed, _ = norm_stats(residual[...])
    hidden[...] = (normed * small[1:2, :] + small[3:4, :]).astype(bf16)
    cot_half[...] = cot[...].astype(bf16)

    def units(i, carry):
        at = pl.ds(pl.multiple_of(i * 256, 256), 256)
        pre_act = dot(hidden[...], expand[:, at]) + small[4:5, at]
        value, gradient = gelu_pair(pre_act)
        act[:, at] = value.astype(bf16)
        slope[:, at] = gradient
        return carry

    lax.fori_loop(0, 4, units, 0)
    store_parts(meta, cot_half, act, outs)


def ffn_second_kernel(meta, residual, cot_half, act, slope, expand, *refs):
    blocks = refs[:9]
    pre_half, later_keep, later_give, red_keep, red_give, grads, reduce, part = refs[9:]
    assemble(meta, blocks, reduce)
    grads[...] = jnp.zeros_like(grads)

    def units(i, carry):
        at = pl.ds(pl.multiple_of(i * 256, 256), 256)
        pre_grad = dot(cot_half[...], reduce[:, at]) * slope[:, at]
        pre_half[:, at] = pre_grad.astype(bf16)
        grads[2:3, at] = jnp.sum(pre_grad, axis=0, keepdims=True)
        return carry

    lax.fori_loop(0, 4, units, 0)

    def later(i, carry):
        at = pl.ds(pl.multiple_of(i * 256, 256), 256)
        part[:, at] = dot_nt(pre_half[...], expand[at, :])
        return carry

    lax.fori_loop(0, 4, later, 0)
    later_keep[...] = part[rows_of(meta, True), :]
    later_give[...] = part[rows_of(meta, False), :].astype(bf16)
    normed, _ = norm_stats(residual[...])
    grads[0:1, :] = jnp.sum(part[...] * normed, axis=0, keepdims=True)
    grads[1:2, :] = jnp.sum(part[...], axis=0, keepdims=True)

    def reduced(i, carry):
        at = pl.ds(pl.multiple_of(i * 256, 256), 256)
        part[:, at] = dot_nt(act[...], reduce[at, :])
        return carry

    lax.fori_loop(0, 4, reduced, 0)
    red_keep[...] = part[rows_of(meta, True), :]
    red_give[...] = part[rows_of(meta, False), :].astype(bf16)


def expand_grads_kernel(meta, hidden, pre_half, *outs):
    store_parts(meta, hidden, pre_half, outs)


def attention_back_kernel(
    meta, cot, residual, small, s0, s1, s2, s3, merge, query, kv, kv_far, attended,
    seg, seg_col, seg_far, residual_grad, resid_half, query_grad, kv_grad, kv_grad_far,
    part, att_grad
):
    later_grad = total_of(meta, (s0, s1, s2, s3), part)
    normed, inverse = norm_stats(residual[...])
    residual_grad[...] = cot[...] + norm_backward(later_grad, normed, inverse, small[1:2, :])
    resid_half[...] = residual_grad[...].astype(bf16)
    att_grad[...] = dot(resid_half[...], merge[...]).astype(bf16)
    for s in range(2):
        near, far = masks(meta, seg, seg_col, seg_far, s)
        r = slice(s * 128, s * 128 + 128)
        for h in range(4):
            c = slice(h * 64, h * 64 + 64)
            v = slice(256 + h * 64, 256 + h * 64 + 64)
            q, k, k_far = query[r, c], kv[r, c], kv_far[r, c]
            probs, probs_far = head_probs(q, k, k_far, near, far)
            up = att_grad[r, c]
            delta = jnp.sum(up.astype(f32) * attended[r, c].astype(f32), axis=-1, keepdims=True)
            score = (probs * (dot_nt(up, kv[r, v]) - delta)).astype(bf16)
            score_far = (probs_far * (dot_nt(up, kv_far[r, v]) - delta)).astype(bf16)
            query_grad[r, c] = (dot(score, k) + dot(score_far, k_far)) * (HD**-0.5)
            kv_grad[r, c] = dot_tn(score, q)
            kv_grad[r, v] = dot_tn(probs.astype(bf16), up)
            kv_grad_far[r, c] = dot_tn(score_far, q).astype(bf16)
            kv_grad_far[r, v] = dot_tn(probs_far.astype(bf16), up).astype(bf16)


def attention_grads_kernel(
    meta, x, far_a, far_b, hidden, hidden_far, query_grad, kv_grad, kv_grad_far, resid_half,
    attended, attend, grads, early, *refs
):
    outs, proj, sums, part = refs[:9], refs[9], refs[10], refs[11]
    proj[:, :256] = query_grad[...].astype(bf16)
    proj[:, 256:] = kv_grad[...].astype(bf16)
    early[...] = (
        dot_nt(proj[:, :256], attend[0])
        + dot_nt(proj[:, 256:512], attend[1])
        + dot_nt(proj[:, 512:], attend[2])
    )
    part[...] = dot_nt(kv_grad_far[:, :256], attend[1]) + dot_nt(kv_grad_far[:, 256:], attend[2])
    normed, _ = norm_stats(x[...])
    mine, other = part[rows_of(meta, True), :], part[rows_of(meta, False), :]
    sums[0:1, :] = (
        jnp.sum(early[...] * normed, axis=0, keepdims=True)
        + jnp.sum(mine * far_a[...].astype(f32), axis=0, keepdims=True)
        + jnp.sum(other * far_b[...].astype(f32), axis=0, keepdims=True)
    )
    sums[1:2, :] = jnp.sum(early[...] + part[...], axis=0, keepdims=True)
    for j in range(RING):
        at = columns(meta, j)
        lhs, lhs_far = hidden[:, at], hidden_far[:, at]
        pieces = [dot_tn(lhs, proj[:, :256]).astype(bf16)]
        for t in (1, 2):
            c, c_far = slice(t * 256, t * 256 + 256), slice(t * 256 - 256, t * 256)
            pieces.append((dot_tn(lhs, proj[:, c]) + dot_tn(lhs_far, kv_grad_far[:, c_far])).astype(bf16))
        pieces.append(dot_tn(resid_half[:, at], attended[...]).astype(bf16))
        zero = jnp.zeros((1, 128), f32)
        tail = jnp.concatenate(
            [
                jnp.concatenate([sums[0:1, at], grads[0:1, at]], axis=1),
                jnp.concatenate([sums[1:2, at], grads[1:2, at]], axis=1),
                jnp.concatenate([grads[2:3, at], zero], axis=1),
                jnp.zeros((13, 256), f32),
            ],
            axis=0,
        )
        pieces.append(tail.astype(bf16))
        start = 0
        for value in pieces:
            span = slice(start, start + value.shape[0])
            start += value.shape[0]
            if j == 4:
                outs[4][span, :] = value[:, :128]
                outs[5][span, :] = value[:, 128:]
            else:
                out = outs[j] if j < 4 else outs[j + 1]
                out[span, :] = value


def project_back_kernel(meta, early, kv_grad_in, attend, keep, give, part):
    part[...] = (
        early[...]
        + dot_nt(kv_grad_in[:, :256], attend[1])
        + dot_nt(kv_grad_in[:, 256:], attend[2])
    )
    keep[...] = part[rows_of(meta, True), :]
    give[...] = part[rows_of(meta, False), :].astype(bf16)


def first_rows_kernel(meta, up, down, ahead, behind, up_out, down_out):
    up_out[:64, :] = (up[:64, :].astype(f32) + ahead[...].astype(f32)).astype(bf16)
    up_out[64:, :] = up[64:, :]
    down_out[:64, :] = down[:64, :]
    down_out[64:, :] = (down[64:, :].astype(f32) + behind[...].astype(f32)).astype(bf16)


def first_columns_kernel(meta, up, down, ahead, behind, up_out, down_out):
    up_out[:, :128] = (up[:, :128].astype(f32) + ahead[...].astype(f32)).astype(bf16)
    up_out[:, 128:] = up[:, 128:]
    down_out[:, :128] = down[:, :128]
    down_out[:, 128:] = (down[:, 128:].astype(f32) + behind[...].astype(f32)).astype(bf16)


def step_kernel(meta, up, down, ahead, behind, up_out, down_out):
    up_out[...] = (up[...].astype(f32) + ahead[...].astype(f32)).astype(bf16)
    down_out[...] = (down[...].astype(f32) + behind[...].astype(f32)).astype(bf16)


def last_kernel(meta, own, ahead, behind, out):
    out[...] = own[...].astype(f32) + (ahead[...].astype(f32) + behind[...].astype(f32))


def last_pack_kernel(meta, own, ahead, behind, attend, merge, tail):
    def total(start, size):
        r = slice(start, start + size)
        return own[r, :].astype(f32) + (ahead[r, :].astype(f32) + behind[r, :].astype(f32))

    for t in range(3):
        attend[t] = total(t * 128, 128)
    merge[...] = total(384, 128)
    tail[...] = total(512, 16)


def block_out_kernel(meta, residual, s0, s1, s2, s3, out, part):
    out[...] = residual[...] + total_of(meta, (s0, s1, s2, s3), part)


def input_grad_kernel(meta, x, residual_grad, small, s0, s1, s2, s3, out, part):
    early_grad = total_of(meta, (s0, s1, s2, s3), part)
    normed, inverse = norm_stats(x[...])
    out[...] = residual_grad[...] + norm_backward(early_grad, normed, inverse, small[0:1, :])


def send_ahead(value):
    return lax.ppermute(value, AXES, AHEAD)


def send_behind(value):
    return lax.ppermute(value, AXES, BEHIND)


def gather_blocks(own, first, second):
    blocks = [own] + [None] * 8
    ahead, behind = own, own
    for step in range(1, 4):
        ahead = send_ahead(ahead)
        behind = send_behind(behind)
        blocks[9 - step], blocks[step] = ahead, behind
    blocks[4] = send_ahead(first(ahead))
    blocks[5] = send_behind(second(behind))
    return blocks


def sum_blocks(meta, parts, first, last, last_shapes):
    ahead = send_ahead(parts[4])
    behind = send_behind(parts[5])
    for step in range(3, 0, -1):
        up, down = call(
            first if step == 3 else step_kernel, [shape(parts[1].shape, bf16)] * 2,
            [meta, parts[step], parts[9 - step], ahead, behind], 1_000_000,
        )
        ahead = send_ahead(up)
        behind = send_behind(down)
    return call(last, last_shapes, [meta, parts[0], ahead, behind], 1_000_000)


def tp_send(pairs):
    return lambda value: lax.ppermute(value, TP, pairs)


def tp_exchange(keep, give):
    near = tp_send(NEAR)(give)
    pair = (keep + near.astype(f32)).astype(bf16)
    far = tp_send(FAR)(pair)
    pair_other = tp_send(NEAR)(pair)
    return pair, far, pair_other, tp_send(NEAR)(far)


def fast_shards(
    inputs, segment_ids, gains, shifts, attend_weight, merge_weight, expand_weight,
    expand_bias, reduce_weight, cotangent,
):
    shard, ctx = lax.axis_index(AXES[0]), lax.axis_index(CTX)
    place = jnp.where(ctx == 0, shard, RING - 1 - shard)
    spots = lax.rem(place + jnp.arange(RING, dtype=jnp.int32), RING)
    owners = jnp.where(spots < 4, 2 * spots, 2 * (7 - spots) + 1)
    side = lax.rem(lax.axis_index(TP), 2)
    meta = jnp.concatenate([owners, jnp.stack([side, ctx, shard])]).astype(jnp.int32)

    x = inputs.reshape(256, 1024)
    cot = cotangent.reshape(256, 1024)
    rows, half, square = (256, 1024), (128, 1024), (256, 256)
    part = pltpu.VMEM(rows, f32)
    (pack,) = call(
        pack_kernel, [shape((528, 256), bf16)],
        [meta, jnp.swapaxes(attend_weight, 0, 1), merge_weight, gains, shifts, expand_bias,
         segment_ids], 1_000_000,
    )
    blocks = gather_blocks(pack, lambda v: v[:, :128], lambda v: v[:, 128:])
    (normed_half,) = call(norm_half_kernel, [shape(half, bf16)], [meta, x], 1_000_000)
    far_a = lax.ppermute(normed_half, CTX, [(0, 1)])
    far_b = lax.ppermute(far_a, TP, NEAR)
    seg_col = segment_ids.T
    expand_weight, _ = lax.optimization_barrier((expand_weight, blocks[EXPAND_AFTER]))
    expand_blocks = gather_blocks(expand_weight, lambda v: v[:64], lambda v: v[64:])
    reduce_weight, _ = lax.optimization_barrier((reduce_weight, blocks[REDUCE_AFTER]))
    reduce_blocks = gather_blocks(reduce_weight, lambda v: v[:64], lambda v: v[64:])

    hidden_early, hidden_far, query, kv, kv_far, attend, merge, small, seg_far = call(
        qkv_kernel,
        [shape(rows, bf16), shape(rows, bf16), shape(square, bf16), shape((256, 512), bf16),
         shape((256, 512), bf16), shape((3, 1024, 256), bf16), shape((1024, 256), bf16),
         shape((8, 1024), f32), shape((2, 128), jnp.int32)],
        [meta, x, far_a, far_b] + blocks, 700_000_000, [pltpu.VMEM((8, 256), f32)],
    )
    attended, keep, give = call(
        attention_kernel,
        [shape(square, bf16), shape(half, f32), shape(half, bf16)],
        [meta, query, kv, kv_far, segment_ids, seg_col, seg_far, merge],
        300_000_000, [part], 800_000,
    )
    part_shapes = [shape(half, bf16)] * 9
    part_shapes[4] = part_shapes[5] = shape((64, 1024), bf16)
    residual, hidden_later, cot_half, act, slope, expand, *reduce_parts = call(
        ffn_first_kernel,
        [shape(rows, f32)] + [shape(rows, bf16)] * 3 + [shape(rows, f32)]
        + [shape((1024, 1024), bf16)] + part_shapes,
        [meta, x, cot, small, *tp_exchange(keep, give)] + expand_blocks,
        1_100_000_000, [part], 300_000,
    )
    pre_half, later_keep, later_give, red_keep, red_give, grads = call(
        ffn_second_kernel,
        [shape(rows, bf16)] + [shape(half, f32), shape(half, bf16)] * 2 + [shape((8, 1024), f32)],
        [meta, residual, cot_half, act, slope, expand] + reduce_blocks,
        1_600_000_000, [pltpu.VMEM((1024, 1024), bf16), part],
    )
    (reduce_grad,) = sum_blocks(
        meta, reduce_parts, first_rows_kernel, last_kernel, [shape(half, f32)]
    )
    later_sums = tp_exchange(later_keep, later_give)
    expand_parts = call(
        expand_grads_kernel, part_shapes,
        [meta, hidden_later, pre_half], 550_000_000,
    )
    (expand_grad,) = sum_blocks(
        meta, expand_parts, first_rows_kernel, last_kernel, [shape(half, f32)]
    )
    residual_grad, resid_half, query_grad, kv_grad, kv_grad_far = call(
        attention_back_kernel,
        [shape(rows, f32), shape(rows, bf16), shape(square, f32), shape((256, 512), f32),
         shape((256, 512), bf16)],
        [meta, cot, residual, small, *later_sums, merge, query, kv, kv_far, attended,
         segment_ids, seg_col, seg_far],
        500_000_000, [part, pltpu.VMEM(square, bf16)], 800_000,
    )
    kv_grad_in = lax.ppermute(kv_grad_far, CTX, [(1, 0)])
    pack_shapes = [shape((528, 256), bf16)] * 9
    pack_shapes[4] = pack_shapes[5] = shape((528, 128), bf16)
    early, *pack_parts = call(
        attention_grads_kernel, [shape(rows, f32)] + pack_shapes,
        [meta, x, far_a, far_b, hidden_early, hidden_far, query_grad, kv_grad, kv_grad_far,
         resid_half, attended, attend, grads], 1_100_000_000,
        [pltpu.VMEM((256, 768), bf16), pltpu.VMEM((8, 1024), f32), part],
    )
    attend_grad, merge_grad, tail = sum_blocks(
        meta, pack_parts, first_columns_kernel, last_pack_kernel,
        [shape((3, 128, 256), f32), shape((128, 256), f32), shape((16, 256), f32)],
    )
    early_keep, early_give = call(
        project_back_kernel, [shape(half, f32), shape(half, bf16)],
        [meta, early, kv_grad_in, attend], 300_000_000, [part],
    )
    early_sums = tp_exchange(early_keep, early_give)
    red_keep, red_give, _ = lax.optimization_barrier((red_keep, red_give, query_grad))
    (block_out,) = call(
        block_out_kernel, [shape(rows, f32)],
        [meta, residual, *tp_exchange(red_keep, red_give)], 1_000_000, [part],
    )
    (input_grad,) = call(
        input_grad_kernel, [shape(rows, f32)],
        [meta, x, residual_grad, small, *early_sums], 5_000_000, [part],
    )
    norms = tail[:2]
    norms = norms + lax.ppermute(norms, TP, NEAR)
    norms = norms + lax.ppermute(norms, TP, FAR)
    return (
        block_out.reshape(inputs.shape),
        input_grad.reshape(inputs.shape),
        norms[0].reshape(2, 128),
        norms[1].reshape(2, 128),
        jnp.swapaxes(attend_grad, 0, 1),
        merge_grad,
        expand_grad,
        tail[2:3, :128],
        reduce_grad,
    )


EXPAND_AFTER = 0
REDUCE_AFTER = 2


def fits(mesh_sizes, *args):
    shapes = tuple(a.shape for a in args)
    return mesh_sizes == (4, 2, 4) and shapes == (
        (2, 128, 1024), (2, 128), (2, 128), (2, 128), (128, 3, 256), (128, 256),
        (128, 1024), (1, 128), (128, 1024), (2, 128, 1024),
    )


def either(*args):
    sizes = tuple(lax.axis_size(name) for name in (*AXES, TP))
    if not fits(sizes, *args):
        return shards(*args)
    return fast_shards(*args)


def solution(mesh):
    in_specs = (
        P("shard", "ctx", None),
        P("shard", "ctx"),
        P(None, ("shard", "ctx")),
        P(None, ("shard", "ctx")),
        P(("shard", "ctx"), None, "tp"),
        P(("shard", "ctx"), "tp"),
        P(("shard", "ctx"), "tp"),
        P("tp", ("shard", "ctx")),
        P(("shard", "ctx"), "tp"),
        P("shard", "ctx", None),
    )
    out_specs = (
        P("shard", "ctx", None),
        P("shard", "ctx", None),
        P(None, ("shard", "ctx")),
        P(None, ("shard", "ctx")),
        P(("shard", "ctx"), None, "tp"),
        P(("shard", "ctx"), "tp"),
        P(("shard", "ctx"), "tp"),
        P("tp", ("shard", "ctx")),
        P(("shard", "ctx"), "tp"),
    )
    return jax.shard_map(either, mesh=mesh, in_specs=in_specs, out_specs=out_specs, check_vma=False)
```

```python
import math

import jax
import jax.numpy as jnp
from jax import lax
from jax.experimental import pallas as pl
from jax.experimental.pallas import tpu as pltpu
from jax.sharding import PartitionSpec as P

HD = 64


epsilon = 1e-05
masked_score = -1e30
gelu_scale = 0.7978845608028654
gelu_cubic = 0.044715


def norm_forward(values, gain, shift):
    average = jnp.mean(values, axis=-1, keepdims=True)
    centered = values - average
    variance = jnp.mean(centered * centered, axis=-1, keepdims=True)
    inverse = lax.rsqrt(variance + epsilon)
    normed = centered * inverse
    return (normed, inverse, normed * gain.astype(jnp.float32) + shift.astype(jnp.float32))


def norm_backward(upstream, normed, inverse, gain):
    scaled = upstream * gain.astype(jnp.float32)
    first_mean = jnp.mean(scaled, axis=-1, keepdims=True)
    second_mean = jnp.mean(scaled * normed, axis=-1, keepdims=True)
    return inverse * (scaled - first_mean - normed * second_mean)


def gelu_pair(pre_act):
    inner_arg = gelu_scale * (pre_act + gelu_cubic * pre_act * pre_act * pre_act)
    tangent = jnp.tanh(inner_arg)
    gelu_value = 0.5 * pre_act * (1.0 + tangent)
    gelu_slope = 0.5 * (1.0 + tangent) + 0.5 * pre_act * (1.0 - tangent * tangent) * gelu_scale * (
        1.0 + 3.0 * gelu_cubic * pre_act * pre_act
    )
    return (gelu_value, gelu_slope)


def shards(
    inputs,
    segment_ids,
    gains,
    shifts,
    attend_weight,
    merge_weight,
    expand_weight,
    expand_bias,
    reduce_weight,
    cotangent,
):
    seq_count, group_len, model_width = inputs.shape
    row_count = seq_count * group_len
    full_len = group_len * lax.axis_size("ctx")
    head_scale = HD ** (-0.5)
    gathered = (
        lax.all_gather(attend_weight, ("shard", "ctx"), axis=0, tiled=True),
        lax.all_gather(merge_weight, ("shard", "ctx"), axis=0, tiled=True),
        lax.all_gather(expand_weight, ("shard", "ctx"), axis=0, tiled=True),
        lax.all_gather(reduce_weight, ("shard", "ctx"), axis=0, tiled=True),
        lax.all_gather(expand_bias, ("shard", "ctx"), axis=1, tiled=True),
        lax.all_gather(gains, ("shard", "ctx"), axis=1, tiled=True),
        lax.all_gather(shifts, ("shard", "ctx"), axis=1, tiled=True),
    )
    attend_full, merge_full, expand_full, reduce_full, bias_full, gains_full, shifts_full = gathered
    local_cols = attend_full.shape[2]
    head_local = local_cols // HD
    flat_in = inputs.reshape(row_count, model_width)
    normed_early, inverse_early, affine_early = norm_forward(flat_in, gains_full[0], shifts_full[0])
    hidden_early = affine_early.astype(jnp.bfloat16)
    projected = jnp.einsum(
        "rd,dtc->rtc", hidden_early, attend_full, preferred_element_type=jnp.float32
    )
    query_heads = (
        (projected[:, 0] * head_scale)
        .astype(jnp.bfloat16)
        .reshape(seq_count, group_len, head_local, HD)
    )
    key_rows = projected[:, 1].astype(jnp.bfloat16).reshape(seq_count, group_len, local_cols)
    value_rows = projected[:, 2].astype(jnp.bfloat16).reshape(seq_count, group_len, local_cols)
    all_keys, all_values, all_segments = (
        lax.all_gather(key_rows, "ctx", axis=1, tiled=True),
        lax.all_gather(value_rows, "ctx", axis=1, tiled=True),
        lax.all_gather(segment_ids, "ctx", axis=1, tiled=True),
    )
    key_heads = all_keys.reshape(seq_count, full_len, head_local, HD)
    value_heads = all_values.reshape(seq_count, full_len, head_local, HD)
    query_pos = lax.axis_index("ctx") * group_len + jnp.arange(group_len, dtype=jnp.int32)
    key_pos = jnp.arange(full_len, dtype=jnp.int32)
    allowed = (segment_ids[:, :, None] == all_segments[:, None, :]) & (
        key_pos[None, None, :] <= query_pos[None, :, None]
    )
    allowed = allowed[:, None]

    def score_block():
        raw_scores = jnp.einsum(
            "sqhd,skhd->shqk", query_heads, key_heads, preferred_element_type=jnp.float32
        )
        return jnp.where(allowed, raw_scores, masked_score)

    scores = score_block()
    row_top = jnp.max(scores, axis=-1, keepdims=True)
    log_total = row_top + jnp.log(jnp.sum(jnp.exp(scores - row_top), axis=-1, keepdims=True))
    attn_probs = jnp.exp(scores - log_total)
    probs_half = attn_probs.astype(jnp.bfloat16)
    attended_heads = jnp.einsum(
        "shqk,skhd->sqhd", probs_half, value_heads, preferred_element_type=jnp.float32
    ).astype(jnp.bfloat16)
    attended = attended_heads.reshape(row_count, local_cols)
    merge_part = jnp.einsum("rc,oc->ro", attended, merge_full, preferred_element_type=jnp.float32)
    residual = flat_in + lax.psum(merge_part, "tp")
    normed_later, inverse_later, affine_later = norm_forward(
        residual, gains_full[1], shifts_full[1]
    )
    hidden_later = affine_later.astype(jnp.bfloat16)
    pre_act = jnp.dot(
        hidden_later, expand_full, preferred_element_type=jnp.float32
    ) + bias_full.astype(jnp.float32)
    gelu_value, gelu_slope = gelu_pair(pre_act)
    activated = gelu_value.astype(jnp.bfloat16)
    reduce_part = jnp.einsum(
        "rf,of->ro", activated, reduce_full, preferred_element_type=jnp.float32
    )
    block_out = residual + lax.psum(reduce_part.astype(jnp.bfloat16), "tp").astype(jnp.float32)
    back_set = (
        lax.all_gather(attend_weight, ("shard", "ctx"), axis=0, tiled=True),
        lax.all_gather(merge_weight, ("shard", "ctx"), axis=0, tiled=True),
        lax.all_gather(expand_weight, ("shard", "ctx"), axis=0, tiled=True),
        lax.all_gather(reduce_weight, ("shard", "ctx"), axis=0, tiled=True),
        lax.all_gather(gains, ("shard", "ctx"), axis=1, tiled=True),
    )
    attend_back, merge_back, expand_back, reduce_back, gains_back = back_set
    output_grad = cotangent.reshape(row_count, model_width)
    cot_half = output_grad.astype(jnp.bfloat16)
    reduce_grad = jnp.einsum("ro,rf->of", cot_half, activated, preferred_element_type=jnp.float32)
    pre_grad = jnp.dot(cot_half, reduce_back, preferred_element_type=jnp.float32) * gelu_slope
    pre_half = pre_grad.astype(jnp.bfloat16)
    bias_grad = jnp.sum(pre_grad, axis=0, keepdims=True)
    expand_grad = jnp.einsum(
        "rd,rf->df", hidden_later, pre_half, preferred_element_type=jnp.float32
    )
    later_part = jnp.einsum("rf,df->rd", pre_half, expand_back, preferred_element_type=jnp.float32)
    later_grad = lax.psum(later_part, "tp")
    residual_grad = output_grad + norm_backward(
        later_grad, normed_later, inverse_later, gains_back[1]
    )
    resid_half = residual_grad.astype(jnp.bfloat16)
    merge_grad = jnp.einsum("ro,rc->oc", resid_half, attended, preferred_element_type=jnp.float32)
    attended_grad = jnp.dot(resid_half, merge_back, preferred_element_type=jnp.float32).astype(
        jnp.bfloat16
    )
    grad_heads = attended_grad.reshape(seq_count, group_len, head_local, HD)
    scores_again = score_block()
    probs_again = jnp.exp(scores_again - log_total)
    probs_again_half = probs_again.astype(jnp.bfloat16)
    row_delta = jnp.einsum(
        "sqhd,sqhd->shq", grad_heads, attended_heads, preferred_element_type=jnp.float32
    )
    prob_grad = jnp.einsum(
        "sqhd,skhd->shqk", grad_heads, value_heads, preferred_element_type=jnp.float32
    )
    score_grad = probs_again * (prob_grad - row_delta[..., None])
    score_half = score_grad.astype(jnp.bfloat16)
    query_grad = (
        jnp.einsum("shqk,skhd->sqhd", score_half, key_heads, preferred_element_type=jnp.float32)
        * head_scale
    )
    keys_part = jnp.einsum(
        "shqk,sqhd->skhd", score_half, query_heads, preferred_element_type=jnp.float32
    ).reshape(seq_count, full_len, local_cols)
    values_part = jnp.einsum(
        "shqk,sqhd->skhd", probs_again_half, grad_heads, preferred_element_type=jnp.float32
    ).reshape(seq_count, full_len, local_cols)
    keys_grad, values_grad = (
        lax.psum_scatter(keys_part, "ctx", scatter_dimension=1, tiled=True),
        lax.psum_scatter(values_part, "ctx", scatter_dimension=1, tiled=True),
    )
    proj_grad = jnp.stack(
        [
            query_grad.reshape(row_count, local_cols),
            keys_grad.reshape(row_count, local_cols),
            values_grad.reshape(row_count, local_cols),
        ],
        axis=1,
    ).astype(jnp.bfloat16)
    attend_grad = jnp.einsum(
        "rd,rtc->dtc", hidden_early, proj_grad, preferred_element_type=jnp.float32
    )
    early_part = jnp.einsum(
        "rtc,dtc->rd", proj_grad, attend_back, preferred_element_type=jnp.float32
    )
    early_grad = lax.psum(early_part, "tp")
    input_grad = residual_grad + norm_backward(
        early_grad, normed_early, inverse_early, gains_back[0]
    )
    gains_grad = jnp.stack(
        [jnp.sum(early_grad * normed_early, axis=0), jnp.sum(later_grad * normed_later, axis=0)]
    )
    shifts_grad = jnp.stack([jnp.sum(early_grad, axis=0), jnp.sum(later_grad, axis=0)])
    shares = (
        lax.psum_scatter(attend_grad, ("shard", "ctx"), scatter_dimension=0, tiled=True),
        lax.psum_scatter(merge_grad, ("shard", "ctx"), scatter_dimension=0, tiled=True),
        lax.psum_scatter(expand_grad, ("shard", "ctx"), scatter_dimension=0, tiled=True),
        lax.psum_scatter(reduce_grad, ("shard", "ctx"), scatter_dimension=0, tiled=True),
        lax.psum_scatter(bias_grad, ("shard", "ctx"), scatter_dimension=1, tiled=True),
        lax.psum_scatter(gains_grad, ("shard", "ctx"), scatter_dimension=1, tiled=True),
        lax.psum_scatter(shifts_grad, ("shard", "ctx"), scatter_dimension=1, tiled=True),
    )
    return (
        block_out.reshape(inputs.shape),
        input_grad.reshape(inputs.shape),
        shares[5],
        shares[6],
        shares[0],
        shares[1],
        shares[2],
        shares[4],
        shares[3],
    )


VMEM = pl.BlockSpec(memory_space=pltpu.VMEM)
SMEM = pl.BlockSpec(memory_space=pltpu.SMEM)
f32 = jnp.float32
bf16 = jnp.bfloat16
RING = 8
ROOM = 6 << 20
NEAR = [(0, 1), (1, 0), (2, 3), (3, 2)]
FAR = [(0, 2), (2, 0), (1, 3), (3, 1)]
AXES = ("shard", "ctx")
TP = "tp"
CTX = "ctx"
IDS = [2 * p if p < 4 else 2 * (7 - p) + 1 for p in range(RING)]
AHEAD = [(IDS[p], IDS[(p + 1) % RING]) for p in range(RING)]
BEHIND = [(IDS[p], IDS[(p - 1) % RING]) for p in range(RING)]


def shape(dims, dtype):
    return jax.ShapeDtypeStruct(dims, dtype)


def call(kernel, outs, args, flops, scratch=(), transcendentals=0):
    nbytes = sum(a.size * a.dtype.itemsize for a in list(args) + list(outs))
    held = sum(math.prod(a.shape) * jnp.dtype(a.dtype).itemsize for a in scratch)
    return pl.pallas_call(
        kernel,
        out_shape=tuple(outs),
        in_specs=[SMEM] + [VMEM] * (len(args) - 1),
        out_specs=tuple(VMEM for _ in outs),
        scratch_shapes=list(scratch),
        compiler_params=pltpu.CompilerParams(vmem_limit_bytes=nbytes + held + ROOM),
        cost_estimate=pl.CostEstimate(
            flops=flops, bytes_accessed=nbytes, transcendentals=transcendentals
        ),
    )(*args)


def columns(meta, offset):
    return pl.ds(pl.multiple_of(meta[offset] * 128, 128), 128)


def rows_of(meta, mine):
    side = meta[8] if mine else 1 - meta[8]
    return pl.ds(pl.multiple_of(side * 128, 128), 128)


def dot(a, b):
    return jnp.dot(a, b, preferred_element_type=f32)


def dot_nt(a, b):
    return lax.dot_general(a, b, (((1,), (1,)), ((), ())), preferred_element_type=f32)


def dot_tn(a, b):
    return lax.dot_general(a, b, (((0,), (0,)), ((), ())), preferred_element_type=f32)


def norm_stats(values):
    average = jnp.mean(values, axis=-1, keepdims=True)
    centered = values - average
    variance = jnp.mean(centered * centered, axis=-1, keepdims=True)
    inverse = lax.rsqrt(variance + epsilon)
    return centered * inverse, inverse


def whole_block(dims):
    return pl.BlockSpec(dims, lambda i: (0,) * len(dims))


def pack_kernel(attend, merge, gains, shifts, bias, seg, out):
    for t in range(3):
        out[t * 128 : t * 128 + 128, :] = attend[t]
    out[384:512, :] = merge[...]
    zero = jnp.zeros((1, 128), f32)
    low, high, ids = gains[...].astype(f32), shifts[...].astype(f32), seg[...].astype(f32)
    tail = [
        jnp.concatenate([low[0:1], low[1:2]], axis=1),
        jnp.concatenate([high[0:1], high[1:2]], axis=1),
        jnp.concatenate([bias[...].astype(f32), zero], axis=1),
        jnp.concatenate([ids[0:1], ids[1:2]], axis=1),
        jnp.zeros((12, 256), f32),
    ]
    out[512:528, :] = jnp.concatenate(tail, axis=0).astype(bf16)


def norm_half_kernel(meta, x, out):
    normed, _ = norm_stats(x[rows_of(meta, True), :])
    out[...] = normed.astype(bf16)


def qkv_kernel(meta, x, far_a, far_b, *refs):
    blocks = refs[:9]
    (hidden, hidden_far, query, key_value, key_value_far, attend, merge, small, seg_far,
     seg_all) = refs[9:]

    def piece(offset, start, size):
        if offset < 4:
            return blocks[offset][start : start + size, :]
        if offset == 4:
            return jnp.concatenate(
                [blocks[4][start : start + size, :], blocks[5][start : start + size, :]], axis=1
            )
        return blocks[offset + 1][start : start + size, :]

    small[...] = jnp.zeros_like(small)
    for j in range(RING):
        at = columns(meta, j)
        for t in range(3):
            attend[t, at, :] = piece(j, t * 128, 128)
        merge[at, :] = piece(j, 384, 128)
        tail = piece(j, 512, 16).astype(f32)
        small[0:1, at] = tail[0:1, :128]
        small[1:2, at] = tail[0:1, 128:]
        small[2:3, at] = tail[1:2, :128]
        small[3:4, at] = tail[1:2, 128:]
        small[4:5, at] = tail[2:3, :128]
        seg_all[pl.ds(meta[j], 1), :] = tail[3:4, :]
    ids = seg_all[pl.ds(2 * meta[10], 1), :]
    seg_far[0:1, :] = ids[:, :128].astype(jnp.int32)
    seg_far[1:2, :] = ids[:, 128:].astype(jnp.int32)
    gain, shift = small[0:1, :], small[2:3, :]
    normed, _ = norm_stats(x[...])
    hidden[...] = (normed * gain + shift).astype(bf16)
    hidden_far[rows_of(meta, True), :] = (far_a[...].astype(f32) * gain + shift).astype(bf16)
    hidden_far[rows_of(meta, False), :] = (far_b[...].astype(f32) * gain + shift).astype(bf16)
    both, other = hidden[...], hidden_far[...]
    key_value[:, :256] = dot(both, attend[1]).astype(bf16)
    key_value[:, 256:] = dot(both, attend[2]).astype(bf16)
    key_value_far[:, :256] = dot(other, attend[1]).astype(bf16)
    key_value_far[:, 256:] = dot(other, attend[2]).astype(bf16)
    query[...] = (dot(both, attend[0]) * (HD**-0.5)).astype(bf16)


def masks(meta, seg, seg_col, seg_far, s):
    col = seg_col[:, s : s + 1]
    near = col == seg[s : s + 1, :]
    i = lax.broadcasted_iota(jnp.int32, (128, 128), 0)
    j = lax.broadcasted_iota(jnp.int32, (128, 128), 1)
    far = (col == seg_far[s : s + 1, :]) & (meta[9] == 1)
    return near & (j <= i), far


def head_probs(query, key, key_far, near, far):
    score = jnp.where(near, dot_nt(query, key), masked_score)
    score_far = jnp.where(far, dot_nt(query, key_far), masked_score)
    top = jnp.maximum(
        jnp.max(score, axis=-1, keepdims=True), jnp.max(score_far, axis=-1, keepdims=True)
    )
    total = jnp.sum(jnp.exp(score - top), axis=-1, keepdims=True) + jnp.sum(
        jnp.exp(score_far - top), axis=-1, keepdims=True
    )
    log_total = top + jnp.log(total)
    return jnp.exp(score - log_total), jnp.exp(score_far - log_total)


def attention_kernel(
    meta, query, kv, kv_far, seg, seg_col, seg_far, merge, attended, keep, give, part
):
    for s in range(2):
        near, far = masks(meta, seg, seg_col, seg_far, s)
        r = slice(s * 128, s * 128 + 128)
        for h in range(4):
            c = slice(h * 64, h * 64 + 64)
            v = slice(256 + h * 64, 256 + h * 64 + 64)
            probs, probs_far = head_probs(query[r, c], kv[r, c], kv_far[r, c], near, far)
            out = dot(probs.astype(bf16), kv[r, v]) + dot(probs_far.astype(bf16), kv_far[r, v])
            attended[r, c] = out.astype(bf16)
    part[...] = dot_nt(attended[...], merge[...])
    keep[...] = part[rows_of(meta, True), :]
    give[...] = part[rows_of(meta, False), :].astype(bf16)


def total_of(meta, sums, full):
    pair, far, pair_other, far_other = sums
    full[rows_of(meta, True), :] = pair[...].astype(f32) + far[...].astype(f32)
    full[rows_of(meta, False), :] = pair_other[...].astype(f32) + far_other[...].astype(f32)
    return full[...]


def assemble(meta, blocks, full):
    for j in range(RING):
        at = columns(meta, j)
        if j == 4:
            start = pl.multiple_of(meta[4] * 128, 128)
            full[pl.ds(start, 64), :] = blocks[4][...]
            full[pl.ds(pl.multiple_of(start + 64, 64), 64), :] = blocks[5][...]
        else:
            full[at, :] = (blocks[j] if j < 4 else blocks[j + 1])[...]


def store_parts(meta, left, right, outs):
    for j in range(RING):
        value = dot_tn(left[:, columns(meta, j)], right[...]).astype(bf16)
        if j == 4:
            outs[4][...] = value[:64]
            outs[5][...] = value[64:]
        else:
            (outs[j] if j < 4 else outs[j + 1])[...] = value


def ffn_first_kernel(meta, x, cot, small, s0, s1, s2, s3, *refs):
    blocks = refs[:9]
    residual, hidden, cot_half, act, slope, expand = refs[9:15]
    outs, part = refs[15:24], refs[24]
    assemble(meta, blocks, expand)
    residual[...] = x[...] + total_of(meta, (s0, s1, s2, s3), part)
    normed, _ = norm_stats(residual[...])
    hidden[...] = (normed * small[1:2, :] + small[3:4, :]).astype(bf16)
    cot_half[...] = cot[...].astype(bf16)

    def units(i, carry):
        at = pl.ds(pl.multiple_of(i * 256, 256), 256)
        pre_act = dot(hidden[...], expand[:, at]) + small[4:5, at]
        value, gradient = gelu_pair(pre_act)
        act[:, at] = value.astype(bf16)
        slope[:, at] = gradient
        return carry

    lax.fori_loop(0, 4, units, 0)
    store_parts(meta, cot_half, act, outs)


def ffn_second_kernel(meta, residual, cot_half, slope, expand, *refs):
    blocks = refs[:9]
    pre_half, later_keep, later_give, grads, reduce, part = refs[9:]
    assemble(meta, blocks, reduce)
    grads[...] = jnp.zeros_like(grads)

    def units(i, carry):
        at = pl.ds(pl.multiple_of(i * 256, 256), 256)
        pre_grad = dot(cot_half[...], reduce[:, at]) * slope[:, at]
        pre_half[:, at] = pre_grad.astype(bf16)
        grads[2:3, at] = jnp.sum(pre_grad, axis=0, keepdims=True)
        return carry

    lax.fori_loop(0, 4, units, 0)

    def later(i, carry):
        at = pl.ds(pl.multiple_of(i * 256, 256), 256)
        part[:, at] = dot_nt(pre_half[...], expand[at, :])
        return carry

    lax.fori_loop(0, 4, later, 0)
    later_keep[...] = part[rows_of(meta, True), :]
    later_give[...] = part[rows_of(meta, False), :].astype(bf16)
    normed, _ = norm_stats(residual[...])
    grads[0:1, :] = jnp.sum(part[...] * normed, axis=0, keepdims=True)
    grads[1:2, :] = jnp.sum(part[...], axis=0, keepdims=True)


def reduced_kernel(meta, act, reduce, red_keep, red_give, part):
    def reduced(i, carry):
        at = pl.ds(pl.multiple_of(i * 256, 256), 256)
        part[:, at] = dot_nt(act[...], reduce[at, :])
        return carry

    lax.fori_loop(0, 4, reduced, 0)
    red_keep[...] = part[rows_of(meta, True), :]
    red_give[...] = part[rows_of(meta, False), :].astype(bf16)


def expand_grads_kernel(meta, hidden, pre_half, *outs):
    store_parts(meta, hidden, pre_half, outs)


def attention_back_kernel(
    meta, cot, residual, small, s0, s1, s2, s3, merge, query, kv, kv_far, attended,
    seg, seg_col, seg_far, residual_grad, resid_half, query_grad, kv_grad, kv_grad_far,
    part, att_grad
):
    later_grad = total_of(meta, (s0, s1, s2, s3), part)
    normed, inverse = norm_stats(residual[...])
    residual_grad[...] = cot[...] + norm_backward(later_grad, normed, inverse, small[1:2, :])
    resid_half[...] = residual_grad[...].astype(bf16)
    att_grad[...] = dot(resid_half[...], merge[...]).astype(bf16)
    for s in range(2):
        near, far = masks(meta, seg, seg_col, seg_far, s)
        r = slice(s * 128, s * 128 + 128)
        for h in range(4):
            c = slice(h * 64, h * 64 + 64)
            v = slice(256 + h * 64, 256 + h * 64 + 64)
            q, k, k_far = query[r, c], kv[r, c], kv_far[r, c]
            probs, probs_far = head_probs(q, k, k_far, near, far)
            up = att_grad[r, c]
            delta = jnp.sum(up.astype(f32) * attended[r, c].astype(f32), axis=-1, keepdims=True)
            score = (probs * (dot_nt(up, kv[r, v]) - delta)).astype(bf16)
            score_far = (probs_far * (dot_nt(up, kv_far[r, v]) - delta)).astype(bf16)
            query_grad[r, c] = (dot(score, k) + dot(score_far, k_far)) * (HD**-0.5)
            kv_grad[r, c] = dot_tn(score, q)
            kv_grad[r, v] = dot_tn(probs.astype(bf16), up)
            kv_grad_far[r, c] = dot_tn(score_far, q).astype(bf16)
            kv_grad_far[r, v] = dot_tn(probs_far.astype(bf16), up).astype(bf16)


def attention_grads_kernel(
    meta, x, far_a, far_b, hidden, hidden_far, query_grad, kv_grad, kv_grad_far, resid_half,
    attended, attend, grads, early, *refs
):
    outs, proj, sums, part = refs[:9], refs[9], refs[10], refs[11]
    proj[:, :256] = query_grad[...].astype(bf16)
    proj[:, 256:] = kv_grad[...].astype(bf16)
    early[...] = (
        dot_nt(proj[:, :256], attend[0])
        + dot_nt(proj[:, 256:512], attend[1])
        + dot_nt(proj[:, 512:], attend[2])
    )
    part[...] = dot_nt(kv_grad_far[:, :256], attend[1]) + dot_nt(kv_grad_far[:, 256:], attend[2])
    normed, _ = norm_stats(x[...])
    mine, other = part[rows_of(meta, True), :], part[rows_of(meta, False), :]
    sums[0:1, :] = (
        jnp.sum(early[...] * normed, axis=0, keepdims=True)
        + jnp.sum(mine * far_a[...].astype(f32), axis=0, keepdims=True)
        + jnp.sum(other * far_b[...].astype(f32), axis=0, keepdims=True)
    )
    sums[1:2, :] = jnp.sum(early[...] + part[...], axis=0, keepdims=True)
    for j in range(RING):
        at = columns(meta, j)
        lhs, lhs_far = hidden[:, at], hidden_far[:, at]
        pieces = [dot_tn(lhs, proj[:, :256]).astype(bf16)]
        for t in (1, 2):
            c, c_far = slice(t * 256, t * 256 + 256), slice(t * 256 - 256, t * 256)
            pieces.append((dot_tn(lhs, proj[:, c]) + dot_tn(lhs_far, kv_grad_far[:, c_far])).astype(bf16))
        pieces.append(dot_tn(resid_half[:, at], attended[...]).astype(bf16))
        zero = jnp.zeros((1, 128), f32)
        tail = jnp.concatenate(
            [
                jnp.concatenate([sums[0:1, at], grads[0:1, at]], axis=1),
                jnp.concatenate([sums[1:2, at], grads[1:2, at]], axis=1),
                jnp.concatenate([grads[2:3, at], zero], axis=1),
                jnp.zeros((13, 256), f32),
            ],
            axis=0,
        )
        pieces.append(tail.astype(bf16))
        start = 0
        for value in pieces:
            span = slice(start, start + value.shape[0])
            start += value.shape[0]
            if j == 4:
                outs[4][span, :] = value[:, :128]
                outs[5][span, :] = value[:, 128:]
            else:
                out = outs[j] if j < 4 else outs[j + 1]
                out[span, :] = value


def project_back_kernel(meta, early, kv_grad_in, attend, keep, give, part):
    part[...] = (
        early[...]
        + dot_nt(kv_grad_in[:, :256], attend[1])
        + dot_nt(kv_grad_in[:, 256:], attend[2])
    )
    keep[...] = part[rows_of(meta, True), :]
    give[...] = part[rows_of(meta, False), :].astype(bf16)


def first_rows_kernel(meta, up, down, ahead, behind, up_out, down_out):
    up_out[:64, :] = (up[:64, :].astype(f32) + ahead[...].astype(f32)).astype(bf16)
    up_out[64:, :] = up[64:, :]
    down_out[:64, :] = down[:64, :]
    down_out[64:, :] = (down[64:, :].astype(f32) + behind[...].astype(f32)).astype(bf16)


def first_columns_kernel(meta, up, down, ahead, behind, up_out, down_out):
    up_out[:, :128] = (up[:, :128].astype(f32) + ahead[...].astype(f32)).astype(bf16)
    up_out[:, 128:] = up[:, 128:]
    down_out[:, :128] = down[:, :128]
    down_out[:, 128:] = (down[:, 128:].astype(f32) + behind[...].astype(f32)).astype(bf16)


def step_kernel(meta, up, down, ahead, behind, up_out, down_out):
    up_out[...] = (up[...].astype(f32) + ahead[...].astype(f32)).astype(bf16)
    down_out[...] = (down[...].astype(f32) + behind[...].astype(f32)).astype(bf16)


def last_kernel(meta, own, ahead, behind, out):
    out[...] = own[...].astype(f32) + (ahead[...].astype(f32) + behind[...].astype(f32))


def last_pack_kernel(meta, own, ahead, behind, attend, merge, tail):
    def total(start, size):
        r = slice(start, start + size)
        return own[r, :].astype(f32) + (ahead[r, :].astype(f32) + behind[r, :].astype(f32))

    for t in range(3):
        attend[t] = total(t * 128, 128)
    merge[...] = total(384, 128)
    tail[...] = total(512, 16)


def block_out_kernel(meta, residual, s0, s1, s2, s3, out, part):
    out[...] = residual[...] + total_of(meta, (s0, s1, s2, s3), part)


def input_grad_kernel(meta, x, residual_grad, small, s0, s1, s2, s3, out, part):
    early_grad = total_of(meta, (s0, s1, s2, s3), part)
    normed, inverse = norm_stats(x[...])
    out[...] = residual_grad[...] + norm_backward(early_grad, normed, inverse, small[0:1, :])


def send_ahead(value):
    return lax.ppermute(value, AXES, AHEAD)


def send_behind(value):
    return lax.ppermute(value, AXES, BEHIND)


def gather_blocks(own, first, second):
    blocks = [own] + [None] * 8
    ahead, behind = own, own
    for step in range(1, 4):
        ahead = send_ahead(ahead)
        behind = send_behind(behind)
        blocks[9 - step], blocks[step] = ahead, behind
    blocks[4] = send_ahead(first(ahead))
    blocks[5] = send_behind(second(behind))
    return blocks


def sum_blocks(meta, parts, first, last, last_shapes):
    ahead = send_ahead(parts[4])
    behind = send_behind(parts[5])
    for step in range(3, 0, -1):
        up, down = call(
            first if step == 3 else step_kernel, [shape(parts[1].shape, bf16)] * 2,
            [meta, parts[step], parts[9 - step], ahead, behind], 1_000_000,
        )
        ahead = send_ahead(up)
        behind = send_behind(down)
    return call(last, last_shapes, [meta, parts[0], ahead, behind], 1_000_000)


def tp_send(pairs):
    return lambda value: lax.ppermute(value, TP, pairs)


def tp_exchange(keep, give):
    near = tp_send(NEAR)(give)
    pair = (keep + near.astype(f32)).astype(bf16)
    far = tp_send(FAR)(pair)
    pair_other = tp_send(NEAR)(pair)
    return pair, far, pair_other, tp_send(NEAR)(far)


def fast_shards(
    inputs, segment_ids, gains, shifts, attend_weight, merge_weight, expand_weight,
    expand_bias, reduce_weight, cotangent,
):
    shard, ctx = lax.axis_index(AXES[0]), lax.axis_index(CTX)
    place = jnp.where(ctx == 0, shard, RING - 1 - shard)
    spots = lax.rem(place + jnp.arange(RING, dtype=jnp.int32), RING)
    owners = jnp.where(spots < 4, 2 * spots, 2 * (7 - spots) + 1)
    side = lax.rem(lax.axis_index(TP), 2)
    meta = jnp.concatenate([owners, jnp.stack([side, ctx, shard])]).astype(jnp.int32)

    x = inputs.reshape(256, 1024)
    cot = cotangent.reshape(256, 1024)
    rows, half, square = (256, 1024), (128, 1024), (256, 256)
    part = pltpu.VMEM(rows, f32)
    pack_args = [
        jnp.swapaxes(attend_weight, 0, 1), merge_weight, gains, shifts, expand_bias, segment_ids
    ]
    pack_args = [pltpu.with_memory_space_constraint(a, pltpu.HBM) for a in pack_args]
    pack = pl.pallas_call(
        pack_kernel,
        grid=(1,),
        out_shape=shape((528, 256), bf16),
        in_specs=[whole_block(a.shape) for a in pack_args],
        out_specs=whole_block((528, 256)),
        compiler_params=pltpu.CompilerParams(vmem_limit_bytes=ROOM),
    )(*pack_args)
    blocks = gather_blocks(pack, lambda v: v[:, :128], lambda v: v[:, 128:])
    (normed_half,) = call(norm_half_kernel, [shape(half, bf16)], [meta, x], 1_000_000)
    far_a = lax.ppermute(normed_half, CTX, [(0, 1)])
    far_b = lax.ppermute(far_a, TP, NEAR)
    seg_col = segment_ids.T
    expand_weight, _ = lax.optimization_barrier((expand_weight, blocks[EXPAND_AFTER]))
    expand_blocks = gather_blocks(expand_weight, lambda v: v[:64], lambda v: v[64:])
    reduce_weight, _ = lax.optimization_barrier((reduce_weight, blocks[REDUCE_AFTER]))
    reduce_blocks = gather_blocks(reduce_weight, lambda v: v[:64], lambda v: v[64:])

    hidden_early, hidden_far, query, kv, kv_far, attend, merge, small, seg_far = call(
        qkv_kernel,
        [shape(rows, bf16), shape(rows, bf16), shape(square, bf16), shape((256, 512), bf16),
         shape((256, 512), bf16), shape((3, 1024, 256), bf16), shape((1024, 256), bf16),
         shape((8, 1024), f32), shape((2, 128), jnp.int32)],
        [meta, x, far_a, far_b] + blocks, 700_000_000, [pltpu.VMEM((8, 256), f32)],
    )
    attended, keep, give = call(
        attention_kernel,
        [shape(square, bf16), shape(half, f32), shape(half, bf16)],
        [meta, query, kv, kv_far, segment_ids, seg_col, seg_far, merge],
        300_000_000, [part], 800_000,
    )
    part_shapes = [shape(half, bf16)] * 9
    part_shapes[4] = part_shapes[5] = shape((64, 1024), bf16)
    residual, hidden_later, cot_half, act, slope, expand, *reduce_parts = call(
        ffn_first_kernel,
        [shape(rows, f32)] + [shape(rows, bf16)] * 3 + [shape(rows, f32)]
        + [shape((1024, 1024), bf16)] + part_shapes,
        [meta, x, cot, small, *tp_exchange(keep, give)] + expand_blocks,
        1_100_000_000, [part], 300_000,
    )
    pre_half, later_keep, later_give, grads, reduce = call(
        ffn_second_kernel,
        [shape(rows, bf16), shape(half, f32), shape(half, bf16), shape((8, 1024), f32),
         shape((1024, 1024), bf16)],
        [meta, residual, cot_half, slope, expand] + reduce_blocks, 1_100_000_000, [part],
    )
    red_keep, red_give = call(
        reduced_kernel, [shape(half, f32), shape(half, bf16)], [meta, act, reduce],
        550_000_000, [part],
    )
    (reduce_grad,) = sum_blocks(
        meta, reduce_parts, first_rows_kernel, last_kernel, [shape(half, f32)]
    )
    later_sums = tp_exchange(later_keep, later_give)
    expand_parts = call(
        expand_grads_kernel, part_shapes,
        [meta, hidden_later, pre_half], 550_000_000,
    )
    (expand_grad,) = sum_blocks(
        meta, expand_parts, first_rows_kernel, last_kernel, [shape(half, f32)]
    )
    residual_grad, resid_half, query_grad, kv_grad, kv_grad_far = call(
        attention_back_kernel,
        [shape(rows, f32), shape(rows, bf16), shape(square, f32), shape((256, 512), f32),
         shape((256, 512), bf16)],
        [meta, cot, residual, small, *later_sums, merge, query, kv, kv_far, attended,
         segment_ids, seg_col, seg_far],
        500_000_000, [part, pltpu.VMEM(square, bf16)], 800_000,
    )
    kv_grad_in = lax.ppermute(kv_grad_far, CTX, [(1, 0)])
    pack_shapes = [shape((528, 256), bf16)] * 9
    pack_shapes[4] = pack_shapes[5] = shape((528, 128), bf16)
    early, *pack_parts = call(
        attention_grads_kernel, [shape(rows, f32)] + pack_shapes,
        [meta, x, far_a, far_b, hidden_early, hidden_far, query_grad, kv_grad, kv_grad_far,
         resid_half, attended, attend, grads], 1_100_000_000,
        [pltpu.VMEM((256, 768), bf16), pltpu.VMEM((8, 1024), f32), part],
    )
    attend_grad, merge_grad, tail = sum_blocks(
        meta, pack_parts, first_columns_kernel, last_pack_kernel,
        [shape((3, 128, 256), f32), shape((128, 256), f32), shape((16, 256), f32)],
    )
    early_keep, early_give = call(
        project_back_kernel, [shape(half, f32), shape(half, bf16)],
        [meta, early, kv_grad_in, attend], 300_000_000, [part],
    )
    early_sums = tp_exchange(early_keep, early_give)
    red_keep, red_give, _ = lax.optimization_barrier((red_keep, red_give, query_grad))
    (block_out,) = call(
        block_out_kernel, [shape(rows, f32)],
        [meta, residual, *tp_exchange(red_keep, red_give)], 1_000_000, [part],
    )
    (input_grad,) = call(
        input_grad_kernel, [shape(rows, f32)],
        [meta, x, residual_grad, small, *early_sums], 5_000_000, [part],
    )
    norms = tail[:2]
    norms = norms + lax.ppermute(norms, TP, NEAR)
    norms = norms + lax.ppermute(norms, TP, FAR)
    return (
        block_out.reshape(inputs.shape),
        input_grad.reshape(inputs.shape),
        norms[0].reshape(2, 128),
        norms[1].reshape(2, 128),
        jnp.swapaxes(attend_grad, 0, 1),
        merge_grad,
        expand_grad,
        tail[2:3, :128],
        reduce_grad,
    )


EXPAND_AFTER = 0
REDUCE_AFTER = 2


def fits(mesh_sizes, *args):
    shapes = tuple(a.shape for a in args)
    return mesh_sizes == (4, 2, 4) and shapes == (
        (2, 128, 1024), (2, 128), (2, 128), (2, 128), (128, 3, 256), (128, 256),
        (128, 1024), (1, 128), (128, 1024), (2, 128, 1024),
    )


def either(*args):
    sizes = tuple(lax.axis_size(name) for name in (*AXES, TP))
    if not fits(sizes, *args):
        return shards(*args)
    return fast_shards(*args)


def solution(mesh):
    in_specs = (
        P("shard", "ctx", None),
        P("shard", "ctx"),
        P(None, ("shard", "ctx")),
        P(None, ("shard", "ctx")),
        P(("shard", "ctx"), None, "tp"),
        P(("shard", "ctx"), "tp"),
        P(("shard", "ctx"), "tp"),
        P("tp", ("shard", "ctx")),
        P(("shard", "ctx"), "tp"),
        P("shard", "ctx", None),
    )
    out_specs = (
        P("shard", "ctx", None),
        P("shard", "ctx", None),
        P(None, ("shard", "ctx")),
        P(None, ("shard", "ctx")),
        P(("shard", "ctx"), None, "tp"),
        P(("shard", "ctx"), "tp"),
        P(("shard", "ctx"), "tp"),
        P("tp", ("shard", "ctx")),
        P(("shard", "ctx"), "tp"),
    )
    return jax.shard_map(either, mesh=mesh, in_specs=in_specs, out_specs=out_specs, check_vma=False)
```

```python
import math

import jax
import jax.numpy as jnp
from jax import lax
from jax.experimental import pallas as pl
from jax.experimental.pallas import tpu as pltpu
from jax.sharding import PartitionSpec as P

HD = 64


epsilon = 1e-05
masked_score = -1e30
gelu_scale = 0.7978845608028654
gelu_cubic = 0.044715


def norm_forward(values, gain, shift):
    average = jnp.mean(values, axis=-1, keepdims=True)
    centered = values - average
    variance = jnp.mean(centered * centered, axis=-1, keepdims=True)
    inverse = lax.rsqrt(variance + epsilon)
    normed = centered * inverse
    return (normed, inverse, normed * gain.astype(jnp.float32) + shift.astype(jnp.float32))


def norm_backward(upstream, normed, inverse, gain):
    scaled = upstream * gain.astype(jnp.float32)
    first_mean = jnp.mean(scaled, axis=-1, keepdims=True)
    second_mean = jnp.mean(scaled * normed, axis=-1, keepdims=True)
    return inverse * (scaled - first_mean - normed * second_mean)


def gelu_pair(pre_act):
    inner_arg = gelu_scale * (pre_act + gelu_cubic * pre_act * pre_act * pre_act)
    tangent = jnp.tanh(inner_arg)
    gelu_value = 0.5 * pre_act * (1.0 + tangent)
    gelu_slope = 0.5 * (1.0 + tangent) + 0.5 * pre_act * (1.0 - tangent * tangent) * gelu_scale * (
        1.0 + 3.0 * gelu_cubic * pre_act * pre_act
    )
    return (gelu_value, gelu_slope)


def shards(
    inputs,
    segment_ids,
    gains,
    shifts,
    attend_weight,
    merge_weight,
    expand_weight,
    expand_bias,
    reduce_weight,
    cotangent,
):
    seq_count, group_len, model_width = inputs.shape
    row_count = seq_count * group_len
    full_len = group_len * lax.axis_size("ctx")
    head_scale = HD ** (-0.5)
    gathered = (
        lax.all_gather(attend_weight, ("shard", "ctx"), axis=0, tiled=True),
        lax.all_gather(merge_weight, ("shard", "ctx"), axis=0, tiled=True),
        lax.all_gather(expand_weight, ("shard", "ctx"), axis=0, tiled=True),
        lax.all_gather(reduce_weight, ("shard", "ctx"), axis=0, tiled=True),
        lax.all_gather(expand_bias, ("shard", "ctx"), axis=1, tiled=True),
        lax.all_gather(gains, ("shard", "ctx"), axis=1, tiled=True),
        lax.all_gather(shifts, ("shard", "ctx"), axis=1, tiled=True),
    )
    attend_full, merge_full, expand_full, reduce_full, bias_full, gains_full, shifts_full = gathered
    local_cols = attend_full.shape[2]
    head_local = local_cols // HD
    flat_in = inputs.reshape(row_count, model_width)
    normed_early, inverse_early, affine_early = norm_forward(flat_in, gains_full[0], shifts_full[0])
    hidden_early = affine_early.astype(jnp.bfloat16)
    projected = jnp.einsum(
        "rd,dtc->rtc", hidden_early, attend_full, preferred_element_type=jnp.float32
    )
    query_heads = (
        (projected[:, 0] * head_scale)
        .astype(jnp.bfloat16)
        .reshape(seq_count, group_len, head_local, HD)
    )
    key_rows = projected[:, 1].astype(jnp.bfloat16).reshape(seq_count, group_len, local_cols)
    value_rows = projected[:, 2].astype(jnp.bfloat16).reshape(seq_count, group_len, local_cols)
    all_keys, all_values, all_segments = (
        lax.all_gather(key_rows, "ctx", axis=1, tiled=True),
        lax.all_gather(value_rows, "ctx", axis=1, tiled=True),
        lax.all_gather(segment_ids, "ctx", axis=1, tiled=True),
    )
    key_heads = all_keys.reshape(seq_count, full_len, head_local, HD)
    value_heads = all_values.reshape(seq_count, full_len, head_local, HD)
    query_pos = lax.axis_index("ctx") * group_len + jnp.arange(group_len, dtype=jnp.int32)
    key_pos = jnp.arange(full_len, dtype=jnp.int32)
    allowed = (segment_ids[:, :, None] == all_segments[:, None, :]) & (
        key_pos[None, None, :] <= query_pos[None, :, None]
    )
    allowed = allowed[:, None]

    def score_block():
        raw_scores = jnp.einsum(
            "sqhd,skhd->shqk", query_heads, key_heads, preferred_element_type=jnp.float32
        )
        return jnp.where(allowed, raw_scores, masked_score)

    scores = score_block()
    row_top = jnp.max(scores, axis=-1, keepdims=True)
    log_total = row_top + jnp.log(jnp.sum(jnp.exp(scores - row_top), axis=-1, keepdims=True))
    attn_probs = jnp.exp(scores - log_total)
    probs_half = attn_probs.astype(jnp.bfloat16)
    attended_heads = jnp.einsum(
        "shqk,skhd->sqhd", probs_half, value_heads, preferred_element_type=jnp.float32
    ).astype(jnp.bfloat16)
    attended = attended_heads.reshape(row_count, local_cols)
    merge_part = jnp.einsum("rc,oc->ro", attended, merge_full, preferred_element_type=jnp.float32)
    residual = flat_in + lax.psum(merge_part, "tp")
    normed_later, inverse_later, affine_later = norm_forward(
        residual, gains_full[1], shifts_full[1]
    )
    hidden_later = affine_later.astype(jnp.bfloat16)
    pre_act = jnp.dot(
        hidden_later, expand_full, preferred_element_type=jnp.float32
    ) + bias_full.astype(jnp.float32)
    gelu_value, gelu_slope = gelu_pair(pre_act)
    activated = gelu_value.astype(jnp.bfloat16)
    reduce_part = jnp.einsum(
        "rf,of->ro", activated, reduce_full, preferred_element_type=jnp.float32
    )
    block_out = residual + lax.psum(reduce_part.astype(jnp.bfloat16), "tp").astype(jnp.float32)
    back_set = (
        lax.all_gather(attend_weight, ("shard", "ctx"), axis=0, tiled=True),
        lax.all_gather(merge_weight, ("shard", "ctx"), axis=0, tiled=True),
        lax.all_gather(expand_weight, ("shard", "ctx"), axis=0, tiled=True),
        lax.all_gather(reduce_weight, ("shard", "ctx"), axis=0, tiled=True),
        lax.all_gather(gains, ("shard", "ctx"), axis=1, tiled=True),
    )
    attend_back, merge_back, expand_back, reduce_back, gains_back = back_set
    output_grad = cotangent.reshape(row_count, model_width)
    cot_half = output_grad.astype(jnp.bfloat16)
    reduce_grad = jnp.einsum("ro,rf->of", cot_half, activated, preferred_element_type=jnp.float32)
    pre_grad = jnp.dot(cot_half, reduce_back, preferred_element_type=jnp.float32) * gelu_slope
    pre_half = pre_grad.astype(jnp.bfloat16)
    bias_grad = jnp.sum(pre_grad, axis=0, keepdims=True)
    expand_grad = jnp.einsum(
        "rd,rf->df", hidden_later, pre_half, preferred_element_type=jnp.float32
    )
    later_part = jnp.einsum("rf,df->rd", pre_half, expand_back, preferred_element_type=jnp.float32)
    later_grad = lax.psum(later_part, "tp")
    residual_grad = output_grad + norm_backward(
        later_grad, normed_later, inverse_later, gains_back[1]
    )
    resid_half = residual_grad.astype(jnp.bfloat16)
    merge_grad = jnp.einsum("ro,rc->oc", resid_half, attended, preferred_element_type=jnp.float32)
    attended_grad = jnp.dot(resid_half, merge_back, preferred_element_type=jnp.float32).astype(
        jnp.bfloat16
    )
    grad_heads = attended_grad.reshape(seq_count, group_len, head_local, HD)
    scores_again = score_block()
    probs_again = jnp.exp(scores_again - log_total)
    probs_again_half = probs_again.astype(jnp.bfloat16)
    row_delta = jnp.einsum(
        "sqhd,sqhd->shq", grad_heads, attended_heads, preferred_element_type=jnp.float32
    )
    prob_grad = jnp.einsum(
        "sqhd,skhd->shqk", grad_heads, value_heads, preferred_element_type=jnp.float32
    )
    score_grad = probs_again * (prob_grad - row_delta[..., None])
    score_half = score_grad.astype(jnp.bfloat16)
    query_grad = (
        jnp.einsum("shqk,skhd->sqhd", score_half, key_heads, preferred_element_type=jnp.float32)
        * head_scale
    )
    keys_part = jnp.einsum(
        "shqk,sqhd->skhd", score_half, query_heads, preferred_element_type=jnp.float32
    ).reshape(seq_count, full_len, local_cols)
    values_part = jnp.einsum(
        "shqk,sqhd->skhd", probs_again_half, grad_heads, preferred_element_type=jnp.float32
    ).reshape(seq_count, full_len, local_cols)
    keys_grad, values_grad = (
        lax.psum_scatter(keys_part, "ctx", scatter_dimension=1, tiled=True),
        lax.psum_scatter(values_part, "ctx", scatter_dimension=1, tiled=True),
    )
    proj_grad = jnp.stack(
        [
            query_grad.reshape(row_count, local_cols),
            keys_grad.reshape(row_count, local_cols),
            values_grad.reshape(row_count, local_cols),
        ],
        axis=1,
    ).astype(jnp.bfloat16)
    attend_grad = jnp.einsum(
        "rd,rtc->dtc", hidden_early, proj_grad, preferred_element_type=jnp.float32
    )
    early_part = jnp.einsum(
        "rtc,dtc->rd", proj_grad, attend_back, preferred_element_type=jnp.float32
    )
    early_grad = lax.psum(early_part, "tp")
    input_grad = residual_grad + norm_backward(
        early_grad, normed_early, inverse_early, gains_back[0]
    )
    gains_grad = jnp.stack(
        [jnp.sum(early_grad * normed_early, axis=0), jnp.sum(later_grad * normed_later, axis=0)]
    )
    shifts_grad = jnp.stack([jnp.sum(early_grad, axis=0), jnp.sum(later_grad, axis=0)])
    shares = (
        lax.psum_scatter(attend_grad, ("shard", "ctx"), scatter_dimension=0, tiled=True),
        lax.psum_scatter(merge_grad, ("shard", "ctx"), scatter_dimension=0, tiled=True),
        lax.psum_scatter(expand_grad, ("shard", "ctx"), scatter_dimension=0, tiled=True),
        lax.psum_scatter(reduce_grad, ("shard", "ctx"), scatter_dimension=0, tiled=True),
        lax.psum_scatter(bias_grad, ("shard", "ctx"), scatter_dimension=1, tiled=True),
        lax.psum_scatter(gains_grad, ("shard", "ctx"), scatter_dimension=1, tiled=True),
        lax.psum_scatter(shifts_grad, ("shard", "ctx"), scatter_dimension=1, tiled=True),
    )
    return (
        block_out.reshape(inputs.shape),
        input_grad.reshape(inputs.shape),
        shares[5],
        shares[6],
        shares[0],
        shares[1],
        shares[2],
        shares[4],
        shares[3],
    )


VMEM = pl.BlockSpec(memory_space=pltpu.VMEM)
SMEM = pl.BlockSpec(memory_space=pltpu.SMEM)
f32 = jnp.float32
bf16 = jnp.bfloat16
RING = 8
ROOM = 6 << 20
NEAR = [(0, 1), (1, 0), (2, 3), (3, 2)]
FAR = [(0, 2), (2, 0), (1, 3), (3, 1)]
AXES = ("shard", "ctx")
TP = "tp"
CTX = "ctx"
IDS = [2 * p if p < 4 else 2 * (7 - p) + 1 for p in range(RING)]
AHEAD = [(IDS[p], IDS[(p + 1) % RING]) for p in range(RING)]
BEHIND = [(IDS[p], IDS[(p - 1) % RING]) for p in range(RING)]


def shape(dims, dtype):
    return jax.ShapeDtypeStruct(dims, dtype)


def call(kernel, outs, args, flops, scratch=(), transcendentals=0):
    nbytes = sum(a.size * a.dtype.itemsize for a in list(args) + list(outs))
    held = sum(math.prod(a.shape) * jnp.dtype(a.dtype).itemsize for a in scratch)
    return pl.pallas_call(
        kernel,
        out_shape=tuple(outs),
        in_specs=[SMEM] + [VMEM] * (len(args) - 1),
        out_specs=tuple(VMEM for _ in outs),
        scratch_shapes=list(scratch),
        compiler_params=pltpu.CompilerParams(vmem_limit_bytes=nbytes + held + ROOM),
        cost_estimate=pl.CostEstimate(
            flops=flops, bytes_accessed=nbytes, transcendentals=transcendentals
        ),
    )(*args)


def columns(meta, offset):
    return pl.ds(pl.multiple_of(meta[offset] * 128, 128), 128)


def rows_of(meta, mine):
    side = meta[8] if mine else 1 - meta[8]
    return pl.ds(pl.multiple_of(side * 128, 128), 128)


def dot(a, b):
    return jnp.dot(a, b, preferred_element_type=f32)


def dot_nt(a, b):
    return lax.dot_general(a, b, (((1,), (1,)), ((), ())), preferred_element_type=f32)


def dot_tn(a, b):
    return lax.dot_general(a, b, (((0,), (0,)), ((), ())), preferred_element_type=f32)


def norm_stats(values):
    average = jnp.mean(values, axis=-1, keepdims=True)
    centered = values - average
    variance = jnp.mean(centered * centered, axis=-1, keepdims=True)
    inverse = lax.rsqrt(variance + epsilon)
    return centered * inverse, inverse


def whole_block(dims):
    return pl.BlockSpec(dims, lambda i: (0,) * len(dims))


def pack_kernel(attend, merge, gains, shifts, bias, seg, out):
    for t in range(3):
        out[t * 128 : t * 128 + 128, :] = attend[t]
    out[384:512, :] = merge[...]
    zero = jnp.zeros((1, 128), f32)
    low, high, ids = gains[...].astype(f32), shifts[...].astype(f32), seg[...].astype(f32)
    tail = [
        jnp.concatenate([low[0:1], low[1:2]], axis=1),
        jnp.concatenate([high[0:1], high[1:2]], axis=1),
        jnp.concatenate([bias[...].astype(f32), zero], axis=1),
        jnp.concatenate([ids[0:1], ids[1:2]], axis=1),
        jnp.zeros((12, 256), f32),
    ]
    out[512:528, :] = jnp.concatenate(tail, axis=0).astype(bf16)


def norm_half_kernel(meta, x, out):
    normed, _ = norm_stats(x[rows_of(meta, True), :])
    out[...] = normed.astype(bf16)


def qkv_kernel(meta, x, far_a, far_b, *refs):
    blocks = refs[:9]
    (hidden, hidden_far, query, key_value, key_value_far, attend, merge, small, seg_far,
     seg_all) = refs[9:]

    def piece(offset, start, size):
        if offset < 4:
            return blocks[offset][start : start + size, :]
        if offset == 4:
            return jnp.concatenate(
                [blocks[4][start : start + size, :], blocks[5][start : start + size, :]], axis=1
            )
        return blocks[offset + 1][start : start + size, :]

    small[...] = jnp.zeros_like(small)
    for j in range(RING):
        at = columns(meta, j)
        for t in range(3):
            attend[t, at, :] = piece(j, t * 128, 128)
        merge[at, :] = piece(j, 384, 128)
        tail = piece(j, 512, 16).astype(f32)
        small[0:1, at] = tail[0:1, :128]
        small[1:2, at] = tail[0:1, 128:]
        small[2:3, at] = tail[1:2, :128]
        small[3:4, at] = tail[1:2, 128:]
        small[4:5, at] = tail[2:3, :128]
        seg_all[pl.ds(meta[j], 1), :] = tail[3:4, :]
    ids = seg_all[pl.ds(2 * meta[10], 1), :]
    seg_far[0:1, :] = ids[:, :128].astype(jnp.int32)
    seg_far[1:2, :] = ids[:, 128:].astype(jnp.int32)
    gain, shift = small[0:1, :], small[2:3, :]
    normed, _ = norm_stats(x[...])
    hidden[...] = (normed * gain + shift).astype(bf16)
    hidden_far[rows_of(meta, True), :] = (far_a[...].astype(f32) * gain + shift).astype(bf16)
    hidden_far[rows_of(meta, False), :] = (far_b[...].astype(f32) * gain + shift).astype(bf16)
    both, other = hidden[...], hidden_far[...]
    key_value[:, :256] = dot(both, attend[1]).astype(bf16)
    key_value[:, 256:] = dot(both, attend[2]).astype(bf16)
    key_value_far[:, :256] = dot(other, attend[1]).astype(bf16)
    key_value_far[:, 256:] = dot(other, attend[2]).astype(bf16)
    query[...] = (dot(both, attend[0]) * (HD**-0.5)).astype(bf16)


def masks(meta, seg, seg_col, seg_far, s):
    col = seg_col[:, s : s + 1]
    near = col == seg[s : s + 1, :]
    i = lax.broadcasted_iota(jnp.int32, (128, 128), 0)
    j = lax.broadcasted_iota(jnp.int32, (128, 128), 1)
    far = (col == seg_far[s : s + 1, :]) & (meta[9] == 1)
    return near & (j <= i), far


def head_probs(query, key, key_far, near, far):
    score = jnp.where(near, dot_nt(query, key), masked_score)
    score_far = jnp.where(far, dot_nt(query, key_far), masked_score)
    top = jnp.maximum(
        jnp.max(score, axis=-1, keepdims=True), jnp.max(score_far, axis=-1, keepdims=True)
    )
    total = jnp.sum(jnp.exp(score - top), axis=-1, keepdims=True) + jnp.sum(
        jnp.exp(score_far - top), axis=-1, keepdims=True
    )
    log_total = top + jnp.log(total)
    return jnp.exp(score - log_total), jnp.exp(score_far - log_total)


def attention_kernel(
    meta, query, kv, kv_far, seg, seg_col, seg_far, merge, attended, keep, give, part
):
    for s in range(2):
        near, far = masks(meta, seg, seg_col, seg_far, s)
        r = slice(s * 128, s * 128 + 128)
        for h in range(4):
            c = slice(h * 64, h * 64 + 64)
            v = slice(256 + h * 64, 256 + h * 64 + 64)
            probs, probs_far = head_probs(query[r, c], kv[r, c], kv_far[r, c], near, far)
            out = dot(probs.astype(bf16), kv[r, v]) + dot(probs_far.astype(bf16), kv_far[r, v])
            attended[r, c] = out.astype(bf16)
    part[...] = dot_nt(attended[...], merge[...])
    keep[...] = part[rows_of(meta, True), :]
    give[...] = part[rows_of(meta, False), :].astype(bf16)


def total_of(meta, sums, full):
    pair, far, pair_other, far_other = sums
    full[rows_of(meta, True), :] = pair[...].astype(f32) + far[...].astype(f32)
    full[rows_of(meta, False), :] = pair_other[...].astype(f32) + far_other[...].astype(f32)
    return full[...]


def assemble(meta, blocks, full):
    for j in range(RING):
        at = columns(meta, j)
        if j == 4:
            start = pl.multiple_of(meta[4] * 128, 128)
            full[pl.ds(start, 64), :] = blocks[4][...]
            full[pl.ds(pl.multiple_of(start + 64, 64), 64), :] = blocks[5][...]
        else:
            full[at, :] = (blocks[j] if j < 4 else blocks[j + 1])[...]


def store_parts(meta, left, right, outs):
    for j in range(RING):
        value = dot_tn(left[:, columns(meta, j)], right[...]).astype(bf16)
        if j == 4:
            outs[4][...] = value[:64]
            outs[5][...] = value[64:]
        else:
            (outs[j] if j < 4 else outs[j + 1])[...] = value


def ffn_first_kernel(meta, x, cot, small, s0, s1, s2, s3, *refs):
    blocks = refs[:9]
    residual, hidden, cot_half, act, slope, expand = refs[9:15]
    outs, part = refs[15:24], refs[24]
    assemble(meta, blocks, expand)
    residual[...] = x[...] + total_of(meta, (s0, s1, s2, s3), part)
    normed, _ = norm_stats(residual[...])
    hidden[...] = (normed * small[1:2, :] + small[3:4, :]).astype(bf16)
    cot_half[...] = cot[...].astype(bf16)

    def units(i, carry):
        at = pl.ds(pl.multiple_of(i * 256, 256), 256)
        pre_act = dot(hidden[...], expand[:, at]) + small[4:5, at]
        value, gradient = gelu_pair(pre_act)
        act[:, at] = value.astype(bf16)
        slope[:, at] = gradient
        return carry

    lax.fori_loop(0, 4, units, 0)
    store_parts(meta, cot_half, act, outs)


def ffn_second_kernel(meta, residual, cot_half, slope, expand, *refs):
    blocks = refs[:9]
    pre_half, later_keep, later_give, grads, reduce, part = refs[9:]
    assemble(meta, blocks, reduce)
    grads[...] = jnp.zeros_like(grads)

    def units(i, carry):
        at = pl.ds(pl.multiple_of(i * 256, 256), 256)
        pre_grad = dot(cot_half[...], reduce[:, at]) * slope[:, at]
        pre_half[:, at] = pre_grad.astype(bf16)
        grads[2:3, at] = jnp.sum(pre_grad, axis=0, keepdims=True)
        return carry

    lax.fori_loop(0, 4, units, 0)

    def later(i, carry):
        at = pl.ds(pl.multiple_of(i * 256, 256), 256)
        part[:, at] = dot_nt(pre_half[...], expand[at, :])
        return carry

    lax.fori_loop(0, 4, later, 0)
    later_keep[...] = part[rows_of(meta, True), :]
    later_give[...] = part[rows_of(meta, False), :].astype(bf16)
    normed, _ = norm_stats(residual[...])
    grads[0:1, :] = jnp.sum(part[...] * normed, axis=0, keepdims=True)
    grads[1:2, :] = jnp.sum(part[...], axis=0, keepdims=True)


def reduced_kernel(meta, act, reduce, red_keep, red_give, part):
    def reduced(i, carry):
        at = pl.ds(pl.multiple_of(i * 256, 256), 256)
        part[:, at] = dot_nt(act[...], reduce[at, :])
        return carry

    lax.fori_loop(0, 4, reduced, 0)
    red_keep[...] = part[rows_of(meta, True), :]
    red_give[...] = part[rows_of(meta, False), :].astype(bf16)


def expand_grads_kernel(meta, hidden, pre_half, *outs):
    store_parts(meta, hidden, pre_half, outs)


def attention_back_kernel(
    meta, cot, residual, small, s0, s1, s2, s3, merge, query, kv, kv_far, attended,
    seg, seg_col, seg_far, residual_grad, resid_half, query_grad, kv_grad, kv_grad_far,
    part, att_grad
):
    later_grad = total_of(meta, (s0, s1, s2, s3), part)
    normed, inverse = norm_stats(residual[...])
    residual_grad[...] = cot[...] + norm_backward(later_grad, normed, inverse, small[1:2, :])
    resid_half[...] = residual_grad[...].astype(bf16)
    att_grad[...] = dot(resid_half[...], merge[...]).astype(bf16)
    for s in range(2):
        near, far = masks(meta, seg, seg_col, seg_far, s)
        r = slice(s * 128, s * 128 + 128)
        for h in range(4):
            c = slice(h * 64, h * 64 + 64)
            v = slice(256 + h * 64, 256 + h * 64 + 64)
            q, k, k_far = query[r, c], kv[r, c], kv_far[r, c]
            probs, probs_far = head_probs(q, k, k_far, near, far)
            up = att_grad[r, c]
            delta = jnp.sum(up.astype(f32) * attended[r, c].astype(f32), axis=-1, keepdims=True)
            score = (probs * (dot_nt(up, kv[r, v]) - delta)).astype(bf16)
            score_far = (probs_far * (dot_nt(up, kv_far[r, v]) - delta)).astype(bf16)
            query_grad[r, c] = (dot(score, k) + dot(score_far, k_far)) * (HD**-0.5)
            kv_grad[r, c] = dot_tn(score, q)
            kv_grad[r, v] = dot_tn(probs.astype(bf16), up)
            kv_grad_far[r, c] = dot_tn(score_far, q).astype(bf16)
            kv_grad_far[r, v] = dot_tn(probs_far.astype(bf16), up).astype(bf16)


def attention_grads_kernel(
    meta, x, far_a, far_b, hidden, hidden_far, query_grad, kv_grad, kv_grad_far, resid_half,
    attended, attend, grads, early, *refs
):
    outs, proj, sums, part = refs[:9], refs[9], refs[10], refs[11]
    proj[:, :256] = query_grad[...].astype(bf16)
    proj[:, 256:] = kv_grad[...].astype(bf16)
    early[...] = (
        dot_nt(proj[:, :256], attend[0])
        + dot_nt(proj[:, 256:512], attend[1])
        + dot_nt(proj[:, 512:], attend[2])
    )
    part[...] = dot_nt(kv_grad_far[:, :256], attend[1]) + dot_nt(kv_grad_far[:, 256:], attend[2])
    normed, _ = norm_stats(x[...])
    mine, other = part[rows_of(meta, True), :], part[rows_of(meta, False), :]
    sums[0:1, :] = (
        jnp.sum(early[...] * normed, axis=0, keepdims=True)
        + jnp.sum(mine * far_a[...].astype(f32), axis=0, keepdims=True)
        + jnp.sum(other * far_b[...].astype(f32), axis=0, keepdims=True)
    )
    sums[1:2, :] = jnp.sum(early[...] + part[...], axis=0, keepdims=True)
    for j in range(RING):
        at = columns(meta, j)
        lhs, lhs_far = hidden[:, at], hidden_far[:, at]
        pieces = [dot_tn(lhs, proj[:, :256]).astype(bf16)]
        for t in (1, 2):
            c, c_far = slice(t * 256, t * 256 + 256), slice(t * 256 - 256, t * 256)
            pieces.append((dot_tn(lhs, proj[:, c]) + dot_tn(lhs_far, kv_grad_far[:, c_far])).astype(bf16))
        pieces.append(dot_tn(resid_half[:, at], attended[...]).astype(bf16))
        zero = jnp.zeros((1, 128), f32)
        tail = jnp.concatenate(
            [
                jnp.concatenate([sums[0:1, at], grads[0:1, at]], axis=1),
                jnp.concatenate([sums[1:2, at], grads[1:2, at]], axis=1),
                jnp.concatenate([grads[2:3, at], zero], axis=1),
                jnp.zeros((13, 256), f32),
            ],
            axis=0,
        )
        pieces.append(tail.astype(bf16))
        start = 0
        for value in pieces:
            span = slice(start, start + value.shape[0])
            start += value.shape[0]
            if j == 4:
                outs[4][span, :] = value[:, :128]
                outs[5][span, :] = value[:, 128:]
            else:
                out = outs[j] if j < 4 else outs[j + 1]
                out[span, :] = value


def project_back_kernel(meta, early, kv_grad_in, attend, keep, give, part):
    part[...] = (
        early[...]
        + dot_nt(kv_grad_in[:, :256], attend[1])
        + dot_nt(kv_grad_in[:, 256:], attend[2])
    )
    keep[...] = part[rows_of(meta, True), :]
    give[...] = part[rows_of(meta, False), :].astype(bf16)


def first_rows_kernel(meta, up, down, ahead, behind, up_out, down_out):
    up_out[:64, :] = (up[:64, :].astype(f32) + ahead[...].astype(f32)).astype(bf16)
    up_out[64:, :] = up[64:, :]
    down_out[:64, :] = down[:64, :]
    down_out[64:, :] = (down[64:, :].astype(f32) + behind[...].astype(f32)).astype(bf16)


def first_columns_kernel(meta, up, down, ahead, behind, up_out, down_out):
    up_out[:, :128] = (up[:, :128].astype(f32) + ahead[...].astype(f32)).astype(bf16)
    up_out[:, 128:] = up[:, 128:]
    down_out[:, :128] = down[:, :128]
    down_out[:, 128:] = (down[:, 128:].astype(f32) + behind[...].astype(f32)).astype(bf16)


def step_kernel(meta, up, down, ahead, behind, up_out, down_out):
    up_out[...] = (up[...].astype(f32) + ahead[...].astype(f32)).astype(bf16)
    down_out[...] = (down[...].astype(f32) + behind[...].astype(f32)).astype(bf16)


def last_kernel(meta, own, ahead, behind, out):
    out[...] = own[...].astype(f32) + (ahead[...].astype(f32) + behind[...].astype(f32))


def last_pack_kernel(meta, own, ahead, behind, attend, merge, norms, bias):
    def total(start, size):
        r = slice(start, start + size)
        return own[r, :].astype(f32) + (ahead[r, :].astype(f32) + behind[r, :].astype(f32))

    for t in range(3):
        attend[t] = total(t * 128, 128)
    merge[...] = total(384, 128)
    tail = total(512, 16)
    norms[...] = tail[0:2, :]
    bias[...] = tail[2:3, :128]


def block_out_kernel(meta, residual, s0, s1, s2, s3, out, part):
    out[...] = residual[...] + total_of(meta, (s0, s1, s2, s3), part)


def input_grad_kernel(meta, x, residual_grad, small, s0, s1, s2, s3, out, part):
    early_grad = total_of(meta, (s0, s1, s2, s3), part)
    normed, inverse = norm_stats(x[...])
    out[...] = residual_grad[...] + norm_backward(early_grad, normed, inverse, small[0:1, :])


def send_ahead(value):
    return lax.ppermute(value, AXES, AHEAD)


def send_behind(value):
    return lax.ppermute(value, AXES, BEHIND)


def gather_blocks(own, first, second):
    blocks = [own] + [None] * 8
    ahead, behind = own, own
    for step in range(1, 4):
        ahead = send_ahead(ahead)
        behind = send_behind(behind)
        blocks[9 - step], blocks[step] = ahead, behind
    blocks[4] = send_ahead(first(ahead))
    blocks[5] = send_behind(second(behind))
    return blocks


def sum_blocks(meta, parts, first, last, last_shapes):
    ahead = send_ahead(parts[4])
    behind = send_behind(parts[5])
    for step in range(3, 0, -1):
        up, down = call(
            first if step == 3 else step_kernel, [shape(parts[1].shape, bf16)] * 2,
            [meta, parts[step], parts[9 - step], ahead, behind], 1_000_000,
        )
        ahead = send_ahead(up)
        behind = send_behind(down)
    return call(last, last_shapes, [meta, parts[0], ahead, behind], 1_000_000)


def tp_send(pairs):
    return lambda value: lax.ppermute(value, TP, pairs)


def tp_exchange(keep, give):
    near = tp_send(NEAR)(give)
    pair = (keep + near.astype(f32)).astype(bf16)
    far = tp_send(FAR)(pair)
    pair_other = tp_send(NEAR)(pair)
    return pair, far, pair_other, tp_send(NEAR)(far)


def fast_shards(
    inputs, segment_ids, gains, shifts, attend_weight, merge_weight, expand_weight,
    expand_bias, reduce_weight, cotangent,
):
    shard, ctx = lax.axis_index(AXES[0]), lax.axis_index(CTX)
    place = jnp.where(ctx == 0, shard, RING - 1 - shard)
    spots = lax.rem(place + jnp.arange(RING, dtype=jnp.int32), RING)
    owners = jnp.where(spots < 4, 2 * spots, 2 * (7 - spots) + 1)
    side = lax.rem(lax.axis_index(TP), 2)
    meta = jnp.concatenate([owners, jnp.stack([side, ctx, shard])]).astype(jnp.int32)

    x = inputs.reshape(256, 1024)
    cot = cotangent.reshape(256, 1024)
    rows, half, square = (256, 1024), (128, 1024), (256, 256)
    part = pltpu.VMEM(rows, f32)
    pack_args = [
        jnp.swapaxes(attend_weight, 0, 1), merge_weight, gains, shifts, expand_bias, segment_ids
    ]
    pack_args = [pltpu.with_memory_space_constraint(a, pltpu.HBM) for a in pack_args]
    pack = pl.pallas_call(
        pack_kernel,
        grid=(1,),
        out_shape=shape((528, 256), bf16),
        in_specs=[whole_block(a.shape) for a in pack_args],
        out_specs=whole_block((528, 256)),
        compiler_params=pltpu.CompilerParams(vmem_limit_bytes=ROOM),
    )(*pack_args)
    blocks = gather_blocks(pack, lambda v: v[:, :128], lambda v: v[:, 128:])
    (normed_half,) = call(norm_half_kernel, [shape(half, bf16)], [meta, x], 1_000_000)
    far_a = lax.ppermute(normed_half, CTX, [(0, 1)])
    far_b = lax.ppermute(far_a, TP, NEAR)
    seg_col = segment_ids.T
    expand_weight, _ = lax.optimization_barrier((expand_weight, blocks[EXPAND_AFTER]))
    expand_blocks = gather_blocks(expand_weight, lambda v: v[:64], lambda v: v[64:])
    reduce_weight, _ = lax.optimization_barrier((reduce_weight, blocks[REDUCE_AFTER]))
    reduce_blocks = gather_blocks(reduce_weight, lambda v: v[:64], lambda v: v[64:])

    hidden_early, hidden_far, query, kv, kv_far, attend, merge, small, seg_far = call(
        qkv_kernel,
        [shape(rows, bf16), shape(rows, bf16), shape(square, bf16), shape((256, 512), bf16),
         shape((256, 512), bf16), shape((3, 1024, 256), bf16), shape((1024, 256), bf16),
         shape((8, 1024), f32), shape((2, 128), jnp.int32)],
        [meta, x, far_a, far_b] + blocks, 700_000_000, [pltpu.VMEM((8, 256), f32)],
    )
    attended, keep, give = call(
        attention_kernel,
        [shape(square, bf16), shape(half, f32), shape(half, bf16)],
        [meta, query, kv, kv_far, segment_ids, seg_col, seg_far, merge],
        300_000_000, [part], 800_000,
    )
    part_shapes = [shape(half, bf16)] * 9
    part_shapes[4] = part_shapes[5] = shape((64, 1024), bf16)
    residual, hidden_later, cot_half, act, slope, expand, *reduce_parts = call(
        ffn_first_kernel,
        [shape(rows, f32)] + [shape(rows, bf16)] * 3 + [shape(rows, f32)]
        + [shape((1024, 1024), bf16)] + part_shapes,
        [meta, x, cot, small, *tp_exchange(keep, give)] + expand_blocks,
        1_100_000_000, [part], 300_000,
    )
    pre_half, later_keep, later_give, grads, reduce = call(
        ffn_second_kernel,
        [shape(rows, bf16), shape(half, f32), shape(half, bf16), shape((8, 1024), f32),
         shape((1024, 1024), bf16)],
        [meta, residual, cot_half, slope, expand] + reduce_blocks, 1_100_000_000, [part],
    )
    red_keep, red_give = call(
        reduced_kernel, [shape(half, f32), shape(half, bf16)], [meta, act, reduce],
        550_000_000, [part],
    )
    (reduce_grad,) = sum_blocks(
        meta, reduce_parts, first_rows_kernel, last_kernel, [shape(half, f32)]
    )
    later_sums = tp_exchange(later_keep, later_give)
    expand_parts = call(
        expand_grads_kernel, part_shapes,
        [meta, hidden_later, pre_half], 550_000_000,
    )
    (expand_grad,) = sum_blocks(
        meta, expand_parts, first_rows_kernel, last_kernel, [shape(half, f32)]
    )
    residual_grad, resid_half, query_grad, kv_grad, kv_grad_far = call(
        attention_back_kernel,
        [shape(rows, f32), shape(rows, bf16), shape(square, f32), shape((256, 512), f32),
         shape((256, 512), bf16)],
        [meta, cot, residual, small, *later_sums, merge, query, kv, kv_far, attended,
         segment_ids, seg_col, seg_far],
        500_000_000, [part, pltpu.VMEM(square, bf16)], 800_000,
    )
    kv_grad_in = lax.ppermute(kv_grad_far, CTX, [(1, 0)])
    pack_shapes = [shape((528, 256), bf16)] * 9
    pack_shapes[4] = pack_shapes[5] = shape((528, 128), bf16)
    early, *pack_parts = call(
        attention_grads_kernel, [shape(rows, f32)] + pack_shapes,
        [meta, x, far_a, far_b, hidden_early, hidden_far, query_grad, kv_grad, kv_grad_far,
         resid_half, attended, attend, grads], 1_100_000_000,
        [pltpu.VMEM((256, 768), bf16), pltpu.VMEM((8, 1024), f32), part],
    )
    attend_grad, merge_grad, norms, bias_grad = sum_blocks(
        meta, pack_parts, first_columns_kernel, last_pack_kernel,
        [shape((3, 128, 256), f32), shape((128, 256), f32), shape((2, 256), f32),
         shape((1, 128), f32)],
    )
    early_keep, early_give = call(
        project_back_kernel, [shape(half, f32), shape(half, bf16)],
        [meta, early, kv_grad_in, attend], 300_000_000, [part],
    )
    early_sums = tp_exchange(early_keep, early_give)
    red_keep, red_give, _ = lax.optimization_barrier((red_keep, red_give, query_grad))
    (block_out,) = call(
        block_out_kernel, [shape(rows, f32)],
        [meta, residual, *tp_exchange(red_keep, red_give)], 1_000_000, [part],
    )
    (input_grad,) = call(
        input_grad_kernel, [shape(rows, f32)],
        [meta, x, residual_grad, small, *early_sums], 5_000_000, [part],
    )
    norms = norms + lax.ppermute(norms, TP, NEAR)
    norms = norms + lax.ppermute(norms, TP, FAR)
    return (
        block_out.reshape(inputs.shape),
        input_grad.reshape(inputs.shape),
        norms[0].reshape(2, 128),
        norms[1].reshape(2, 128),
        jnp.swapaxes(attend_grad, 0, 1),
        merge_grad,
        expand_grad,
        bias_grad,
        reduce_grad,
    )


EXPAND_AFTER = 0
REDUCE_AFTER = 1


def fits(mesh_sizes, *args):
    shapes = tuple(a.shape for a in args)
    return mesh_sizes == (4, 2, 4) and shapes == (
        (2, 128, 1024), (2, 128), (2, 128), (2, 128), (128, 3, 256), (128, 256),
        (128, 1024), (1, 128), (128, 1024), (2, 128, 1024),
    )


def either(*args):
    sizes = tuple(lax.axis_size(name) for name in (*AXES, TP))
    if not fits(sizes, *args):
        return shards(*args)
    return fast_shards(*args)


def solution(mesh):
    in_specs = (
        P("shard", "ctx", None),
        P("shard", "ctx"),
        P(None, ("shard", "ctx")),
        P(None, ("shard", "ctx")),
        P(("shard", "ctx"), None, "tp"),
        P(("shard", "ctx"), "tp"),
        P(("shard", "ctx"), "tp"),
        P("tp", ("shard", "ctx")),
        P(("shard", "ctx"), "tp"),
        P("shard", "ctx", None),
    )
    out_specs = (
        P("shard", "ctx", None),
        P("shard", "ctx", None),
        P(None, ("shard", "ctx")),
        P(None, ("shard", "ctx")),
        P(("shard", "ctx"), None, "tp"),
        P(("shard", "ctx"), "tp"),
        P(("shard", "ctx"), "tp"),
        P("tp", ("shard", "ctx")),
        P(("shard", "ctx"), "tp"),
    )
    return jax.shard_map(either, mesh=mesh, in_specs=in_specs, out_specs=out_specs, check_vma=False)
```
